32 devices in a mesh: seq: 4 (over z), fsdp: 8 (over y, x, core).
Axes of the slice: x: 2, y: 2, z: 4, core: 2. Of those that a mesh axis runs over, the one named last changes fastest.
Arguments:
- tokens: float32 [32, 1024, 768], P('fsdp', 'seq')
- time_embed: float32 [32, 128], P('fsdp'), may hold values from -6 to 6
- lengths: int32 [32], P('fsdp'), may hold values from 256 to 1024, as said below
- positions: int32 [32, 1024], P('fsdp', 'seq'), may hold values from 0 to 3070, as said below
- ada_weight: float32 [128, 4608], P('fsdp'), may hold values from -0.5 to 0.5
- ada_bias: float32 [4608], P('fsdp'), may hold values from -3 to 3
- attn_gain: float32 [768], P('fsdp'), may hold values from 0.25 to 1.75
- qkv_weight: float32 [768, 2304], P('fsdp'), may hold values from -0.21875 to 0.21875
- proj_weight: float32 [768, 768], P('fsdp'), may hold values from -2.5 to 2.5
- mlp_gain: float32 [768], P('fsdp'), may hold values from 0.25 to 1.75
- up_weight: float32 [768, 3072], P('fsdp'), may hold values from -0.21875 to 0.21875
- up_bias: float32 [3072], P('fsdp'), may hold values from -3 to 3
- down_weight: float32 [3072, 768], P('fsdp'), may hold values from -0.109375 to 0.109375
- down_bias: float32 [768], P('fsdp'), may hold values from -3 to 3
- cotangent: float32 [32, 1024, 768], P('fsdp', 'seq'), may hold values from -6 to 6
Outputs:
- block_out: float32 [32, 1024, 768], P('fsdp', 'seq')
- tokens_grad: float32 [32, 1024, 768], P('fsdp', 'seq')
- time_grad: float32 [32, 128], P('fsdp')
- ada_weight_grad: float32 [128, 4608], P('fsdp')
- ada_bias_grad: float32 [4608], P('fsdp')
- attn_gain_grad: float32 [768], P('fsdp')
- qkv_weight_grad: float32 [768, 2304], P('fsdp')
- proj_weight_grad: float32 [768, 768], P('fsdp')
- mlp_gain_grad: float32 [768], P('fsdp')
- up_weight_grad: float32 [768, 3072], P('fsdp')
- up_bias_grad: float32 [3072], P('fsdp')
- down_weight_grad: float32 [3072, 768], P('fsdp')
- down_bias_grad: float32 [768], P('fsdp')
- rms_residual: float32 [], replicated
- rms_attention: float32 [], replicated
- rms_feedforward: float32 [], replicated
The draws below stay inside these ranges and needn't reach their ends.
Inputs may be any that keep to these rules, and one draw needn't show every extreme that they name: `lengths`: some sequence has all 1024 tokens valid and some only 256. `positions`: strictly increasing along each sequence; some sequence begins at 0 and some ends at 3070.
All inputs are finite; a program needn't handle non-finite values.
Results may differ from the reference program's by a relative error of at most 0.0003.
Values sent between devices are 32-bit elements; how exact they have to be, the bound alone decides.
No kernel may reach another device: no remote copies, remote signals or barrier semaphores. Data moves between devices by JAX's collectives and lax.ppermute only.
A program may use at most 256 MiB of HBM per device.

```python
import jax
import jax.numpy as jnp
from jax import lax

D = 768
H = 12
HD = 64
FF = 3072
COND = 128
LEN = 1024
SEQS = 32


def draw_tokens(key, part):
    values = jax.random.normal(key, (SEQS, LEN, D), jnp.float32)
    ramp = 0.6 + 1.2 * jnp.arange(SEQS, dtype=jnp.float32) / max(SEQS - 1, 1)
    return values * ramp[:, None, None]


def draw_lengths(key, part):
    first_key, second_key = jax.random.split(key)
    drawn = jax.random.randint(first_key, (SEQS,), LEN // 4, LEN + 1)
    order = jax.random.permutation(second_key, SEQS)
    drawn = drawn.at[order[0]].set(LEN).at[order[1]].set(LEN // 4)
    return drawn.astype(jnp.int32)


def draw_positions(key, part):
    first_key, second_key, third_key = jax.random.split(jax.random.fold_in(key, 7), 3)
    starts = jax.random.randint(first_key, (SEQS,), 0, LEN)
    gaps = jax.random.randint(second_key, (SEQS, LEN), 1, 3)
    order = jax.random.permutation(third_key, SEQS)
    starts = starts.at[order[0]].set(0).at[order[1]].set(LEN - 1)
    gaps = gaps.at[order[0], 0].set(1)
    gaps = gaps.at[order[1]].set(jnp.full((LEN,), 2, jnp.int32))
    return (starts[:, None] + jnp.cumsum(gaps, axis=1) - 1).astype(jnp.int32)


def block_levels(rng, shape, cuts, smallest, high):
    factor_of = 1.0
    for dim, blocks in cuts:
        draws = jax.random.uniform(jax.random.fold_in(jax.random.fold_in(rng, 6), dim), (blocks,), jnp.float32, smallest / len(cuts), high / len(cuts))
        factor_of = factor_of * jnp.repeat(jnp.exp(draws), shape[dim] // blocks).reshape((-1,) + (1,) * (len(shape) - 1 - dim))
    return factor_of


def centred(own_key, extent, deviation, reach, cuts=(), kind=jnp.bfloat16):
    values = jax.random.normal(own_key, extent, jnp.float32) * deviation
    if len(cuts) > 0:
        values = block_levels(own_key, extent, cuts, -0.22, 0.18) * values
    return jnp.clip(values, min=-reach, max=reach).astype(kind)


def setup_inputs(seed: int = 0) -> dict:
    streams_of = jax.random.split(jax.random.key(seed), 16)
    return {
        "tokens": draw_tokens(jax.random.fold_in(streams_of[15], 71), 0),
        "time_embed": centred(streams_of[1], (SEQS, COND), 1.0, 6.0, ((0, 8),), jnp.float32),
        "lengths": draw_lengths(jax.random.fold_in(streams_of[15], 71), 0),
        "positions": draw_positions(jax.random.fold_in(streams_of[15], 71), 0),
        "ada_weight": centred(streams_of[4], (COND, 6 * D), COND ** -0.5, 0.5, ((0, 8),), jnp.float32),
        "ada_bias": centred(streams_of[5], (6 * D,), 0.5, 3.0, ((0, 8),), jnp.float32),
        "attn_gain": jnp.clip(1.0 + 0.15 * jax.random.normal(streams_of[6], (D,), jnp.float32), 0.25, 1.75),
        "qkv_weight": centred(streams_of[7], (D, 3 * D), D ** -0.5, 0.21875, ((0, 8),), jnp.float32),
        "proj_weight": centred(streams_of[8], (D, D), (max(D // 128, 1)) ** -0.5, 2.5, ((0, 8),), jnp.float32),
        "mlp_gain": jnp.clip(1.0 + 0.15 * jax.random.normal(streams_of[9], (D,), jnp.float32), 0.25, 1.75),
        "up_weight": centred(streams_of[10], (D, FF), D ** -0.5, 0.21875, ((0, 8),), jnp.float32),
        "up_bias": centred(streams_of[11], (FF,), 0.5, 3.0, ((0, 8),), jnp.float32),
        "down_weight": centred(streams_of[12], (FF, D), FF ** -0.5, 0.109375, ((0, 8),), jnp.float32),
        "down_bias": centred(streams_of[13], (D,), 0.5, 3.0, ((0, 8),), jnp.float32),
        "cotangent": centred(streams_of[14], (SEQS, LEN, D), 1.0, 6.0, ((0, 8), (1, 4)), jnp.float32),
    }


epsilon = 1e-05
highest = lax.Precision.HIGHEST

def layer_norm(field, gain):
    average = lax.optimization_barrier(jnp.mean(field, axis=-1, keepdims=True))
    centered = field - average
    variance = lax.optimization_barrier(jnp.mean(centered * centered, axis=-1, keepdims=True))
    return centered * lax.rsqrt(variance + epsilon) * gain

def modulate(field, gain, shift, scale):
    return layer_norm(field, gain) * (1.0 + scale[:, None, :]) + shift[:, None, :]

def gelu_tanh(value):
    inner = 0.7978845608028654 * (value + 0.044715 * value * value * value)
    return 0.5 * value * (1.0 + jnp.tanh(inner))

def rotary_tables(positions, head_size):
    inverse = 1.0 / 10000.0 ** (jnp.arange(0, head_size, 2, dtype=jnp.float32) / head_size)
    angles = positions.astype(jnp.float32)[..., None] * inverse
    angles = jnp.concatenate([angles, angles], axis=-1)
    return (jnp.cos(angles)[..., None, :], jnp.sin(angles)[..., None, :])

def rotate(field, cosine, sine):
    half = field.shape[-1] // 2
    turned = jnp.concatenate([-field[..., half:], field[..., :half]], axis=-1)
    return field * cosine + turned * sine

def attend_sequence(inputs):
    queries, keys_all, values_all, key_mask = inputs
    scores = jnp.einsum('qhd,khd->hqk', queries, keys_all, precision=highest) * HD ** (-0.5)
    scores = jnp.where(key_mask[None, None, :], scores, -1e+30)
    weights = jax.nn.softmax(scores, axis=-1)
    return jnp.einsum('hqk,khd->qhd', weights, values_all, precision=highest)

def reference(tokens, time_embed, lengths, positions, ada_weight, ada_bias, attn_gain, qkv_weight, proj_weight, mlp_gain, up_weight, up_bias, down_weight, down_bias, cotangent):
    key_mask = jnp.arange(LEN)[None, :] < lengths[:, None]
    cosine, sine = rotary_tables(positions, HD)

    def forward(tokens, time_embed, ada_weight, ada_bias, attn_gain, qkv_weight, proj_weight, mlp_gain, up_weight, up_bias, down_weight, down_bias):
        modulation = jnp.dot(jax.nn.silu(time_embed), ada_weight, precision=highest) + ada_bias
        shift_attn, scale_attn, gate_attn, shift_mlp, scale_mlp, gate_mlp = jnp.split(modulation, 6, axis=1)
        normed_attn = modulate(tokens, attn_gain, shift_attn, scale_attn)
        projected = jnp.einsum('std,de->ste', normed_attn, qkv_weight, precision=highest).reshape(SEQS, LEN, 3, H, HD)
        queries = rotate(projected[:, :, 0], cosine, sine)
        keys_all = rotate(projected[:, :, 1], cosine, sine)
        attended = lax.map(jax.checkpoint(attend_sequence), (queries, keys_all, projected[:, :, 2], key_mask))
        attn_branch = gate_attn[:, None, :] * jnp.einsum('std,de->ste', attended.reshape(SEQS, LEN, D), proj_weight, precision=highest)
        middle = tokens + attn_branch
        normed_mlp = modulate(middle, mlp_gain, shift_mlp, scale_mlp)
        hidden_act = gelu_tanh(jnp.einsum('std,df->stf', normed_mlp, up_weight, precision=highest) + up_bias)
        mlp_branch = gate_mlp[:, None, :] * (jnp.einsum('stf,fd->std', hidden_act, down_weight, precision=highest) + down_bias)
        return (middle + mlp_branch, (attn_branch, mlp_branch))
    block_out, back_fn, branches = jax.vjp(forward, tokens, time_embed, ada_weight, ada_bias, attn_gain, qkv_weight, proj_weight, mlp_gain, up_weight, up_bias, down_weight, down_bias, has_aux=True)
    grads = back_fn(cotangent)
    valid = key_mask.astype(jnp.float32)[..., None]
    count = jnp.sum(valid)

    def root_mean(field):
        return jnp.sqrt(jnp.sum(valid * field * field) / (count * D))
    return (block_out, grads[0], grads[1], grads[2], grads[3], grads[4], grads[5], grads[6], grads[7], grads[8], grads[9], grads[10], grads[11], root_mean(tokens), root_mean(branches[0]), root_mean(branches[1]))
```

```python
from functools import partial

import jax
import jax.numpy as jnp
from jax import lax
from jax.experimental import pallas as pl
from jax.experimental.pallas import tpu as pltpu
from jax.sharding import PartitionSpec as P

H = 12
HD = 64
PAIR = 2 * HD
LOG2E = 1.4426950408889634
LN2 = 0.6931471805599453

epsilon = 1e-05
highest = lax.Precision.HIGHEST
high = lax.Precision.HIGH
f32 = jnp.float32
bf16 = jnp.bfloat16


def layer_norm(field, gain):
    average = jnp.mean(field, axis=-1, keepdims=True)
    centered = field - average
    variance = jnp.mean(centered * centered, axis=-1, keepdims=True)
    return centered * lax.rsqrt(variance + epsilon) * gain


def modulate(field, gain, shift, scale):
    return layer_norm(field, gain) * (1.0 + scale) + shift


def gelu_tanh(value):
    inner = 0.7978845608028654 * (value + 0.044715 * value * value * value)
    return 0.5 * value * (1.0 + jnp.tanh(inner))


def rotary_tables(positions):
    inverse = 1.0 / 10000.0 ** (jnp.arange(0, HD, 2, dtype=f32) / HD)
    angles = positions.astype(f32)[:, None] * inverse
    cosine, sine = jnp.cos(angles), jnp.sin(angles)
    return jnp.tile(cosine, (1, 4)), jnp.tile(sine, (1, 4))


def rotate(u, cosine, sine, lane):
    first = (lane % HD) < (HD // 2)
    turned = jnp.where(first, -pltpu.roll(u, PAIR - HD // 2, 1), pltpu.roll(u, HD // 2, 1))
    return u * cosine + turned * sine


def rotate_back(g, cosine, sine, lane):
    first = (lane % HD) < (HD // 2)
    w = g * sine
    return g * cosine + jnp.where(first, pltpu.roll(w, PAIR - HD // 2, 1), -pltpu.roll(w, HD // 2, 1))


def parts(u):
    hi = u.astype(bf16).astype(f32)
    return hi, (u - hi).astype(bf16).astype(f32)


def both(u, head, lane):
    turned = pltpu.roll(u, HD, 1)
    return jnp.where((lane < HD) == (head == 0), u, turned)


def beside(left, right, head, lane):
    low = left if head == 0 else pltpu.roll(left, HD, 1)
    high_lanes = pltpu.roll(right, HD, 1) if head == 0 else right
    return jnp.where(lane < HD, low, high_lanes)


def three_terms(column, lane):
    a = column.astype(bf16).astype(f32)
    b = (column - a).astype(bf16).astype(f32)
    c = column - a - b
    return jnp.where(lane == HD, a, jnp.where(lane == HD + 1, b, jnp.where(lane == HD + 2, c, 0.0)))


def split_bf16(u):
    hi = u.astype(bf16)
    return hi, (u - hi.astype(f32)).astype(bf16)


def dot_nt(a, b):
    return lax.dot_general(a, b, (((1,), (1,)), ((), ())), preferred_element_type=f32)


def dot_nn(a, b):
    return lax.dot_general(a, b, (((1,), (0,)), ((), ())), preferred_element_type=f32)


def forward_kernel(
    len_ref, q_ref, k_ref, v_ref, cos_ref, sin_ref, out_ref, lse_ref, qs, ks, vs, acc, *, rows
):
    full_len = q_ref.shape[0]
    lane = lax.broadcasted_iota(jnp.int32, (full_len, PAIR), 1)
    place = lax.broadcasted_iota(jnp.int32, (full_len, PAIR), 0)
    cosine, sine = cos_ref[...], sin_ref[...]
    q = rotate(q_ref[...], cosine, sine, lane) * (HD**-0.5 * LOG2E)
    k = rotate(k_ref[...], cosine, sine, lane)
    q_hi, q_lo = parts(q)
    k_hi, k_lo = parts(k)
    v_hi, v_lo = parts(v_ref[...])
    bias = jnp.where(place < len_ref[0], 0.0, -1e30)
    for head in range(2):
        qs[head, :, :PAIR] = both(q_hi, head, lane).astype(bf16)
        qs[head, :, PAIR:] = jnp.where(
            lane < HD, beside(q_lo, q_lo, head, lane), jnp.where(lane == HD, 1.0, 0.0)
        ).astype(bf16)
        ks[head, :, :PAIR] = beside(k_hi, k_lo, head, lane).astype(bf16)
        ks[head, :, PAIR:] = jnp.where(
            lane < HD, beside(k_hi, k_hi, head, lane), jnp.where(lane == HD, bias, 0.0)
        ).astype(bf16)
        vs[head] = beside(v_hi, v_lo, head, lane).astype(bf16)

    low = lax.broadcasted_iota(jnp.int32, (rows, PAIR), 1) < HD

    def step(block, carry):
        at = pl.ds(pl.multiple_of(block * rows, rows), rows)
        outs, lses = [], []
        for head in range(2):
            scores = dot_nt(qs[head, at, :], ks[head])
            largest = jnp.max(scores, axis=1, keepdims=True)
            expo = jnp.exp2(scores - largest)
            total = jnp.sum(expo, axis=1, keepdims=True)
            hi, lo = split_bf16(expo)
            both_parts = dot_nn(hi, vs[head]) + dot_nn(lo, vs[head])
            outs.append((both_parts + pltpu.roll(both_parts, HD, 1)) / total)
            lses.append(largest + jnp.log2(total))
        out_ref[at, :] = jnp.where(low, outs[0], outs[1])
        lse_ref[at, :] = jnp.where(low, lses[0], lses[1])
        return carry

    lax.fori_loop(0, full_len // rows, step, 0)


def backward_kernel(
    len_ref,
    q_ref,
    k_ref,
    v_ref,
    cos_ref,
    sin_ref,
    out_in_ref,
    lse_ref,
    do_ref,
    grad_ref,
    qs,
    ks,
    vs,
    dos,
    kd,
    qt,
    dot_t,
    dq,
    dkt,
    dvt,
    *,
    rows,
):
    full_len = q_ref.shape[0]
    which = pl.program_id(1)
    lane = lax.broadcasted_iota(jnp.int32, (full_len, PAIR), 1)

    @pl.when(which == 0)
    def _():
        place = lax.broadcasted_iota(jnp.int32, (full_len, PAIR), 0)
        cosine, sine = cos_ref[...], sin_ref[...]
        q = rotate(q_ref[...], cosine, sine, lane) * (HD**-0.5 * LOG2E)
        k = rotate(k_ref[...], cosine, sine, lane)
        out_grad = do_ref[...]
        q_hi, q_lo = parts(q)
        k_hi, k_lo = parts(k)
        v_hi, v_lo = parts(v_ref[...])
        g_hi, g_lo = parts(out_grad)
        product = out_grad * out_in_ref[...]
        lse = lse_ref[...]
        bias = jnp.where(place < len_ref[0], 0.0, -1e30)
        ones = jnp.where((lane >= HD) & (lane < HD + 3), 1.0, 0.0)
        for head in range(2):
            mine = (lane < HD) == (head == 0)
            delta = jnp.sum(jnp.where(mine, product, 0.0), axis=1, keepdims=True)
            lse_head = jnp.max(jnp.where(mine, lse, -3e38), axis=1, keepdims=True)
            qs[head, :, :PAIR] = both(q_hi, head, lane).astype(bf16)
            qs[head, :, PAIR:] = jnp.where(
                lane < HD,
                beside(q_lo, q_lo, head, lane),
                three_terms(-lse_head, lane) + jnp.where(lane == HD + 3, 1.0, 0.0),
            ).astype(bf16)
            ks[head, :, :PAIR] = beside(k_hi, k_lo, head, lane).astype(bf16)
            ks[head, :, PAIR:] = jnp.where(
                lane < HD, beside(k_hi, k_hi, head, lane), ones + jnp.where(lane == HD + 3, bias, 0.0)
            ).astype(bf16)
            dos[head, :, :PAIR] = both(g_hi, head, lane).astype(bf16)
            dos[head, :, PAIR:] = jnp.where(
                lane < HD, beside(g_lo, g_lo, head, lane), three_terms(-delta, lane)
            ).astype(bf16)
            vs[head, :, :PAIR] = beside(v_hi, v_lo, head, lane).astype(bf16)
            vs[head, :, PAIR:] = jnp.where(lane < HD, beside(v_hi, v_hi, head, lane), ones).astype(bf16)
            kd[head] = beside(k_hi, k_lo, head, lane).astype(bf16)
            qt[head] = beside(q_hi, q_lo, head, lane).T.astype(bf16)
            dot_t[head] = beside(g_hi, g_lo, head, lane).T.astype(bf16)
        dkt[...] = jnp.zeros_like(dkt)
        dvt[...] = jnp.zeros_like(dvt)
        low = lax.broadcasted_iota(jnp.int32, (rows, PAIR), 1) < HD

        def step(block, carry):
            at = pl.ds(pl.multiple_of(block * rows, rows), rows)
            outs = []
            for head in range(2):
                weights = jnp.exp2(dot_nt(qs[head, at, :], ks[head]))
                score_grad = weights * dot_nt(dos[head, at, :], vs[head])
                w_hi, w_lo = split_bf16(weights)
                s_hi, s_lo = split_bf16(score_grad)
                both_parts = dot_nn(s_hi, kd[head]) + dot_nn(s_lo, kd[head])
                outs.append(both_parts + pltpu.roll(both_parts, HD, 1))
                q_t = qt[head, :, at]
                g_t = dot_t[head, :, at]
                dkt[head] += dot_nn(q_t, s_hi) + dot_nn(q_t, s_lo)
                dvt[head] += dot_nn(g_t, w_hi) + dot_nn(g_t, w_lo)
            dq[at, :] = jnp.where(low, outs[0], outs[1])
            return carry

        lax.fori_loop(0, full_len // rows, step, 0)
        grad_ref[...] = rotate_back(dq[...] * HD**-0.5, cosine, sine, lane)

    @pl.when(which == 1)
    def _():
        stacked = jnp.concatenate([dkt[h, :HD, :] + dkt[h, HD:, :] for h in range(2)], axis=0)
        grad_ref[...] = rotate_back(stacked.T * LN2, cos_ref[...], sin_ref[...], lane)

    @pl.when(which == 2)
    def _():
        stacked = jnp.concatenate([dvt[h, :HD, :] + dvt[h, HD:, :] for h in range(2)], axis=0)
        grad_ref[...] = stacked.T


def attention_forward(length, qkv, cosine, sine):
    full_len, three = qkv.shape
    width = three // 3
    pairs = width // PAIR
    rows = min(256, full_len)

    def column(offset):
        return pl.BlockSpec((full_len, PAIR), lambda p, ln: (0, p + offset))

    table = pl.BlockSpec((full_len, PAIR), lambda p, ln: (0, 0))
    wide = jax.ShapeDtypeStruct((full_len, width), f32)
    return pl.pallas_call(
        partial(forward_kernel, rows=rows),
        name="attention_forward",
        out_shape=(wide, wide),
        grid_spec=pltpu.PrefetchScalarGridSpec(
            num_scalar_prefetch=1,
            grid=(pairs,),
            in_specs=[column(0), column(pairs), column(2 * pairs), table, table],
            out_specs=(column(0), column(0)),
            scratch_shapes=[
                pltpu.VMEM((2, full_len, 2 * PAIR), bf16),
                pltpu.VMEM((2, full_len, 2 * PAIR), bf16),
                pltpu.VMEM((2, full_len, PAIR), bf16),
                pltpu.VMEM((8, 128), f32),
            ],
        ),
        cost_estimate=pl.CostEstimate(
            flops=24 * full_len * full_len * width, bytes_accessed=20 * full_len * width, transcendentals=0
        ),
    )(length, qkv, qkv, qkv, cosine, sine)


def attention_backward(length, qkv, cosine, sine, attended, lse, out_grad):
    full_len, three = qkv.shape
    width = three // 3
    pairs = width // PAIR
    rows = min(256, full_len)

    def column(offset):
        return pl.BlockSpec((full_len, PAIR), lambda p, c, ln: (0, p + offset))

    table = pl.BlockSpec((full_len, PAIR), lambda p, c, ln: (0, 0))
    stacked = pltpu.VMEM((2, full_len, 2 * PAIR), bf16)
    turned = pltpu.VMEM((2, PAIR, full_len), bf16)
    summed = pltpu.VMEM((2, PAIR, full_len), f32)
    return pl.pallas_call(
        partial(backward_kernel, rows=rows),
        name="attention_backward",
        out_shape=jax.ShapeDtypeStruct((full_len, three), f32),
        grid_spec=pltpu.PrefetchScalarGridSpec(
            num_scalar_prefetch=1,
            grid=(pairs, 3),
            in_specs=[
                column(0),
                column(pairs),
                column(2 * pairs),
                table,
                table,
                column(0),
                column(0),
                column(0),
            ],
            out_specs=pl.BlockSpec((full_len, PAIR), lambda p, c, ln: (0, c * pairs + p)),
            scratch_shapes=[
                stacked,
                stacked,
                stacked,
                stacked,
                pltpu.VMEM((2, full_len, PAIR), bf16),
                turned,
                turned,
                pltpu.VMEM((full_len, PAIR), f32),
                summed,
                summed,
            ],
        ),
        cost_estimate=pl.CostEstimate(
            flops=60 * full_len * full_len * width, bytes_accessed=32 * full_len * width, transcendentals=0
        ),
    )(length, qkv, qkv, qkv, cosine, sine, attended, lse, out_grad)


def padded_row(pieces):
    row = jnp.concatenate([piece.reshape(-1) for piece in pieces])
    return jnp.pad(row, (0, -row.shape[0] % 128))[None, :]


def cut(row, sizes):
    out, start = [], 0
    for size in sizes:
        out.append(row[:, start : start + size])
        start += size
    return out


def shards(
    tokens,
    time_embed,
    lengths,
    positions,
    ada_weight,
    ada_bias,
    attn_gain,
    qkv_weight,
    proj_weight,
    mlp_gain,
    up_weight,
    up_bias,
    down_weight,
    down_bias,
    cotangent,
):
    groups = lax.axis_size("seq")
    owners = lax.axis_size("fsdp")
    mine_seq = lax.axis_index("seq")
    mine_fsdp = lax.axis_index("fsdp")
    seqs_here, local_len, width = tokens.shape
    cond = time_embed.shape[1]
    full_len = local_len * groups
    hidden = up_weight.shape[1]
    assert seqs_here == groups

    def to_sequence(field):
        return lax.all_to_all(field, "seq", split_axis=0, concat_axis=1, tiled=True)[0]

    def to_tokens(field):
        return lax.all_to_all(field[None], "seq", split_axis=1, concat_axis=0, tiled=True)

    def gather(shard):
        return lax.all_gather(shard, "fsdp", axis=0, tiled=True)

    x = to_sequence(tokens)
    places = to_sequence(positions)
    length = lax.dynamic_slice(lengths, (mine_seq,), (1,))
    small = [time_embed, ada_bias, attn_gain, mlp_gain, up_bias, down_bias]
    small_sizes = [piece.size for piece in small]
    packed = gather(padded_row(small))
    time_all, ada_bias_full, attn_gain_full, mlp_gain_full, up_bias_full, down_bias_full = cut(
        packed, small_sizes
    )
    time_all = time_all.reshape(owners * seqs_here, cond)
    ada_bias_full, attn_gain_full, mlp_gain_full, up_bias_full, down_bias_full = (
        piece.reshape(1, -1)
        for piece in (ada_bias_full, attn_gain_full, mlp_gain_full, up_bias_full, down_bias_full)
    )
    silu_all = jax.nn.silu(time_all)
    ada_rows = ada_weight.shape[0]
    silu_cols = lax.dynamic_slice(silu_all, (0, mine_fsdp * ada_rows), (owners * seqs_here, ada_rows))
    silu_group = lax.dynamic_slice(
        silu_cols.reshape(owners, seqs_here, ada_rows), (0, mine_seq, 0), (owners, 1, ada_rows)
    )[:, 0]
    modulation = (
        lax.psum_scatter(
            jnp.dot(silu_group, ada_weight, precision=highest), "fsdp", scatter_dimension=0, tiled=True
        )
        + ada_bias_full
    )
    shift_attn, scale_attn, gate_attn, shift_mlp, scale_mlp, gate_mlp = jnp.split(modulation, 6, axis=1)
    qkv_full = gather(qkv_weight)
    proj_full = gather(proj_weight)
    up_full = gather(up_weight)
    down_full = gather(down_weight)
    cosine, sine = rotary_tables(places)
    valid = (jnp.arange(full_len, dtype=jnp.int32) < length)[:, None]

    normed_attn = modulate(x, attn_gain_full, shift_attn, scale_attn)
    qkv = jnp.dot(normed_attn, qkv_full, precision=high)
    cot_in, _ = lax.optimization_barrier((cotangent, x))
    cot = to_sequence(cot_in)
    attended, lse = attention_forward(length, qkv, cosine, sine)
    proj_out = jnp.dot(attended, proj_full, precision=high)
    attn_branch = gate_attn * proj_out
    middle = x + attn_branch
    normed_mlp = modulate(middle, mlp_gain_full, shift_mlp, scale_mlp)
    pre_act = jnp.dot(normed_mlp, up_full, precision=high) + up_bias_full
    hidden_act = gelu_tanh(pre_act)
    down_out = jnp.dot(hidden_act, down_full, precision=high) + down_bias_full
    mlp_branch = gate_mlp * down_out
    block_out = to_tokens(middle + mlp_branch)

    def valid_sum(field):
        return jnp.sum(jnp.where(valid, field * field, 0.0))

    sums = jnp.stack(
        [valid_sum(x), valid_sum(attn_branch), valid_sum(mlp_branch), jnp.sum(valid.astype(f32))]
    )

    mlp_grad = cot * gate_mlp
    gate_mlp_grad = jnp.sum(cot * down_out, axis=0)
    down_bias_grad = jnp.sum(mlp_grad, axis=0)
    act_grad = lax.dot_general(mlp_grad, down_full, (((1,), (1,)), ((), ())), precision=high)
    gelu_value, gelu_back = jax.vjp(gelu_tanh, pre_act)
    (pre_grad,) = gelu_back(act_grad)
    up_bias_grad = jnp.sum(pre_grad, axis=0)
    normed_mlp_grad = lax.dot_general(pre_grad, up_full, (((1,), (1,)), ((), ())), precision=high)
    norm_value, norm_mlp_back = jax.vjp(modulate, middle, mlp_gain_full, shift_mlp, scale_mlp)
    middle_part, mlp_gain_grad, shift_mlp_grad, scale_mlp_grad = norm_mlp_back(normed_mlp_grad)
    middle_grad = cot + middle_part
    proj_grad = middle_grad * gate_attn
    gate_attn_grad = jnp.sum(middle_grad * proj_out, axis=0)
    attended_grad = lax.dot_general(proj_grad, proj_full, (((1,), (1,)), ((), ())), precision=high)

    def weight_grad(left, right):
        return lax.dot_general(left, right, (((0,), (0,)), ((), ())), precision=high)

    def scatter(grad):
        return lax.psum_scatter(grad, "fsdp", scatter_dimension=0, tiled=True)

    down_shard = scatter(weight_grad(hidden_act, mlp_grad))
    up_shard = scatter(weight_grad(normed_mlp, pre_grad))
    proj_shard = scatter(weight_grad(attended, proj_grad))
    early = [
        gate_attn_grad,
        shift_mlp_grad,
        scale_mlp_grad,
        gate_mlp_grad,
        mlp_gain_grad,
        up_bias_grad,
        down_bias_grad,
        sums,
    ]
    early_all = lax.all_gather(padded_row(early), ("fsdp", "seq"), axis=0, tiled=True)
    gate_attn_rows, shift_mlp_rows, scale_mlp_rows, gate_mlp_rows, *early_rest = cut(
        early_all, [piece.size for piece in early]
    )

    qkv_grad = attention_backward(length, qkv, cosine, sine, attended, lse, attended_grad)
    normed_attn_grad = lax.dot_general(qkv_grad, qkv_full, (((1,), (1,)), ((), ())), precision=high)
    norm_attn_value, norm_attn_back = jax.vjp(modulate, x, attn_gain_full, shift_attn, scale_attn)
    tokens_part, attn_gain_grad, shift_attn_grad, scale_attn_grad = norm_attn_back(normed_attn_grad)
    tokens_grad = to_tokens(middle_grad + tokens_part)
    qkv_shard = scatter(weight_grad(normed_attn, qkv_grad))
    late = [shift_attn_grad, scale_attn_grad, attn_gain_grad]
    late_all = lax.all_gather(padded_row(late), ("fsdp", "seq"), axis=0, tiled=True)
    shift_attn_rows, scale_attn_rows, attn_gain_rows = cut(late_all, [piece.size for piece in late])
    modulation_rows = jnp.concatenate(
        [shift_attn_rows, scale_attn_rows, gate_attn_rows, shift_mlp_rows, scale_mlp_rows, gate_mlp_rows],
        axis=1,
    )

    ada_weight_grad = lax.dot_general(
        silu_cols, modulation_rows, (((0,), (0,)), ((), ())), precision=highest
    )
    time_cols = lax.dot_general(modulation_rows, ada_weight, (((1,), (1,)), ((), ())), precision=highest)
    time_cols = lax.all_gather(time_cols, "fsdp", axis=0)
    time_rows = lax.dynamic_slice(
        time_cols, (0, mine_fsdp * seqs_here, 0), (owners, seqs_here, ada_rows)
    )
    time_part = jnp.swapaxes(time_rows, 0, 1).reshape(seqs_here, cond)
    silu_value, silu_back = jax.vjp(jax.nn.silu, time_embed)
    (time_grad,) = silu_back(time_part)

    def owned(rows):
        total = jnp.sum(rows, axis=0)
        size = total.shape[0] // owners
        return lax.dynamic_slice(total, (mine_fsdp * size,), (size,))

    mlp_gain_rows, up_bias_rows, down_bias_rows, sums_rows = early_rest
    totals = jnp.sum(sums_rows, axis=0)
    rms = jnp.sqrt(totals[:3] / (totals[3] * width))
    down_total, up_total, proj_total = lax.psum((down_shard, up_shard, proj_shard), "seq")
    qkv_total = lax.psum(qkv_shard, "seq")
    return (
        block_out,
        tokens_grad,
        time_grad,
        ada_weight_grad,
        owned(modulation_rows),
        owned(attn_gain_rows),
        qkv_total,
        proj_total,
        owned(mlp_gain_rows),
        up_total,
        owned(up_bias_rows),
        down_total,
        owned(down_bias_rows),
        rms[0],
        rms[1],
        rms[2],
    )


def solution(mesh):
    field = P("fsdp", "seq", None)
    matrix = P("fsdp", None)
    vector = P("fsdp")
    return jax.shard_map(
        shards,
        mesh=mesh,
        in_specs=(
            field,
            matrix,
            vector,
            P("fsdp", "seq"),
            matrix,
            vector,
            vector,
            matrix,
            matrix,
            vector,
            matrix,
            vector,
            matrix,
            vector,
            field,
        ),
        out_specs=(
            field,
            field,
            matrix,
            matrix,
            vector,
            vector,
            matrix,
            matrix,
            vector,
            matrix,
            vector,
            matrix,
            vector,
            P(),
            P(),
            P(),
        ),
        check_vma=False,
    )
```

```python
from functools import partial

import jax
import jax.numpy as jnp
from jax import lax
from jax.experimental import pallas as pl
from jax.experimental.pallas import tpu as pltpu
from jax.sharding import PartitionSpec as P


HD = 64
PAIR = 2 * HD
LOG2E = 1.4426950408889634
LN2 = 0.6931471805599453

epsilon = 1e-05
highest = lax.Precision.HIGHEST
f32 = jnp.float32
bf16 = jnp.bfloat16


def gelu_and_slope(value):
    square = value * value
    t = jnp.tanh(0.7978845608028654 * (value + 0.044715 * value * square))
    slope = 0.5 * (1.0 + t) + 0.5 * value * (1.0 - t * t) * (
        0.7978845608028654 * (1.0 + 3 * 0.044715 * square)
    )
    return 0.5 * value * (1.0 + t), slope


def rotary_tables(positions):
    inverse = 1.0 / 10000.0 ** (jnp.arange(0, HD, 2, dtype=f32) / HD)
    angles = positions.astype(f32)[:, None] * inverse
    cosine, sine = jnp.cos(angles), jnp.sin(angles)
    return jnp.tile(cosine, (1, 4)), jnp.tile(sine, (1, 4))


def rotate(u, cosine, sine, lane):
    first = (lane % HD) < (HD // 2)
    turned = jnp.where(first, -pltpu.roll(u, PAIR - HD // 2, 1), pltpu.roll(u, HD // 2, 1))
    return u * cosine + turned * sine


def rotate_back(g, cosine, sine, lane):
    first = (lane % HD) < (HD // 2)
    w = g * sine
    return g * cosine + jnp.where(first, pltpu.roll(w, PAIR - HD // 2, 1), -pltpu.roll(w, HD // 2, 1))


def parts(u):
    hi = u.astype(bf16).astype(f32)
    return hi, (u - hi).astype(bf16).astype(f32)


def both(u, head, lane):
    turned = pltpu.roll(u, HD, 1)
    return jnp.where((lane < HD) == (head == 0), u, turned)


def beside(left, right, head, lane):
    low = left if head == 0 else pltpu.roll(left, HD, 1)
    high_lanes = pltpu.roll(right, HD, 1) if head == 0 else right
    return jnp.where(lane < HD, low, high_lanes)


def three_terms(column, lane):
    a = column.astype(bf16).astype(f32)
    b = (column - a).astype(bf16).astype(f32)
    c = column - a - b
    return jnp.where(lane == HD, a, jnp.where(lane == HD + 1, b, jnp.where(lane == HD + 2, c, 0.0)))


def split_bf16(u):
    hi = u.astype(bf16)
    return hi, (u - hi.astype(f32)).astype(bf16)


def dot_nt(a, b):
    return lax.dot_general(a, b, (((1,), (1,)), ((), ())), preferred_element_type=f32)


def dot_nn(a, b):
    return lax.dot_general(a, b, (((1,), (0,)), ((), ())), preferred_element_type=f32)


def forward_kernel(
    len_ref, q_ref, k_ref, v_ref, cos_ref, sin_ref, out_ref, lse_ref, qs, ks, vs, acc, *, rows
):
    full_len = q_ref.shape[0]
    lane = lax.broadcasted_iota(jnp.int32, (full_len, PAIR), 1)
    place = lax.broadcasted_iota(jnp.int32, (full_len, PAIR), 0)
    cosine, sine = cos_ref[...], sin_ref[...]
    q = rotate(q_ref[...], cosine, sine, lane) * (HD**-0.5 * LOG2E)
    k = rotate(k_ref[...], cosine, sine, lane)
    q_hi, q_lo = parts(q)
    k_hi, k_lo = parts(k)
    v_hi, v_lo = parts(v_ref[...])
    bias = jnp.where(place < len_ref[0], 0.0, -1e30)
    for head in range(2):
        qs[head, :, :PAIR] = both(q_hi, head, lane).astype(bf16)
        qs[head, :, PAIR:] = jnp.where(
            lane < HD, beside(q_lo, q_lo, head, lane), jnp.where(lane == HD, 1.0, 0.0)
        ).astype(bf16)
        ks[head, :, :PAIR] = beside(k_hi, k_lo, head, lane).astype(bf16)
        ks[head, :, PAIR:] = jnp.where(
            lane < HD, beside(k_hi, k_hi, head, lane), jnp.where(lane == HD, bias, 0.0)
        ).astype(bf16)
        vs[head] = beside(v_hi, v_lo, head, lane).astype(bf16)

    low = lax.broadcasted_iota(jnp.int32, (rows, PAIR), 1) < HD

    def step(block, carry):
        at = pl.ds(pl.multiple_of(block * rows, rows), rows)
        outs, lses = [], []
        for head in range(2):
            scores = dot_nt(qs[head, at, :], ks[head])
            largest = jnp.max(scores, axis=1, keepdims=True)
            expo = jnp.exp2(scores - largest)
            total = jnp.sum(expo, axis=1, keepdims=True)
            hi, lo = split_bf16(expo)
            both_parts = dot_nn(hi, vs[head]) + dot_nn(lo, vs[head])
            outs.append((both_parts + pltpu.roll(both_parts, HD, 1)) / total)
            lses.append(largest + jnp.log2(total))
        out_ref[at, :] = jnp.where(low, outs[0], outs[1])
        lse_ref[at, :] = jnp.where(low, lses[0], lses[1])
        return carry

    lax.fori_loop(0, full_len // rows, step, 0)


def backward_kernel(
    len_ref,
    q_ref,
    k_ref,
    v_ref,
    cos_ref,
    sin_ref,
    out_in_ref,
    lse_ref,
    do_ref,
    grad_ref,
    qs,
    ks,
    vs,
    dos,
    kd,
    qt,
    dot_t,
    dq,
    dkt,
    dvt,
    *,
    rows,
):
    full_len = q_ref.shape[0]
    which = pl.program_id(1)
    lane = lax.broadcasted_iota(jnp.int32, (full_len, PAIR), 1)

    @pl.when(which == 0)
    def _():
        place = lax.broadcasted_iota(jnp.int32, (full_len, PAIR), 0)
        cosine, sine = cos_ref[...], sin_ref[...]
        q = rotate(q_ref[...], cosine, sine, lane) * (HD**-0.5 * LOG2E)
        k = rotate(k_ref[...], cosine, sine, lane)
        out_grad = do_ref[...]
        q_hi, q_lo = parts(q)
        k_hi, k_lo = parts(k)
        v_hi, v_lo = parts(v_ref[...])
        g_hi, g_lo = parts(out_grad)
        product = out_grad * out_in_ref[...]
        lse = lse_ref[...]
        bias = jnp.where(place < len_ref[0], 0.0, -1e30)
        ones = jnp.where((lane >= HD) & (lane < HD + 3), 1.0, 0.0)
        for head in range(2):
            mine = (lane < HD) == (head == 0)
            delta = jnp.sum(jnp.where(mine, product, 0.0), axis=1, keepdims=True)
            lse_head = jnp.max(jnp.where(mine, lse, -3e38), axis=1, keepdims=True)
            qs[head, :, :PAIR] = both(q_hi, head, lane).astype(bf16)
            qs[head, :, PAIR:] = jnp.where(
                lane < HD,
                beside(q_lo, q_lo, head, lane),
                three_terms(-lse_head, lane) + jnp.where(lane == HD + 3, 1.0, 0.0),
            ).astype(bf16)
            ks[head, :, :PAIR] = beside(k_hi, k_lo, head, lane).astype(bf16)
            ks[head, :, PAIR:] = jnp.where(
                lane < HD, beside(k_hi, k_hi, head, lane), ones + jnp.where(lane == HD + 3, bias, 0.0)
            ).astype(bf16)
            dos[head, :, :PAIR] = both(g_hi, head, lane).astype(bf16)
            dos[head, :, PAIR:] = jnp.where(
                lane < HD, beside(g_lo, g_lo, head, lane), three_terms(-delta, lane)
            ).astype(bf16)
            vs[head, :, :PAIR] = beside(v_hi, v_lo, head, lane).astype(bf16)
            vs[head, :, PAIR:] = jnp.where(lane < HD, beside(v_hi, v_hi, head, lane), ones).astype(bf16)
            kd[head] = beside(k_hi, k_lo, head, lane).astype(bf16)
            qt[head] = beside(q_hi, q_lo, head, lane).T.astype(bf16)
            dot_t[head] = beside(g_hi, g_lo, head, lane).T.astype(bf16)
        dkt[...] = jnp.zeros_like(dkt)
        dvt[...] = jnp.zeros_like(dvt)
        low = lax.broadcasted_iota(jnp.int32, (rows, PAIR), 1) < HD

        def step(block, carry):
            at = pl.ds(pl.multiple_of(block * rows, rows), rows)
            outs = []
            for head in range(2):
                weights = jnp.exp2(dot_nt(qs[head, at, :], ks[head]))
                score_grad = weights * dot_nt(dos[head, at, :], vs[head])
                w_hi, w_lo = split_bf16(weights)
                s_hi, s_lo = split_bf16(score_grad)
                both_parts = dot_nn(s_hi, kd[head]) + dot_nn(s_lo, kd[head])
                outs.append(both_parts + pltpu.roll(both_parts, HD, 1))
                q_t = qt[head, :, at]
                g_t = dot_t[head, :, at]
                dkt[head] += dot_nn(q_t, s_hi) + dot_nn(q_t, s_lo)
                dvt[head] += dot_nn(g_t, w_hi) + dot_nn(g_t, w_lo)
            dq[at, :] = jnp.where(low, outs[0], outs[1])
            return carry

        lax.fori_loop(0, full_len // rows, step, 0)
        grad_ref[...] = rotate_back(dq[...] * HD**-0.5, cosine, sine, lane)

    @pl.when(which == 1)
    def _():
        stacked = jnp.concatenate([dkt[h, :HD, :] + dkt[h, HD:, :] for h in range(2)], axis=0)
        grad_ref[...] = rotate_back(stacked.T * LN2, cos_ref[...], sin_ref[...], lane)

    @pl.when(which == 2)
    def _():
        stacked = jnp.concatenate([dvt[h, :HD, :] + dvt[h, HD:, :] for h in range(2)], axis=0)
        grad_ref[...] = stacked.T


def attention_forward(length, qkv, cosine, sine):
    full_len, three = qkv.shape
    width = three // 3
    pairs = width // PAIR
    rows = min(256, full_len)

    def column(offset):
        return pl.BlockSpec((full_len, PAIR), lambda p, ln: (0, p + offset))

    table = pl.BlockSpec((full_len, PAIR), lambda p, ln: (0, 0))
    wide = jax.ShapeDtypeStruct((full_len, width), f32)
    return pl.pallas_call(
        partial(forward_kernel, rows=rows),
        name="attention_forward",
        out_shape=(wide, wide),
        grid_spec=pltpu.PrefetchScalarGridSpec(
            num_scalar_prefetch=1,
            grid=(pairs,),
            in_specs=[column(0), column(pairs), column(2 * pairs), table, table],
            out_specs=(column(0), column(0)),
            scratch_shapes=[
                pltpu.VMEM((2, full_len, 2 * PAIR), bf16),
                pltpu.VMEM((2, full_len, 2 * PAIR), bf16),
                pltpu.VMEM((2, full_len, PAIR), bf16),
                pltpu.VMEM((8, 128), f32),
            ],
        ),
        cost_estimate=pl.CostEstimate(
            flops=24 * full_len * full_len * width, bytes_accessed=20 * full_len * width, transcendentals=0
        ),
    )(length, qkv, qkv, qkv, cosine, sine)


def attention_backward(length, qkv, cosine, sine, attended, lse, out_grad):
    full_len, three = qkv.shape
    width = three // 3
    pairs = width // PAIR
    rows = min(256, full_len)

    def column(offset):
        return pl.BlockSpec((full_len, PAIR), lambda p, c, ln: (0, p + offset))

    table = pl.BlockSpec((full_len, PAIR), lambda p, c, ln: (0, 0))
    stacked = pltpu.VMEM((2, full_len, 2 * PAIR), bf16)
    turned = pltpu.VMEM((2, PAIR, full_len), bf16)
    summed = pltpu.VMEM((2, PAIR, full_len), f32)
    return pl.pallas_call(
        partial(backward_kernel, rows=rows),
        name="attention_backward",
        out_shape=jax.ShapeDtypeStruct((full_len, three), f32),
        grid_spec=pltpu.PrefetchScalarGridSpec(
            num_scalar_prefetch=1,
            grid=(pairs, 3),
            in_specs=[
                column(0),
                column(pairs),
                column(2 * pairs),
                table,
                table,
                column(0),
                column(0),
                column(0),
            ],
            out_specs=pl.BlockSpec((full_len, PAIR), lambda p, c, ln: (0, c * pairs + p)),
            scratch_shapes=[
                stacked,
                stacked,
                stacked,
                stacked,
                pltpu.VMEM((2, full_len, PAIR), bf16),
                turned,
                turned,
                pltpu.VMEM((full_len, PAIR), f32),
                summed,
                summed,
            ],
        ),
        cost_estimate=pl.CostEstimate(
            flops=60 * full_len * full_len * width, bytes_accessed=32 * full_len * width, transcendentals=0
        ),
    )(length, qkv, qkv, qkv, cosine, sine, attended, lse, out_grad)


ATTN_GAIN, ATTN_SHIFT, ATTN_SCALE, ATTN_GATE, MLP_GAIN, MLP_SHIFT, MLP_SCALE, MLP_GATE, DOWN_BIAS = range(9)
VECTORS = 16
COLUMNS = 256


def put_left(ref, u, axis):
    hi, lo = split_bf16(u)
    size = u.shape[axis]
    for place, part in enumerate((hi, lo, hi)):
        if axis == 1:
            ref[:, place * size : (place + 1) * size] = part
        else:
            ref[place * size : (place + 1) * size, :] = part


def put_right(ref, u, axis):
    hi, lo = split_bf16(u)
    size = u.shape[axis]
    for place, part in enumerate((hi, hi, lo)):
        if axis == 1:
            ref[:, place * size : (place + 1) * size] = part
        else:
            ref[place * size : (place + 1) * size, :] = part


def normalized(v):
    average = jnp.mean(v, axis=-1, keepdims=True)
    centered = v - average
    rstd = lax.rsqrt(jnp.mean(centered * centered, axis=-1, keepdims=True) + epsilon)
    return centered * rstd, rstd


def modulated(v, vec_ref, gain, shift, scale):
    xhat, _ = normalized(v)
    return xhat * row(vec_ref, gain) * (1.0 + row(vec_ref, scale)) + row(vec_ref, shift)


def row(ref, index):
    return ref[index : index + 1, :]


def column_sum(u):
    return jnp.sum(u, axis=0, keepdims=True)


def norm_backward(e_ref, v_ref, extra_ref, vec_ref, gain, scale, out_ref, sums_ref, other_ref):
    full_len = v_ref.shape[0]
    rows = min(128, full_len)
    factor = (1.0 + row(vec_ref, scale)) * row(vec_ref, gain)

    def step(block, carry):
        at = pl.ds(pl.multiple_of(block * rows, rows), rows)
        e = e_ref[at, :]
        xhat, rstd = normalized(v_ref[at, :])
        f = e * factor
        grad = rstd * (
            f
            - jnp.mean(f, axis=-1, keepdims=True)
            - xhat * jnp.mean(f * xhat, axis=-1, keepdims=True)
        )
        out = extra_ref[at, :] + grad
        out_ref[at, :] = out
        new = [column_sum(e), column_sum(e * xhat)]
        if other_ref is not None:
            new.append(column_sum(out * other_ref[at, :]))
        return tuple(c + n for c, n in zip(carry, new))

    zero = jnp.zeros((1, v_ref.shape[1]), f32)
    count = 2 if other_ref is None else 3
    total = lax.fori_loop(0, full_len // rows, step, (zero,) * count)
    sums_ref[...] = jnp.zeros_like(sums_ref)
    sums_ref[0:1, :] = total[0]
    sums_ref[1:2, :] = total[1] * row(vec_ref, gain)
    sums_ref[2:3, :] = total[1] * (1.0 + row(vec_ref, scale))
    if other_ref is not None:
        sums_ref[3:4, :] = total[2]


def qkv_kernel(x_ref, vec_ref, w_ref, out_ref, left, right):
    @pl.when(pl.program_id(0) == 0)
    def _():
        put_left(left, modulated(x_ref[...], vec_ref, ATTN_GAIN, ATTN_SHIFT, ATTN_SCALE), 1)

    put_right(right, w_ref[...], 0)
    out_ref[...] = dot_nn(left[...], right[...])


def proj_kernel(
    len_ref, att_ref, x_ref, vec_ref, w_ref, proj_ref, middle_ref, sums_ref, left, right
):
    @pl.when(pl.program_id(0) == 0)
    def _():
        put_left(left, att_ref[...], 1)

    put_right(right, w_ref[...], 0)
    proj = dot_nn(left[...], right[...])
    x = x_ref[...]
    branch = row(vec_ref, ATTN_GATE) * proj
    proj_ref[...] = proj
    middle_ref[...] = x + branch
    valid = lax.broadcasted_iota(jnp.int32, x.shape, 0) < len_ref[0]
    sums_ref[...] = jnp.zeros_like(sums_ref)
    sums_ref[0:1, :] = column_sum(jnp.where(valid, x * x, 0.0))
    sums_ref[1:2, :] = column_sum(jnp.where(valid, branch * branch, 0.0))


def mlp_forward_kernel(
    len_ref,
    middle_ref,
    vec_ref,
    up_ref,
    bias_ref,
    down_ref,
    act_ref,
    slope_ref,
    down_out_ref,
    out_ref,
    sums_ref,
    left,
    up_cat,
    act_cat,
    down_cat,
    acc,
    *,
    rows,
):
    step = pl.program_id(0)
    full_len = middle_ref.shape[0]

    @pl.when(step == 0)
    def _():
        put_left(left, modulated(middle_ref[...], vec_ref, MLP_GAIN, MLP_SHIFT, MLP_SCALE), 1)
        acc[...] = jnp.zeros_like(acc)

    put_right(up_cat, up_ref[...], 0)
    put_right(down_cat, down_ref[...], 0)
    for block in range(full_len // rows):
        at = pl.ds(block * rows, rows)
        pre = dot_nn(left[at, :], up_cat[...]) + bias_ref[...]
        act, slope = gelu_and_slope(pre)
        act_ref[at, :] = act
        slope_ref[at, :] = slope
        put_left(act_cat.at[at, :], act, 1)
        acc[at, :] += dot_nn(act_cat[at, :], down_cat[...])

    @pl.when(step == pl.num_programs(0) - 1)
    def _():
        down_out = acc[...] + row(vec_ref, DOWN_BIAS)
        branch = row(vec_ref, MLP_GATE) * down_out
        down_out_ref[...] = down_out
        out_ref[...] = middle_ref[...] + branch
        valid = lax.broadcasted_iota(jnp.int32, branch.shape, 0) < len_ref[0]
        sums_ref[...] = jnp.zeros_like(sums_ref)
        sums_ref[0:1, :] = column_sum(jnp.where(valid, branch * branch, 0.0))


def down_grad_kernel(cot_ref, down_out_ref, vec_ref, act_ref, grad_ref, sums_ref, left, right):
    @pl.when(pl.program_id(0) == 0)
    def _():
        cot = cot_ref[...]
        grad = cot * row(vec_ref, MLP_GATE)
        put_left(left, grad.T, 1)
        sums_ref[...] = jnp.zeros_like(sums_ref)
        sums_ref[0:1, :] = column_sum(cot * down_out_ref[...])
        sums_ref[1:2, :] = column_sum(grad)

    put_right(right, act_ref[...], 0)
    grad_ref[...] = dot_nn(left[...], right[...]).T


def mlp_backward_kernel(
    cot_ref,
    middle_ref,
    proj_ref,
    vec_ref,
    down_ref,
    up_ref,
    slope_ref,
    up_grad_ref,
    bias_grad_ref,
    middle_grad_ref,
    sums_ref,
    left,
    turned,
    down_cat,
    up_cat,
    pre_cat,
    pre_stack,
    acc,
    *,
    rows,
):
    step = pl.program_id(0)
    full_len = middle_ref.shape[0]

    @pl.when(step == 0)
    def _():
        put_left(left, cot_ref[...] * row(vec_ref, MLP_GATE), 1)
        normed = modulated(middle_ref[...], vec_ref, MLP_GAIN, MLP_SHIFT, MLP_SCALE)
        put_left(turned, normed.T, 1)
        acc[...] = jnp.zeros_like(acc)

    put_right(down_cat, down_ref[...], 1)
    put_right(up_cat, up_ref[...], 1)
    bias_grad = jnp.zeros_like(bias_grad_ref)
    for block in range(full_len // rows):
        at = pl.ds(block * rows, rows)
        pre_grad = dot_nt(left[at, :], down_cat[...]) * slope_ref[at, :]
        bias_grad += column_sum(pre_grad)
        hi, lo = split_bf16(pre_grad)
        columns = hi.shape[1]
        for place, part in enumerate((hi, lo, hi)):
            pre_cat[at, place * columns : (place + 1) * columns] = part
        for place, part in enumerate((hi, hi, lo)):
            pre_stack[pl.ds(place * full_len + block * rows, rows), :] = part
        acc[at, :] += dot_nt(pre_cat[at, :], up_cat[...])
    bias_grad_ref[...] = bias_grad
    up_grad_ref[...] = dot_nn(turned[...], pre_stack[...])

    @pl.when(step == pl.num_programs(0) - 1)
    def _():
        norm_backward(
            acc, middle_ref, cot_ref, vec_ref, MLP_GAIN, MLP_SCALE, middle_grad_ref, sums_ref, proj_ref
        )


def proj_backward_kernel(
    grad_ref, grad_block_ref, att_ref, vec_ref, vec_block_ref, w_ref, out_ref, w_grad_ref,
    left, turned, w_cat, stack,
):
    @pl.when(pl.program_id(0) == 0)
    def _():
        put_left(left, grad_ref[...] * row(vec_ref, ATTN_GATE), 1)
        put_left(turned, att_ref[...].T, 1)

    put_right(w_cat, w_ref[...], 1)
    out_ref[...] = dot_nt(left[...], w_cat[...])
    put_right(stack, grad_block_ref[...] * row(vec_block_ref, ATTN_GATE), 0)
    w_grad_ref[...] = dot_nn(turned[...], stack[...])


def tokens_grad_kernel(
    grad_ref, w_ref, x_ref, extra_ref, vec_ref, out_ref, sums_ref, left, w_cat, acc
):
    step = pl.program_id(0)

    @pl.when(step == 0)
    def _():
        acc[...] = jnp.zeros_like(acc)

    put_left(left, grad_ref[...], 1)
    put_right(w_cat, w_ref[...], 1)
    acc[...] += dot_nt(left[...], w_cat[...])

    @pl.when(step == pl.num_programs(0) - 1)
    def _():
        norm_backward(acc, x_ref, extra_ref, vec_ref, ATTN_GAIN, ATTN_SCALE, out_ref, sums_ref, None)


def qkv_grad_kernel(x_ref, vec_ref, grad_ref, out_ref, turned, stack):
    @pl.when(pl.program_id(0) == 0)
    def _():
        normed = modulated(x_ref[...], vec_ref, ATTN_GAIN, ATTN_SHIFT, ATTN_SCALE)
        put_left(turned, normed.T, 1)

    put_right(stack, grad_ref[...], 0)
    out_ref[...] = dot_nn(turned[...], stack[...])


def whole(shape):
    return pl.BlockSpec(shape, lambda *ids: (0,) * len(shape), pipeline_mode=pl.Buffered(1))


def by_columns(rows, columns):
    return pl.BlockSpec((rows, columns), lambda j, *refs: (0, j))


def by_rows(rows, columns):
    return pl.BlockSpec((rows, columns), lambda j, *refs: (j, 0))


def dense(body, grid, in_specs, out_specs, out_shapes, scratch, products, args, scalars=0):
    moved = sum(a.size for a in args) + sum(o.size for o in out_shapes)
    return pl.pallas_call(
        body,
        out_shape=tuple(out_shapes),
        grid_spec=pltpu.PrefetchScalarGridSpec(
            num_scalar_prefetch=scalars,
            grid=(grid,),
            in_specs=in_specs,
            out_specs=tuple(out_specs),
            scratch_shapes=[pltpu.VMEM(shape, kind) for shape, kind in scratch],
        ),
        compiler_params=pltpu.CompilerParams(vmem_limit_bytes=60 << 20),
        cost_estimate=pl.CostEstimate(flops=6 * products, bytes_accessed=4 * moved, transcendentals=0),
    )(*args)


def array(*shape):
    return jax.ShapeDtypeStruct(shape, f32)


def mm_qkv(x, vectors, weight):
    t, d = x.shape
    n = weight.shape[1]
    c = COLUMNS
    return dense(
        qkv_kernel,
        n // c,
        [whole((t, d)), whole((VECTORS, d)), by_columns(d, c)],
        [by_columns(t, c)],
        [array(t, n)],
        [((t, 3 * d), bf16), ((3 * d, c), bf16)],
        t * d * n,
        (x, vectors, weight),
    )[0]


def mm_proj(length, attended, x, vectors, weight):
    t, d = x.shape
    c = COLUMNS
    return dense(
        proj_kernel,
        d // c,
        [whole((t, d)), by_columns(t, c), by_columns(VECTORS, c), by_columns(d, c)],
        [by_columns(t, c), by_columns(t, c), by_columns(8, c)],
        [array(t, d), array(t, d), array(8, d)],
        [((t, 3 * d), bf16), ((3 * d, c), bf16)],
        t * d * d,
        (length, attended, x, vectors, weight),
        scalars=1,
    )


def mlp_forward(length, middle, vectors, up, up_bias, down):
    t, d = middle.shape
    n = up.shape[1]
    c = 2 * COLUMNS
    return dense(
        partial(mlp_forward_kernel, rows=min(256, t)),
        n // c,
        [whole((t, d)), whole((VECTORS, d)), by_columns(d, c), by_columns(1, c), by_rows(c, d)],
        [by_columns(t, c), by_columns(t, c), whole((t, d)), whole((t, d)), whole((8, d))],
        [array(t, n), array(t, n), array(t, d), array(t, d), array(8, d)],
        [
            ((t, 3 * d), bf16),
            ((3 * d, c), bf16),
            ((t, 3 * c), bf16),
            ((3 * c, d), bf16),
            ((t, d), f32),
        ],
        2 * t * d * n,
        (length, middle, vectors, up, up_bias, down),
        scalars=1,
    )


def dw_down(cot, down_out, vectors, act):
    t, d = cot.shape
    n = act.shape[1]
    c = COLUMNS
    return dense(
        down_grad_kernel,
        n // c,
        [whole((t, d)), whole((t, d)), whole((VECTORS, d)), by_columns(t, c)],
        [by_rows(c, d), whole((8, d))],
        [array(n, d), array(8, d)],
        [((d, 3 * t), bf16), ((3 * t, c), bf16)],
        t * d * n,
        (cot, down_out, vectors, act),
    )


def mlp_backward(cot, middle, proj_out, vectors, down, up, slope):
    t, d = cot.shape
    n = up.shape[1]
    c = COLUMNS
    return dense(
        partial(mlp_backward_kernel, rows=min(256, t)),
        n // c,
        [
            whole((t, d)),
            whole((t, d)),
            whole((t, d)),
            whole((VECTORS, d)),
            by_rows(c, d),
            by_columns(d, c),
            by_columns(t, c),
        ],
        [by_columns(d, c), by_columns(1, c), whole((t, d)), whole((8, d))],
        [array(d, n), array(1, n), array(t, d), array(8, d)],
        [
            ((t, 3 * d), bf16),
            ((d, 3 * t), bf16),
            ((c, 3 * d), bf16),
            ((d, 3 * c), bf16),
            ((t, 3 * c), bf16),
            ((3 * t, c), bf16),
            ((t, d), f32),
        ],
        3 * t * d * n,
        (cot, middle, proj_out, vectors, down, up, slope),
    )


def proj_backward(middle_grad, attended, vectors, weight):
    t, d = middle_grad.shape
    c = COLUMNS
    return dense(
        proj_backward_kernel,
        d // c,
        [
            whole((t, d)),
            by_columns(t, c),
            whole((t, d)),
            whole((VECTORS, d)),
            by_columns(VECTORS, c),
            by_rows(c, d),
        ],
        [by_columns(t, c), by_columns(d, c)],
        [array(t, d), array(d, d)],
        [((t, 3 * d), bf16), ((d, 3 * t), bf16), ((c, 3 * d), bf16), ((3 * t, c), bf16)],
        2 * t * d * d,
        (middle_grad, middle_grad, attended, vectors, vectors, weight),
    )


def mm_tokens_grad(qkv_grad, weight, x, middle_grad, vectors):
    t, d = x.shape
    n = weight.shape[1]
    c = COLUMNS
    return dense(
        tokens_grad_kernel,
        n // c,
        [by_columns(t, c), by_columns(d, c), whole((t, d)), whole((t, d)), whole((VECTORS, d))],
        [whole((t, d)), whole((8, d))],
        [array(t, d), array(8, d)],
        [((t, 3 * c), bf16), ((d, 3 * c), bf16), ((t, d), f32)],
        t * d * n,
        (qkv_grad, weight, x, middle_grad, vectors),
    )


def dw_qkv(x, vectors, qkv_grad):
    t, d = x.shape
    n = qkv_grad.shape[1]
    c = COLUMNS
    return dense(
        qkv_grad_kernel,
        n // c,
        [whole((t, d)), whole((VECTORS, d)), by_columns(t, c)],
        [by_columns(d, c)],
        [array(d, n)],
        [((d, 3 * t), bf16), ((3 * t, c), bf16)],
        t * d * n,
        (x, vectors, qkv_grad),
    )[0]


def padded_row(pieces):
    row = jnp.concatenate([piece.reshape(-1) for piece in pieces])
    return jnp.pad(row, (0, -row.shape[0] % 128))[None, :]


def cut(row, sizes):
    out, start = [], 0
    for size in sizes:
        out.append(row[:, start : start + size])
        start += size
    return out


def shards(
    tokens,
    time_embed,
    lengths,
    positions,
    ada_weight,
    ada_bias,
    attn_gain,
    qkv_weight,
    proj_weight,
    mlp_gain,
    up_weight,
    up_bias,
    down_weight,
    down_bias,
    cotangent,
):
    groups = lax.axis_size("seq")
    owners = lax.axis_size("fsdp")
    mine_seq = lax.axis_index("seq")
    mine_fsdp = lax.axis_index("fsdp")
    seqs_here, local_len, width = tokens.shape
    cond = time_embed.shape[1]
    full_len = local_len * groups
    assert seqs_here == groups

    def to_sequence(field):
        return lax.all_to_all(field, "seq", split_axis=0, concat_axis=1, tiled=True)[0]

    def to_tokens(field):
        pieces = field.reshape(groups, local_len, width)
        return lax.all_to_all(pieces, "seq", split_axis=0, concat_axis=0, tiled=True)

    def gather(shard):
        return lax.all_gather(shard, "fsdp", axis=0, tiled=True)

    def rows_of_all(row, axes):
        count = lax.axis_size(axes)
        sent = jnp.broadcast_to(row[None], (count,) + row.shape)
        return lax.all_to_all(sent, axes, split_axis=0, concat_axis=0, tiled=True)[:, 0]

    x = to_sequence(tokens)
    places = lax.all_gather(positions, "seq", axis=0)
    places = lax.dynamic_slice(places, (0, mine_seq, 0), (groups, 1, local_len)).reshape(full_len)
    length = lax.dynamic_slice(lengths, (mine_seq,), (1,))
    small = [time_embed, ada_bias, attn_gain, mlp_gain, up_bias, down_bias]
    small_sizes = [piece.size for piece in small]
    packed = gather(padded_row(small))
    time_all, ada_bias_full, attn_gain_full, mlp_gain_full, up_bias_full, down_bias_full = cut(
        packed, small_sizes
    )
    time_all = time_all.reshape(owners * seqs_here, cond)
    ada_bias_full, attn_gain_full, mlp_gain_full, up_bias_full, down_bias_full = (
        piece.reshape(1, -1)
        for piece in (ada_bias_full, attn_gain_full, mlp_gain_full, up_bias_full, down_bias_full)
    )
    silu_all = jax.nn.silu(time_all)
    ada_rows = ada_weight.shape[0]
    silu_cols = lax.dynamic_slice(silu_all, (0, mine_fsdp * ada_rows), (owners * seqs_here, ada_rows))
    silu_group = lax.dynamic_slice(
        silu_cols.reshape(owners, seqs_here, ada_rows), (0, mine_seq, 0), (owners, 1, ada_rows)
    )[:, 0]
    partial_rows = jnp.dot(silu_group, ada_weight, precision=highest)
    partial_rows = lax.dynamic_slice(
        gather(partial_rows[None]),
        (0, mine_fsdp, 0),
        (owners, 1, partial_rows.shape[1]),
    )[:, 0]
    modulation = jnp.sum(partial_rows, axis=0, keepdims=True) + ada_bias_full
    shift_attn, scale_attn, gate_attn, shift_mlp, scale_mlp, gate_mlp = jnp.split(modulation, 6, axis=1)
    vectors = [
        attn_gain_full,
        shift_attn,
        scale_attn,
        gate_attn,
        mlp_gain_full,
        shift_mlp,
        scale_mlp,
        gate_mlp,
        down_bias_full,
    ]
    vectors = jnp.concatenate(vectors + [jnp.zeros((VECTORS - len(vectors), width), f32)], axis=0)
    qkv_full = gather(qkv_weight)
    proj_full = gather(proj_weight)
    up_full = gather(up_weight)
    down_full = gather(down_weight)
    cosine, sine = rotary_tables(places)

    qkv = mm_qkv(x, vectors, qkv_full)
    cot_in, _ = lax.optimization_barrier((cotangent, x))
    cot = to_sequence(cot_in)
    attended, lse = attention_forward(length, qkv, cosine, sine)
    proj_out, middle, attn_sums = mm_proj(length, attended, x, vectors, proj_full)
    hidden_act, gelu_slope, down_out, block_out, mlp_sums = mlp_forward(
        length, middle, vectors, up_full, up_bias_full, down_full
    )
    block_out = to_tokens(block_out)

    def scatter(grad):
        return lax.psum_scatter(grad, "fsdp", scatter_dimension=0, tiled=True)

    down_weight_grad, down_sums = dw_down(cot, down_out, vectors, hidden_act)
    down_shard = scatter(down_weight_grad)
    up_weight_grad, up_bias_grad, middle_grad, mlp_norm_sums = mlp_backward(
        cot, middle, proj_out, vectors, down_full, up_full, gelu_slope
    )
    up_shard = scatter(up_weight_grad)
    attended_grad, proj_weight_grad = proj_backward(middle_grad, attended, vectors, proj_full)
    proj_shard = scatter(proj_weight_grad)
    gate_mlp_grad, down_bias_grad = down_sums[0], down_sums[1]
    shift_mlp_grad, scale_mlp_grad, mlp_gain_grad, gate_attn_grad = (mlp_norm_sums[i] for i in range(4))
    sums = jnp.stack(
        [
            jnp.sum(attn_sums[0]),
            jnp.sum(attn_sums[1]),
            jnp.sum(mlp_sums[0]),
            length[0].astype(f32),
        ]
    )
    early = [
        gate_attn_grad,
        shift_mlp_grad,
        scale_mlp_grad,
        gate_mlp_grad,
        mlp_gain_grad,
        up_bias_grad,
        down_bias_grad,
        sums,
    ]
    early_all = rows_of_all(padded_row(early), ("fsdp", "seq"))
    gate_attn_rows, shift_mlp_rows, scale_mlp_rows, gate_mlp_rows, *early_rest = cut(
        early_all, [piece.size for piece in early]
    )

    qkv_grad = attention_backward(length, qkv, cosine, sine, attended, lse, attended_grad)
    tokens_grad, attn_norm_sums = mm_tokens_grad(qkv_grad, qkv_full, x, middle_grad, vectors)
    shift_attn_grad, scale_attn_grad, attn_gain_grad = (attn_norm_sums[i] for i in range(3))
    tokens_grad = to_tokens(tokens_grad)
    qkv_shard = scatter(dw_qkv(x, vectors, qkv_grad))
    late = [shift_attn_grad, scale_attn_grad, attn_gain_grad]
    late_all = lax.all_gather(padded_row(late), "fsdp", axis=0, tiled=True)
    late_all = lax.all_gather(lax.optimization_barrier(late_all), "seq", axis=0)
    late_all = jnp.swapaxes(late_all, 0, 1).reshape(owners * groups, -1)
    shift_attn_rows, scale_attn_rows, attn_gain_rows = cut(late_all, [piece.size for piece in late])
    modulation_rows = jnp.concatenate(
        [shift_attn_rows, scale_attn_rows, gate_attn_rows, shift_mlp_rows, scale_mlp_rows, gate_mlp_rows],
        axis=1,
    )

    ada_weight_grad = lax.dot_general(
        silu_cols, modulation_rows, (((0,), (0,)), ((), ())), precision=highest
    )
    time_cols = lax.dot_general(modulation_rows, ada_weight, (((1,), (1,)), ((), ())), precision=highest)
    time_cols = lax.all_gather(time_cols, "fsdp", axis=0)
    time_rows = lax.dynamic_slice(
        time_cols, (0, mine_fsdp * seqs_here, 0), (owners, seqs_here, ada_rows)
    )
    time_part = jnp.swapaxes(time_rows, 0, 1).reshape(seqs_here, cond)
    _, silu_back = jax.vjp(jax.nn.silu, time_embed)
    (time_grad,) = silu_back(time_part)

    def owned(rows):
        total = jnp.sum(rows, axis=0)
        size = total.shape[0] // owners
        return lax.dynamic_slice(total, (mine_fsdp * size,), (size,))

    mlp_gain_rows, up_bias_rows, down_bias_rows, sums_rows = early_rest
    totals = jnp.sum(sums_rows, axis=0)
    rms = jnp.sqrt(totals[:3] / (totals[3] * width))
    down_total, up_total, proj_total = lax.psum((down_shard, up_shard, proj_shard), "seq")
    qkv_total = lax.psum(qkv_shard, "seq")
    return (
        block_out,
        tokens_grad,
        time_grad,
        ada_weight_grad,
        owned(modulation_rows),
        owned(attn_gain_rows),
        qkv_total,
        proj_total,
        owned(mlp_gain_rows),
        up_total,
        owned(up_bias_rows),
        down_total,
        owned(down_bias_rows),
        rms[0],
        rms[1],
        rms[2],
    )


def solution(mesh):
    field = P("fsdp", "seq", None)
    matrix = P("fsdp", None)
    vector = P("fsdp")

    return jax.shard_map(
        shards,
        mesh=mesh,
        in_specs=(
            field,
            matrix,
            vector,
            P("fsdp", "seq"),
            matrix,
            vector,
            vector,
            matrix,
            matrix,
            vector,
            matrix,
            vector,
            matrix,
            vector,
            field,
        ),
        out_specs=(
            field,
            field,
            matrix,
            matrix,
            vector,
            vector,
            matrix,
            matrix,
            vector,
            matrix,
            vector,
            matrix,
            vector,
            P(),
            P(),
            P(),
        ),
        check_vma=False,
    )
```

```python
from functools import partial

import jax
import jax.numpy as jnp
from jax import lax
from jax.experimental import pallas as pl
from jax.experimental.pallas import tpu as pltpu
from jax.sharding import PartitionSpec as P


HD = 64
PAIR = 2 * HD
LOG2E = 1.4426950408889634
LN2 = 0.6931471805599453

epsilon = 1e-05
highest = lax.Precision.HIGHEST
f32 = jnp.float32
bf16 = jnp.bfloat16


def gelu_and_slope(value):
    square = value * value
    t = jnp.tanh(0.7978845608028654 * (value + 0.044715 * value * square))
    slope = 0.5 * (1.0 + t) + 0.5 * value * (1.0 - t * t) * (
        0.7978845608028654 * (1.0 + 3 * 0.044715 * square)
    )
    return 0.5 * value * (1.0 + t), slope


def rotary_tables(positions):
    inverse = 1.0 / 10000.0 ** (jnp.arange(0, HD, 2, dtype=f32) / HD)
    angles = positions.astype(f32)[:, None] * inverse
    cosine, sine = jnp.cos(angles), jnp.sin(angles)
    return jnp.tile(cosine, (1, 4)), jnp.tile(sine, (1, 4))


def rotate(u, cosine, sine, lane):
    first = (lane % HD) < (HD // 2)
    turned = jnp.where(first, -pltpu.roll(u, PAIR - HD // 2, 1), pltpu.roll(u, HD // 2, 1))
    return u * cosine + turned * sine


def rotate_back(g, cosine, sine, lane):
    first = (lane % HD) < (HD // 2)
    w = g * sine
    return g * cosine + jnp.where(first, pltpu.roll(w, PAIR - HD // 2, 1), -pltpu.roll(w, HD // 2, 1))


def parts(u):
    hi = u.astype(bf16).astype(f32)
    return hi, (u - hi).astype(bf16).astype(f32)


def both(u, head, lane):
    turned = pltpu.roll(u, HD, 1)
    return jnp.where((lane < HD) == (head == 0), u, turned)


def beside(left, right, head, lane):
    low = left if head == 0 else pltpu.roll(left, HD, 1)
    high_lanes = pltpu.roll(right, HD, 1) if head == 0 else right
    return jnp.where(lane < HD, low, high_lanes)


def three_terms(column, lane):
    a = column.astype(bf16).astype(f32)
    b = (column - a).astype(bf16).astype(f32)
    c = column - a - b
    return jnp.where(lane == HD, a, jnp.where(lane == HD + 1, b, jnp.where(lane == HD + 2, c, 0.0)))


def split_bf16(u):
    hi = u.astype(bf16)
    return hi, (u - hi.astype(f32)).astype(bf16)


def dot_nt(a, b):
    return lax.dot_general(a, b, (((1,), (1,)), ((), ())), preferred_element_type=f32)


def dot_nn(a, b):
    return lax.dot_general(a, b, (((1,), (0,)), ((), ())), preferred_element_type=f32)


def forward_kernel(
    len_ref, q_ref, k_ref, v_ref, cos_ref, sin_ref, out_ref, lse_ref, qs, ks, vs, acc, *, rows
):
    full_len = q_ref.shape[0]
    lane = lax.broadcasted_iota(jnp.int32, (full_len, PAIR), 1)
    place = lax.broadcasted_iota(jnp.int32, (full_len, PAIR), 0)
    cosine, sine = cos_ref[...], sin_ref[...]
    q = rotate(q_ref[...], cosine, sine, lane) * (HD**-0.5 * LOG2E)
    k = rotate(k_ref[...], cosine, sine, lane)
    q_hi, q_lo = parts(q)
    k_hi, k_lo = parts(k)
    v_hi, v_lo = parts(v_ref[...])
    bias = jnp.where(place < len_ref[0], 0.0, -1e30)
    for head in range(2):
        qs[head, :, :PAIR] = both(q_hi, head, lane).astype(bf16)
        qs[head, :, PAIR:] = jnp.where(
            lane < HD, beside(q_lo, q_lo, head, lane), jnp.where(lane == HD, 1.0, 0.0)
        ).astype(bf16)
        ks[head, :, :PAIR] = beside(k_hi, k_lo, head, lane).astype(bf16)
        ks[head, :, PAIR:] = jnp.where(
            lane < HD, beside(k_hi, k_hi, head, lane), jnp.where(lane == HD, bias, 0.0)
        ).astype(bf16)
        vs[head] = beside(v_hi, v_lo, head, lane).astype(bf16)

    low = lax.broadcasted_iota(jnp.int32, (rows, PAIR), 1) < HD

    def step(block, carry):
        at = pl.ds(pl.multiple_of(block * rows, rows), rows)
        outs, lses = [], []
        for head in range(2):
            scores = dot_nt(qs[head, at, :], ks[head])
            largest = jnp.max(scores, axis=1, keepdims=True)
            expo = jnp.exp2(scores - largest)
            total = jnp.sum(expo, axis=1, keepdims=True)
            hi, lo = split_bf16(expo)
            both_parts = dot_nn(hi, vs[head]) + dot_nn(lo, vs[head])
            outs.append((both_parts + pltpu.roll(both_parts, HD, 1)) / total)
            lses.append(largest + jnp.log2(total))
        out_ref[at, :] = jnp.where(low, outs[0], outs[1])
        lse_ref[at, :] = jnp.where(low, lses[0], lses[1])
        return carry

    lax.fori_loop(0, full_len // rows, step, 0)


def backward_kernel(
    len_ref,
    q_ref,
    k_ref,
    v_ref,
    cos_ref,
    sin_ref,
    out_in_ref,
    lse_ref,
    do_ref,
    grad_ref,
    qs,
    ks,
    vs,
    dos,
    kd,
    qt,
    dot_t,
    dq,
    dkt,
    dvt,
    *,
    rows,
):
    full_len = q_ref.shape[0]
    which = pl.program_id(1)
    lane = lax.broadcasted_iota(jnp.int32, (full_len, PAIR), 1)

    @pl.when(which == 0)
    def _():
        place = lax.broadcasted_iota(jnp.int32, (full_len, PAIR), 0)
        cosine, sine = cos_ref[...], sin_ref[...]
        q = rotate(q_ref[...], cosine, sine, lane) * (HD**-0.5 * LOG2E)
        k = rotate(k_ref[...], cosine, sine, lane)
        out_grad = do_ref[...]
        q_hi, q_lo = parts(q)
        k_hi, k_lo = parts(k)
        v_hi, v_lo = parts(v_ref[...])
        g_hi, g_lo = parts(out_grad)
        product = out_grad * out_in_ref[...]
        lse = lse_ref[...]
        bias = jnp.where(place < len_ref[0], 0.0, -1e30)
        ones = jnp.where((lane >= HD) & (lane < HD + 3), 1.0, 0.0)
        for head in range(2):
            mine = (lane < HD) == (head == 0)
            delta = jnp.sum(jnp.where(mine, product, 0.0), axis=1, keepdims=True)
            lse_head = jnp.max(jnp.where(mine, lse, -3e38), axis=1, keepdims=True)
            qs[head, :, :PAIR] = both(q_hi, head, lane).astype(bf16)
            qs[head, :, PAIR:] = jnp.where(
                lane < HD,
                beside(q_lo, q_lo, head, lane),
                three_terms(-lse_head, lane) + jnp.where(lane == HD + 3, 1.0, 0.0),
            ).astype(bf16)
            ks[head, :, :PAIR] = beside(k_hi, k_lo, head, lane).astype(bf16)
            ks[head, :, PAIR:] = jnp.where(
                lane < HD, beside(k_hi, k_hi, head, lane), ones + jnp.where(lane == HD + 3, bias, 0.0)
            ).astype(bf16)
            dos[head, :, :PAIR] = both(g_hi, head, lane).astype(bf16)
            dos[head, :, PAIR:] = jnp.where(
                lane < HD, beside(g_lo, g_lo, head, lane), three_terms(-delta, lane)
            ).astype(bf16)
            vs[head, :, :PAIR] = beside(v_hi, v_lo, head, lane).astype(bf16)
            vs[head, :, PAIR:] = jnp.where(lane < HD, beside(v_hi, v_hi, head, lane), ones).astype(bf16)
            kd[head] = beside(k_hi, k_lo, head, lane).astype(bf16)
            qt[head] = beside(q_hi, q_lo, head, lane).T.astype(bf16)
            dot_t[head] = beside(g_hi, g_lo, head, lane).T.astype(bf16)
        dkt[...] = jnp.zeros_like(dkt)
        dvt[...] = jnp.zeros_like(dvt)
        low = lax.broadcasted_iota(jnp.int32, (rows, PAIR), 1) < HD

        def step(block, carry):
            at = pl.ds(pl.multiple_of(block * rows, rows), rows)
            outs = []
            for head in range(2):
                weights = jnp.exp2(dot_nt(qs[head, at, :], ks[head]))
                score_grad = weights * dot_nt(dos[head, at, :], vs[head])
                w_hi, w_lo = split_bf16(weights)
                s_hi, s_lo = split_bf16(score_grad)
                both_parts = dot_nn(s_hi, kd[head]) + dot_nn(s_lo, kd[head])
                outs.append(both_parts + pltpu.roll(both_parts, HD, 1))
                q_t = qt[head, :, at]
                g_t = dot_t[head, :, at]
                dkt[head] += dot_nn(q_t, s_hi) + dot_nn(q_t, s_lo)
                dvt[head] += dot_nn(g_t, w_hi) + dot_nn(g_t, w_lo)
            dq[at, :] = jnp.where(low, outs[0], outs[1])
            return carry

        lax.fori_loop(0, full_len // rows, step, 0)
        grad_ref[...] = rotate_back(dq[...] * HD**-0.5, cosine, sine, lane)

    @pl.when(which == 1)
    def _():
        stacked = jnp.concatenate([dkt[h, :HD, :] + dkt[h, HD:, :] for h in range(2)], axis=0)
        grad_ref[...] = rotate_back(stacked.T * LN2, cos_ref[...], sin_ref[...], lane)

    @pl.when(which == 2)
    def _():
        stacked = jnp.concatenate([dvt[h, :HD, :] + dvt[h, HD:, :] for h in range(2)], axis=0)
        grad_ref[...] = stacked.T


def attention_forward(length, qkv, cosine, sine):
    full_len, three = qkv.shape
    width = three // 3
    pairs = width // PAIR
    rows = min(256, full_len)

    def column(offset):
        return pl.BlockSpec((full_len, PAIR), lambda p, ln: (0, p + offset))

    table = pl.BlockSpec((full_len, PAIR), lambda p, ln: (0, 0))
    wide = jax.ShapeDtypeStruct((full_len, width), f32)
    return pl.pallas_call(
        partial(forward_kernel, rows=rows),
        name="attention_forward",
        out_shape=(wide, wide),
        grid_spec=pltpu.PrefetchScalarGridSpec(
            num_scalar_prefetch=1,
            grid=(pairs,),
            in_specs=[column(0), column(pairs), column(2 * pairs), table, table],
            out_specs=(column(0), column(0)),
            scratch_shapes=[
                pltpu.VMEM((2, full_len, 2 * PAIR), bf16),
                pltpu.VMEM((2, full_len, 2 * PAIR), bf16),
                pltpu.VMEM((2, full_len, PAIR), bf16),
                pltpu.VMEM((8, 128), f32),
            ],
        ),
        cost_estimate=pl.CostEstimate(
            flops=24 * full_len * full_len * width, bytes_accessed=20 * full_len * width, transcendentals=0
        ),
    )(length, qkv, qkv, qkv, cosine, sine)


def attention_backward(length, qkv, cosine, sine, attended, lse, out_grad):
    full_len, three = qkv.shape
    width = three // 3
    pairs = width // PAIR
    rows = min(256, full_len)

    def column(offset):
        return pl.BlockSpec((full_len, PAIR), lambda p, c, ln: (0, p + offset))

    table = pl.BlockSpec((full_len, PAIR), lambda p, c, ln: (0, 0))
    stacked = pltpu.VMEM((2, full_len, 2 * PAIR), bf16)
    turned = pltpu.VMEM((2, PAIR, full_len), bf16)
    summed = pltpu.VMEM((2, PAIR, full_len), f32)
    return pl.pallas_call(
        partial(backward_kernel, rows=rows),
        name="attention_backward",
        out_shape=jax.ShapeDtypeStruct((full_len, three), f32),
        grid_spec=pltpu.PrefetchScalarGridSpec(
            num_scalar_prefetch=1,
            grid=(pairs, 3),
            in_specs=[
                column(0),
                column(pairs),
                column(2 * pairs),
                table,
                table,
                column(0),
                column(0),
                column(0),
            ],
            out_specs=pl.BlockSpec((full_len, PAIR), lambda p, c, ln: (0, c * pairs + p)),
            scratch_shapes=[
                stacked,
                stacked,
                stacked,
                stacked,
                pltpu.VMEM((2, full_len, PAIR), bf16),
                turned,
                turned,
                pltpu.VMEM((full_len, PAIR), f32),
                summed,
                summed,
            ],
        ),
        cost_estimate=pl.CostEstimate(
            flops=60 * full_len * full_len * width, bytes_accessed=32 * full_len * width, transcendentals=0
        ),
    )(length, qkv, qkv, qkv, cosine, sine, attended, lse, out_grad)


ATTN_GAIN, ATTN_SHIFT, ATTN_SCALE, ATTN_GATE, MLP_GAIN, MLP_SHIFT, MLP_SCALE, MLP_GATE, DOWN_BIAS = range(9)
VECTORS = 16
COLUMNS = 256


def put_left(ref, u, axis):
    hi, lo = split_bf16(u)
    size = u.shape[axis]
    for place, part in enumerate((hi, lo, hi)):
        if axis == 1:
            ref[:, place * size : (place + 1) * size] = part
        else:
            ref[place * size : (place + 1) * size, :] = part


def put_right(ref, u, axis):
    hi, lo = split_bf16(u)
    size = u.shape[axis]
    for place, part in enumerate((hi, hi, lo)):
        if axis == 1:
            ref[:, place * size : (place + 1) * size] = part
        else:
            ref[place * size : (place + 1) * size, :] = part


def normalized(v):
    average = jnp.mean(v, axis=-1, keepdims=True)
    centered = v - average
    rstd = lax.rsqrt(jnp.mean(centered * centered, axis=-1, keepdims=True) + epsilon)
    return centered * rstd, rstd


def modulated(v, vec_ref, gain, shift, scale):
    xhat, _ = normalized(v)
    return xhat * row(vec_ref, gain) * (1.0 + row(vec_ref, scale)) + row(vec_ref, shift)


def row(ref, index):
    return ref[index : index + 1, :]


def column_sum(u):
    return jnp.sum(u, axis=0, keepdims=True)


def norm_backward(e_ref, v_ref, extra_ref, vec_ref, gain, scale, out_ref, sums_ref, other_ref):
    full_len = v_ref.shape[0]
    rows = min(128, full_len)
    factor = (1.0 + row(vec_ref, scale)) * row(vec_ref, gain)

    def step(block, carry):
        at = pl.ds(pl.multiple_of(block * rows, rows), rows)
        e = e_ref[at, :]
        xhat, rstd = normalized(v_ref[at, :])
        f = e * factor
        grad = rstd * (
            f
            - jnp.mean(f, axis=-1, keepdims=True)
            - xhat * jnp.mean(f * xhat, axis=-1, keepdims=True)
        )
        out = extra_ref[at, :] + grad
        out_ref[at, :] = out
        new = [column_sum(e), column_sum(e * xhat)]
        if other_ref is not None:
            new.append(column_sum(out * other_ref[at, :]))
        return tuple(c + n for c, n in zip(carry, new))

    zero = jnp.zeros((1, v_ref.shape[1]), f32)
    count = 2 if other_ref is None else 3
    total = lax.fori_loop(0, full_len // rows, step, (zero,) * count)
    sums_ref[...] = jnp.zeros_like(sums_ref)
    sums_ref[0:1, :] = total[0]
    sums_ref[1:2, :] = total[1] * row(vec_ref, gain)
    sums_ref[2:3, :] = total[1] * (1.0 + row(vec_ref, scale))
    if other_ref is not None:
        sums_ref[3:4, :] = total[2]


def qkv_kernel(x_ref, vec_ref, w_ref, out_ref, left, right):
    @pl.when(pl.program_id(0) == 0)
    def _():
        put_left(left, modulated(x_ref[...], vec_ref, ATTN_GAIN, ATTN_SHIFT, ATTN_SCALE), 1)

    put_right(right, w_ref[...], 0)
    out_ref[...] = dot_nn(left[...], right[...])


def proj_kernel(
    len_ref, att_ref, x_ref, vec_ref, w_ref, proj_ref, middle_ref, sums_ref, left, right
):
    @pl.when(pl.program_id(0) == 0)
    def _():
        put_left(left, att_ref[...], 1)

    put_right(right, w_ref[...], 0)
    proj = dot_nn(left[...], right[...])
    x = x_ref[...]
    branch = row(vec_ref, ATTN_GATE) * proj
    proj_ref[...] = proj
    middle_ref[...] = x + branch
    valid = lax.broadcasted_iota(jnp.int32, x.shape, 0) < len_ref[0]
    sums_ref[...] = jnp.zeros_like(sums_ref)
    sums_ref[0:1, :] = column_sum(jnp.where(valid, x * x, 0.0))
    sums_ref[1:2, :] = column_sum(jnp.where(valid, branch * branch, 0.0))


def up_kernel(middle_ref, vec_ref, up_ref, bias_ref, act_ref, slope_ref, left, right, *, rows):
    @pl.when(pl.program_id(0) == 0)
    def _():
        put_left(left, modulated(middle_ref[...], vec_ref, MLP_GAIN, MLP_SHIFT, MLP_SCALE), 1)

    put_right(right, up_ref[...], 0)
    for block in range(middle_ref.shape[0] // rows):
        at = pl.ds(block * rows, rows)
        pre = dot_nn(left[at, :], right[...]) + bias_ref[...]
        act_ref[at, :], slope_ref[at, :] = gelu_and_slope(pre)


def down_kernel(
    len_ref, act_ref, down_ref, middle_ref, vec_ref, down_out_ref, out_ref, sums_ref, left, right, acc
):
    step = pl.program_id(0)

    @pl.when(step == 0)
    def _():
        acc[...] = jnp.zeros_like(acc)

    put_left(left, act_ref[...], 1)
    put_right(right, down_ref[...], 0)
    acc[...] += dot_nn(left[...], right[...])

    @pl.when(step == pl.num_programs(0) - 1)
    def _():
        down_out = acc[...] + row(vec_ref, DOWN_BIAS)
        branch = row(vec_ref, MLP_GATE) * down_out
        down_out_ref[...] = down_out
        out_ref[...] = middle_ref[...] + branch
        valid = lax.broadcasted_iota(jnp.int32, branch.shape, 0) < len_ref[0]
        sums_ref[...] = jnp.zeros_like(sums_ref)
        sums_ref[0:1, :] = column_sum(jnp.where(valid, branch * branch, 0.0))


def down_grad_kernel(cot_ref, down_out_ref, vec_ref, act_ref, grad_ref, sums_ref, left, right):
    @pl.when(pl.program_id(0) == 0)
    def _():
        cot = cot_ref[...]
        grad = cot * row(vec_ref, MLP_GATE)
        put_left(left, grad.T, 1)
        sums_ref[...] = jnp.zeros_like(sums_ref)
        sums_ref[0:1, :] = column_sum(cot * down_out_ref[...])
        sums_ref[1:2, :] = column_sum(grad)

    put_right(right, act_ref[...], 0)
    grad_ref[...] = dot_nn(left[...], right[...]).T


def mlp_backward_kernel(
    cot_ref,
    middle_ref,
    proj_ref,
    vec_ref,
    down_ref,
    up_ref,
    slope_ref,
    up_grad_ref,
    bias_grad_ref,
    middle_grad_ref,
    sums_ref,
    left,
    turned,
    down_cat,
    up_cat,
    pre_cat,
    pre_stack,
    acc,
    *,
    rows,
):
    step = pl.program_id(0)
    full_len = middle_ref.shape[0]

    @pl.when(step == 0)
    def _():
        put_left(left, cot_ref[...] * row(vec_ref, MLP_GATE), 1)
        normed = modulated(middle_ref[...], vec_ref, MLP_GAIN, MLP_SHIFT, MLP_SCALE)
        put_left(turned, normed.T, 1)
        acc[...] = jnp.zeros_like(acc)

    put_right(down_cat, down_ref[...], 1)
    put_right(up_cat, up_ref[...], 1)
    bias_grad = jnp.zeros_like(bias_grad_ref)
    for block in range(full_len // rows):
        at = pl.ds(block * rows, rows)
        pre_grad = dot_nt(left[at, :], down_cat[...]) * slope_ref[at, :]
        bias_grad += column_sum(pre_grad)
        hi, lo = split_bf16(pre_grad)
        columns = hi.shape[1]
        for place, part in enumerate((hi, lo, hi)):
            pre_cat[at, place * columns : (place + 1) * columns] = part
        for place, part in enumerate((hi, hi, lo)):
            pre_stack[pl.ds(place * full_len + block * rows, rows), :] = part
        acc[at, :] += dot_nt(pre_cat[at, :], up_cat[...])
    bias_grad_ref[...] = bias_grad
    up_grad_ref[...] = dot_nn(turned[...], pre_stack[...])

    @pl.when(step == pl.num_programs(0) - 1)
    def _():
        norm_backward(
            acc, middle_ref, cot_ref, vec_ref, MLP_GAIN, MLP_SCALE, middle_grad_ref, sums_ref, proj_ref
        )


def proj_backward_kernel(
    grad_ref, grad_block_ref, att_ref, vec_ref, vec_block_ref, w_ref, joined_ref, out_ref, w_grad_ref,
    left, turned, w_cat, stack,
):
    del joined_ref

    @pl.when(pl.program_id(0) == 0)
    def _():
        put_left(left, grad_ref[...] * row(vec_ref, ATTN_GATE), 1)
        put_left(turned, att_ref[...].T, 1)

    put_right(w_cat, w_ref[...], 1)
    out_ref[...] = dot_nt(left[...], w_cat[...])
    put_right(stack, grad_block_ref[...] * row(vec_block_ref, ATTN_GATE), 0)
    w_grad_ref[...] = dot_nn(turned[...], stack[...])


def tokens_grad_kernel(
    grad_ref, w_ref, x_ref, extra_ref, vec_ref, out_ref, sums_ref, left, w_cat, acc
):
    step = pl.program_id(0)

    @pl.when(step == 0)
    def _():
        acc[...] = jnp.zeros_like(acc)

    put_left(left, grad_ref[...], 1)
    put_right(w_cat, w_ref[...], 1)
    acc[...] += dot_nt(left[...], w_cat[...])

    @pl.when(step == pl.num_programs(0) - 1)
    def _():
        norm_backward(acc, x_ref, extra_ref, vec_ref, ATTN_GAIN, ATTN_SCALE, out_ref, sums_ref, None)


def qkv_grad_kernel(x_ref, vec_ref, grad_ref, out_ref, turned, stack):
    @pl.when(pl.program_id(0) == 0)
    def _():
        normed = modulated(x_ref[...], vec_ref, ATTN_GAIN, ATTN_SHIFT, ATTN_SCALE)
        put_left(turned, normed.T, 1)

    put_right(stack, grad_ref[...], 0)
    out_ref[...] = dot_nn(turned[...], stack[...])


def whole(shape):
    return pl.BlockSpec(shape, lambda *ids: (0,) * len(shape), pipeline_mode=pl.Buffered(1))


def by_columns(rows, columns, first=0):
    return pl.BlockSpec((rows, columns), lambda j, *refs: (0, first + j))


def by_rows(rows, columns, column=0):
    return pl.BlockSpec((rows, columns), lambda j, *refs: (j, column))


def dense(body, grid, in_specs, out_specs, out_shapes, scratch, products, args, scalars=0, aliases=None):
    moved = sum(a.size for a in args) + sum(o.size for o in out_shapes)
    return pl.pallas_call(
        body,
        out_shape=tuple(out_shapes),
        grid_spec=pltpu.PrefetchScalarGridSpec(
            num_scalar_prefetch=scalars,
            grid=(grid,),
            in_specs=in_specs,
            out_specs=tuple(out_specs),
            scratch_shapes=[pltpu.VMEM(shape, kind) for shape, kind in scratch],
        ),
        input_output_aliases=aliases or {},
        compiler_params=pltpu.CompilerParams(vmem_limit_bytes=60 << 20),
        cost_estimate=pl.CostEstimate(flops=6 * products, bytes_accessed=4 * moved, transcendentals=0),
    )(*args)


def array(*shape):
    return jax.ShapeDtypeStruct(shape, f32)


def mm_qkv(x, vectors, weight):
    t, d = x.shape
    n = 3 * d
    c = COLUMNS
    return dense(
        qkv_kernel,
        n // c,
        [whole((t, d)), whole((VECTORS, d)), by_columns(d, c)],
        [by_columns(t, c)],
        [array(t, n)],
        [((t, 3 * d), bf16), ((3 * d, c), bf16)],
        t * d * n,
        (x, vectors, weight),
    )[0]


def mm_proj(length, attended, x, vectors, weight):
    t, d = x.shape
    c = COLUMNS
    return dense(
        proj_kernel,
        d // c,
        [whole((t, d)), by_columns(t, c), by_columns(VECTORS, c), by_columns(d, c, 3 * d // c)],
        [by_columns(t, c), by_columns(t, c), by_columns(8, c)],
        [array(t, d), array(t, d), array(8, d)],
        [((t, 3 * d), bf16), ((3 * d, c), bf16)],
        t * d * d,
        (length, attended, x, vectors, weight),
        scalars=1,
    )


def mm_up(middle, vectors, up, up_bias):
    t, d = middle.shape
    n = up.shape[1]
    c = COLUMNS
    return dense(
        partial(up_kernel, rows=min(256, t)),
        n // c,
        [whole((t, d)), whole((VECTORS, d)), by_columns(d, c), by_columns(1, c)],
        [by_columns(t, c), by_columns(t, c)],
        [array(t, n), array(t, n)],
        [((t, 3 * d), bf16), ((3 * d, c), bf16)],
        t * d * n,
        (middle, vectors, up, up_bias),
    )


def mm_down(length, act, down, middle, vectors):
    t, n = act.shape
    d = down.shape[1]
    c = 2 * COLUMNS
    return dense(
        down_kernel,
        n // c,
        [by_columns(t, c), by_rows(c, d), whole((t, d)), whole((VECTORS, d))],
        [whole((t, d)), whole((t, d)), whole((8, d))],
        [array(t, d), array(t, d), array(8, d)],
        [((t, 3 * c), bf16), ((3 * c, d), bf16), ((t, d), f32)],
        t * d * n,
        (length, act, down, middle, vectors),
        scalars=1,
    )


def dw_down(cot, down_out, vectors, act):
    t, d = cot.shape
    n = act.shape[1]
    c = COLUMNS
    return dense(
        down_grad_kernel,
        n // c,
        [whole((t, d)), whole((t, d)), whole((VECTORS, d)), by_columns(t, c)],
        [by_rows(c, d), whole((8, d))],
        [array(n, d), array(8, d)],
        [((d, 3 * t), bf16), ((3 * t, c), bf16)],
        t * d * n,
        (cot, down_out, vectors, act),
    )


def mlp_backward(cot, middle, proj_out, vectors, down, up, slope):
    t, d = cot.shape
    n = up.shape[1]
    c = COLUMNS
    return dense(
        partial(mlp_backward_kernel, rows=min(256, t)),
        n // c,
        [
            whole((t, d)),
            whole((t, d)),
            whole((t, d)),
            whole((VECTORS, d)),
            by_rows(c, d),
            by_columns(d, c),
            by_columns(t, c),
        ],
        [by_columns(d, c), by_columns(1, c), whole((t, d)), whole((8, d))],
        [array(d, n + d), array(1, n), array(t, d), array(8, d)],
        [
            ((t, 3 * d), bf16),
            ((d, 3 * t), bf16),
            ((c, 3 * d), bf16),
            ((d, 3 * c), bf16),
            ((t, 3 * c), bf16),
            ((3 * t, c), bf16),
            ((t, d), f32),
        ],
        3 * t * d * n,
        (cot, middle, proj_out, vectors, down, up, slope),
    )


def proj_backward(middle_grad, attended, vectors, weight, joined):
    t, d = middle_grad.shape
    c = COLUMNS
    return dense(
        proj_backward_kernel,
        d // c,
        [
            whole((t, d)),
            by_columns(t, c),
            whole((t, d)),
            whole((VECTORS, d)),
            by_columns(VECTORS, c),
            by_rows(c, d, 3),
            pl.BlockSpec(memory_space=pl.ANY),
        ],
        [by_columns(t, c), by_columns(d, c, joined.shape[1] // c - d // c)],
        [array(t, d), array(*joined.shape)],
        [((t, 3 * d), bf16), ((d, 3 * t), bf16), ((c, 3 * d), bf16), ((3 * t, c), bf16)],
        2 * t * d * d,
        (middle_grad, middle_grad, attended, vectors, vectors, weight, joined),
        aliases={6: 1},
    )


def mm_tokens_grad(qkv_grad, weight, x, middle_grad, vectors):
    t, d = x.shape
    n = 3 * d
    c = COLUMNS
    return dense(
        tokens_grad_kernel,
        n // c,
        [by_columns(t, c), by_columns(d, c), whole((t, d)), whole((t, d)), whole((VECTORS, d))],
        [whole((t, d)), whole((8, d))],
        [array(t, d), array(8, d)],
        [((t, 3 * c), bf16), ((d, 3 * c), bf16), ((t, d), f32)],
        t * d * n,
        (qkv_grad, weight, x, middle_grad, vectors),
    )


def dw_qkv(x, vectors, qkv_grad):
    t, d = x.shape
    n = qkv_grad.shape[1]
    c = COLUMNS
    return dense(
        qkv_grad_kernel,
        n // c,
        [whole((t, d)), whole((VECTORS, d)), by_columns(t, c)],
        [by_columns(d, c)],
        [array(d, n)],
        [((d, 3 * t), bf16), ((3 * t, c), bf16)],
        t * d * n,
        (x, vectors, qkv_grad),
    )[0]


def padded_row(pieces):
    row = jnp.concatenate([piece.reshape(-1) for piece in pieces])
    return jnp.pad(row, (0, -row.shape[0] % 128))[None, :]


def cut(row, sizes):
    out, start = [], 0
    for size in sizes:
        out.append(row[:, start : start + size])
        start += size
    return out


def shards(
    tokens,
    time_embed,
    lengths,
    positions,
    ada_weight,
    ada_bias,
    attn_gain,
    qkv_weight,
    proj_weight,
    mlp_gain,
    up_weight,
    up_bias,
    down_weight,
    down_bias,
    cotangent,
):
    groups = lax.axis_size("seq")
    owners = lax.axis_size("fsdp")
    mine_seq = lax.axis_index("seq")
    mine_fsdp = lax.axis_index("fsdp")
    seqs_here, local_len, width = tokens.shape
    cond = time_embed.shape[1]
    full_len = local_len * groups
    hidden = up_weight.shape[1]
    assert seqs_here == groups

    def to_sequence(field):
        return lax.all_to_all(field, "seq", split_axis=0, concat_axis=1, tiled=True)[0]

    def to_tokens(field):
        pieces = field.reshape(groups, local_len, width)
        return lax.all_to_all(pieces, "seq", split_axis=0, concat_axis=0, tiled=True)

    def gather(shard):
        return lax.all_gather(shard, "fsdp", axis=0, tiled=True)

    def rows_of_all(row, axes):
        count = lax.axis_size(axes)
        sent = jnp.broadcast_to(row[None], (count,) + row.shape)
        return lax.all_to_all(sent, axes, split_axis=0, concat_axis=0, tiled=True)[:, 0]

    def exchanged(rows, axis, count, mine):
        if count > 8:
            all_rows = lax.all_gather(rows, axis, axis=0)
            return lax.dynamic_slice(all_rows, (0, mine, 0), (count, 1, rows.shape[1]))[:, 0]
        out = jnp.zeros_like(rows)
        for shift in range(count):
            target = (mine + shift) % count
            sent = lax.dynamic_slice(rows, (target, 0), (1, rows.shape[1]))
            if shift > 0:
                sent = lax.ppermute(sent, axis, [(i, (i + shift) % count) for i in range(count)])
            out = lax.dynamic_update_slice(out, sent, ((mine - shift) % count, 0))
        return out

    x = to_sequence(tokens)
    places = exchanged(positions, "seq", groups, mine_seq).reshape(full_len)
    length = lax.dynamic_slice(lengths, (mine_seq,), (1,))
    small = [time_embed, ada_bias, attn_gain, mlp_gain, up_bias, down_bias]
    small_sizes = [piece.size for piece in small]
    packed = gather(padded_row(small))
    time_all, ada_bias_full, attn_gain_full, mlp_gain_full, up_bias_full, down_bias_full = cut(
        packed, small_sizes
    )
    time_all = time_all.reshape(owners * seqs_here, cond)
    ada_bias_full, attn_gain_full, mlp_gain_full, up_bias_full, down_bias_full = (
        piece.reshape(1, -1)
        for piece in (ada_bias_full, attn_gain_full, mlp_gain_full, up_bias_full, down_bias_full)
    )
    silu_all = jax.nn.silu(time_all)
    ada_rows = ada_weight.shape[0]
    silu_cols = lax.dynamic_slice(silu_all, (0, mine_fsdp * ada_rows), (owners * seqs_here, ada_rows))
    silu_group = lax.dynamic_slice(
        silu_cols.reshape(owners, seqs_here, ada_rows), (0, mine_seq, 0), (owners, 1, ada_rows)
    )[:, 0]
    partial_rows = jnp.dot(silu_group, ada_weight, precision=highest)
    partial_rows = exchanged(partial_rows, "fsdp", owners, mine_fsdp)
    modulation = jnp.sum(partial_rows, axis=0, keepdims=True) + ada_bias_full
    shift_attn, scale_attn, gate_attn, shift_mlp, scale_mlp, gate_mlp = jnp.split(modulation, 6, axis=1)
    vectors = [
        attn_gain_full,
        shift_attn,
        scale_attn,
        gate_attn,
        mlp_gain_full,
        shift_mlp,
        scale_mlp,
        gate_mlp,
        down_bias_full,
    ]
    vectors = jnp.concatenate(vectors + [jnp.zeros((VECTORS - len(vectors), width), f32)], axis=0)
    attn_full = gather(jnp.concatenate([qkv_weight, proj_weight], axis=1))
    up_full = gather(up_weight)
    down_full = gather(down_weight)
    cosine, sine = rotary_tables(places)

    qkv = mm_qkv(x, vectors, attn_full)
    cot_in, _ = lax.optimization_barrier((cotangent, x))
    cot = to_sequence(cot_in)
    attended, lse = attention_forward(length, qkv, cosine, sine)
    proj_out, middle, attn_sums = mm_proj(length, attended, x, vectors, attn_full)
    hidden_act, gelu_slope = mm_up(middle, vectors, up_full, up_bias_full)
    down_out, block_out, mlp_sums = mm_down(length, hidden_act, down_full, middle, vectors)
    block_out = to_tokens(block_out)

    def scatter(grad):
        return lax.psum_scatter(grad, "fsdp", scatter_dimension=0, tiled=True)

    down_weight_grad, down_sums = dw_down(cot, down_out, vectors, hidden_act)
    down_shard = scatter(down_weight_grad)
    up_weight_grad, up_bias_grad, middle_grad, mlp_norm_sums = mlp_backward(
        cot, middle, proj_out, vectors, down_full, up_full, gelu_slope
    )
    attended_grad, up_proj_grad = proj_backward(middle_grad, attended, vectors, attn_full, up_weight_grad)
    up_shard = scatter(up_proj_grad)
    down_total, up_proj_total = lax.psum((down_shard, up_shard), "seq")
    gate_mlp_grad, down_bias_grad = down_sums[0], down_sums[1]
    shift_mlp_grad, scale_mlp_grad, mlp_gain_grad, gate_attn_grad = (mlp_norm_sums[i] for i in range(4))
    sums = jnp.stack(
        [
            jnp.sum(attn_sums[0]),
            jnp.sum(attn_sums[1]),
            jnp.sum(mlp_sums[0]),
            length[0].astype(f32),
        ]
    )
    early = [
        gate_attn_grad,
        shift_mlp_grad,
        scale_mlp_grad,
        gate_mlp_grad,
        mlp_gain_grad,
        up_bias_grad,
        down_bias_grad,
        sums,
    ]
    early_all = rows_of_all(padded_row(early), ("fsdp", "seq"))
    gate_attn_rows, shift_mlp_rows, scale_mlp_rows, gate_mlp_rows, *early_rest = cut(
        early_all, [piece.size for piece in early]
    )

    qkv_grad = attention_backward(length, qkv, cosine, sine, attended, lse, attended_grad)
    tokens_grad, attn_norm_sums = mm_tokens_grad(qkv_grad, attn_full, x, middle_grad, vectors)
    shift_attn_grad, scale_attn_grad, attn_gain_grad = (attn_norm_sums[i] for i in range(3))
    tokens_grad = to_tokens(tokens_grad)
    qkv_weight_grad, down_total, up_proj_total = lax.optimization_barrier(
        (dw_qkv(x, vectors, qkv_grad), down_total, up_proj_total)
    )
    up_total, proj_total = up_proj_total[:, :hidden], up_proj_total[:, hidden:]
    qkv_shard = scatter(qkv_weight_grad)
    late = [shift_attn_grad, scale_attn_grad, attn_gain_grad]
    late_all = lax.all_gather(padded_row(late), "fsdp", axis=0, tiled=True)
    late_all = lax.all_gather(lax.optimization_barrier(late_all), "seq", axis=0)
    late_all = jnp.swapaxes(late_all, 0, 1).reshape(owners * groups, -1)
    shift_attn_rows, scale_attn_rows, attn_gain_rows = cut(late_all, [piece.size for piece in late])
    modulation_rows = jnp.concatenate(
        [shift_attn_rows, scale_attn_rows, gate_attn_rows, shift_mlp_rows, scale_mlp_rows, gate_mlp_rows],
        axis=1,
    )

    ada_weight_grad = lax.dot_general(
        silu_cols, modulation_rows, (((0,), (0,)), ((), ())), precision=highest
    )
    time_cols = lax.dot_general(modulation_rows, ada_weight, (((1,), (1,)), ((), ())), precision=highest)
    time_cols = lax.all_gather(time_cols, "fsdp", axis=0)
    time_rows = lax.dynamic_slice(
        time_cols, (0, mine_fsdp * seqs_here, 0), (owners, seqs_here, ada_rows)
    )
    time_part = jnp.swapaxes(time_rows, 0, 1).reshape(seqs_here, cond)
    _, silu_back = jax.vjp(jax.nn.silu, time_embed)
    (time_grad,) = silu_back(time_part)

    def owned(rows):
        total = jnp.sum(rows, axis=0)
        size = total.shape[0] // owners
        return lax.dynamic_slice(total, (mine_fsdp * size,), (size,))

    mlp_gain_rows, up_bias_rows, down_bias_rows, sums_rows = early_rest
    totals = jnp.sum(sums_rows, axis=0)
    rms = jnp.sqrt(totals[:3] / (totals[3] * width))
    qkv_total = lax.psum(qkv_shard, "seq")
    return (
        block_out,
        tokens_grad,
        time_grad,
        ada_weight_grad,
        owned(modulation_rows),
        owned(attn_gain_rows),
        qkv_total,
        proj_total,
        owned(mlp_gain_rows),
        up_total,
        owned(up_bias_rows),
        down_total,
        owned(down_bias_rows),
        rms[0],
        rms[1],
        rms[2],
    )


def solution(mesh):
    field = P("fsdp", "seq", None)
    matrix = P("fsdp", None)
    vector = P("fsdp")

    return jax.shard_map(
        shards,
        mesh=mesh,
        in_specs=(
            field,
            matrix,
            vector,
            P("fsdp", "seq"),
            matrix,
            vector,
            vector,
            matrix,
            matrix,
            vector,
            matrix,
            vector,
            matrix,
            vector,
            field,
        ),
        out_specs=(
            field,
            field,
            matrix,
            matrix,
            vector,
            vector,
            matrix,
            matrix,
            vector,
            matrix,
            vector,
            matrix,
            vector,
            P(),
            P(),
            P(),
        ),
        check_vma=False,
    )
```

```python
from functools import partial

import jax
import jax.numpy as jnp
from jax import lax
from jax.experimental import pallas as pl
from jax.experimental.pallas import tpu as pltpu
from jax.sharding import PartitionSpec as P


HD = 64
PAIR = 2 * HD
LOG2E = 1.4426950408889634
LN2 = 0.6931471805599453

epsilon = 1e-05
highest = lax.Precision.HIGHEST
f32 = jnp.float32
bf16 = jnp.bfloat16


def gelu_and_slope(value):
    square = value * value
    t = jnp.tanh(0.7978845608028654 * (value + 0.044715 * value * square))
    slope = 0.5 * (1.0 + t) + 0.5 * value * (1.0 - t * t) * (
        0.7978845608028654 * (1.0 + 3 * 0.044715 * square)
    )
    return 0.5 * value * (1.0 + t), slope


def rotary_tables(positions):
    inverse = 1.0 / 10000.0 ** (jnp.arange(0, HD, 2, dtype=f32) / HD)
    angles = positions.astype(f32)[:, None] * inverse
    cosine, sine = jnp.cos(angles), jnp.sin(angles)
    return jnp.tile(cosine, (1, 4)), jnp.tile(sine, (1, 4))


def rotate(u, cosine, sine, lane):
    first = (lane % HD) < (HD // 2)
    turned = jnp.where(first, -pltpu.roll(u, PAIR - HD // 2, 1), pltpu.roll(u, HD // 2, 1))
    return u * cosine + turned * sine


def rotate_back(g, cosine, sine, lane):
    first = (lane % HD) < (HD // 2)
    w = g * sine
    return g * cosine + jnp.where(first, pltpu.roll(w, PAIR - HD // 2, 1), -pltpu.roll(w, HD // 2, 1))


def parts(u):
    hi = u.astype(bf16).astype(f32)
    return hi, (u - hi).astype(bf16).astype(f32)


def both(u, head, lane):
    turned = pltpu.roll(u, HD, 1)
    return jnp.where((lane < HD) == (head == 0), u, turned)


def beside(left, right, head, lane):
    low = left if head == 0 else pltpu.roll(left, HD, 1)
    high_lanes = pltpu.roll(right, HD, 1) if head == 0 else right
    return jnp.where(lane < HD, low, high_lanes)


def three_terms(column, lane):
    a = column.astype(bf16).astype(f32)
    b = (column - a).astype(bf16).astype(f32)
    c = column - a - b
    return jnp.where(lane == HD, a, jnp.where(lane == HD + 1, b, jnp.where(lane == HD + 2, c, 0.0)))


def split_bf16(u):
    hi = u.astype(bf16)
    return hi, (u - hi.astype(f32)).astype(bf16)


def dot_nt(a, b):
    return lax.dot_general(a, b, (((1,), (1,)), ((), ())), preferred_element_type=f32)


def dot_nn(a, b):
    return lax.dot_general(a, b, (((1,), (0,)), ((), ())), preferred_element_type=f32)


def forward_kernel(
    len_ref, q_ref, k_ref, v_ref, cos_ref, sin_ref, out_ref, lse_ref, qs, ks, vs, acc, *, rows
):
    full_len = q_ref.shape[0]
    lane = lax.broadcasted_iota(jnp.int32, (full_len, PAIR), 1)
    place = lax.broadcasted_iota(jnp.int32, (full_len, PAIR), 0)
    cosine, sine = cos_ref[...], sin_ref[...]
    q = rotate(q_ref[...], cosine, sine, lane) * (HD**-0.5 * LOG2E)
    k = rotate(k_ref[...], cosine, sine, lane)
    q_hi, q_lo = parts(q)
    k_hi, k_lo = parts(k)
    v_hi, v_lo = parts(v_ref[...])
    bias = jnp.where(place < len_ref[0], 0.0, -1e30)
    for head in range(2):
        qs[head, :, :PAIR] = both(q_hi, head, lane).astype(bf16)
        qs[head, :, PAIR:] = jnp.where(
            lane < HD, beside(q_lo, q_lo, head, lane), jnp.where(lane == HD, 1.0, 0.0)
        ).astype(bf16)
        ks[head, :, :PAIR] = beside(k_hi, k_lo, head, lane).astype(bf16)
        ks[head, :, PAIR:] = jnp.where(
            lane < HD, beside(k_hi, k_hi, head, lane), jnp.where(lane == HD, bias, 0.0)
        ).astype(bf16)
        vs[head] = beside(v_hi, v_lo, head, lane).astype(bf16)

    low = lax.broadcasted_iota(jnp.int32, (rows, PAIR), 1) < HD

    def step(block, carry):
        at = pl.ds(pl.multiple_of(block * rows, rows), rows)
        outs, lses = [], []
        for head in range(2):
            scores = dot_nt(qs[head, at, :], ks[head])
            largest = jnp.max(scores, axis=1, keepdims=True)
            expo = jnp.exp2(scores - largest)
            total = jnp.sum(expo, axis=1, keepdims=True)
            hi, lo = split_bf16(expo)
            both_parts = dot_nn(hi, vs[head]) + dot_nn(lo, vs[head])
            outs.append((both_parts + pltpu.roll(both_parts, HD, 1)) / total)
            lses.append(largest + jnp.log2(total))
        out_ref[at, :] = jnp.where(low, outs[0], outs[1])
        lse_ref[at, :] = jnp.where(low, lses[0], lses[1])
        return carry

    lax.fori_loop(0, full_len // rows, step, 0)


def backward_kernel(
    len_ref,
    q_ref,
    k_ref,
    v_ref,
    cos_ref,
    sin_ref,
    out_in_ref,
    lse_ref,
    do_ref,
    grad_ref,
    qs,
    ks,
    vs,
    dos,
    kd,
    qt,
    dot_t,
    dq,
    dkt,
    dvt,
    *,
    rows,
):
    full_len = q_ref.shape[0]
    which = pl.program_id(1)
    lane = lax.broadcasted_iota(jnp.int32, (full_len, PAIR), 1)

    @pl.when(which == 0)
    def _():
        place = lax.broadcasted_iota(jnp.int32, (full_len, PAIR), 0)
        cosine, sine = cos_ref[...], sin_ref[...]
        q = rotate(q_ref[...], cosine, sine, lane) * (HD**-0.5 * LOG2E)
        k = rotate(k_ref[...], cosine, sine, lane)
        out_grad = do_ref[...]
        q_hi, q_lo = parts(q)
        k_hi, k_lo = parts(k)
        v_hi, v_lo = parts(v_ref[...])
        g_hi, g_lo = parts(out_grad)
        product = out_grad * out_in_ref[...]
        lse = lse_ref[...]
        bias = jnp.where(place < len_ref[0], 0.0, -1e30)
        ones = jnp.where((lane >= HD) & (lane < HD + 3), 1.0, 0.0)
        for head in range(2):
            mine = (lane < HD) == (head == 0)
            delta = jnp.sum(jnp.where(mine, product, 0.0), axis=1, keepdims=True)
            lse_head = jnp.max(jnp.where(mine, lse, -3e38), axis=1, keepdims=True)
            qs[head, :, :PAIR] = both(q_hi, head, lane).astype(bf16)
            qs[head, :, PAIR:] = jnp.where(
                lane < HD,
                beside(q_lo, q_lo, head, lane),
                three_terms(-lse_head, lane) + jnp.where(lane == HD + 3, 1.0, 0.0),
            ).astype(bf16)
            ks[head, :, :PAIR] = beside(k_hi, k_lo, head, lane).astype(bf16)
            ks[head, :, PAIR:] = jnp.where(
                lane < HD, beside(k_hi, k_hi, head, lane), ones + jnp.where(lane == HD + 3, bias, 0.0)
            ).astype(bf16)
            dos[head, :, :PAIR] = both(g_hi, head, lane).astype(bf16)
            dos[head, :, PAIR:] = jnp.where(
                lane < HD, beside(g_lo, g_lo, head, lane), three_terms(-delta, lane)
            ).astype(bf16)
            vs[head, :, :PAIR] = beside(v_hi, v_lo, head, lane).astype(bf16)
            vs[head, :, PAIR:] = jnp.where(lane < HD, beside(v_hi, v_hi, head, lane), ones).astype(bf16)
            kd[head] = beside(k_hi, k_lo, head, lane).astype(bf16)
            qt[head] = beside(q_hi, q_lo, head, lane).T.astype(bf16)
            dot_t[head] = beside(g_hi, g_lo, head, lane).T.astype(bf16)
        dkt[...] = jnp.zeros_like(dkt)
        dvt[...] = jnp.zeros_like(dvt)
        low = lax.broadcasted_iota(jnp.int32, (rows, PAIR), 1) < HD

        def step(block, carry):
            at = pl.ds(pl.multiple_of(block * rows, rows), rows)
            outs = []
            for head in range(2):
                weights = jnp.exp2(dot_nt(qs[head, at, :], ks[head]))
                score_grad = weights * dot_nt(dos[head, at, :], vs[head])
                w_hi, w_lo = split_bf16(weights)
                s_hi, s_lo = split_bf16(score_grad)
                both_parts = dot_nn(s_hi, kd[head]) + dot_nn(s_lo, kd[head])
                outs.append(both_parts + pltpu.roll(both_parts, HD, 1))
                q_t = qt[head, :, at]
                g_t = dot_t[head, :, at]
                dkt[head] += dot_nn(q_t, s_hi) + dot_nn(q_t, s_lo)
                dvt[head] += dot_nn(g_t, w_hi) + dot_nn(g_t, w_lo)
            dq[at, :] = jnp.where(low, outs[0], outs[1])
            return carry

        lax.fori_loop(0, full_len // rows, step, 0)
        grad_ref[...] = rotate_back(dq[...] * HD**-0.5, cosine, sine, lane)

    @pl.when(which == 1)
    def _():
        stacked = jnp.concatenate([dkt[h, :HD, :] + dkt[h, HD:, :] for h in range(2)], axis=0)
        grad_ref[...] = rotate_back(stacked.T * LN2, cos_ref[...], sin_ref[...], lane)

    @pl.when(which == 2)
    def _():
        stacked = jnp.concatenate([dvt[h, :HD, :] + dvt[h, HD:, :] for h in range(2)], axis=0)
        grad_ref[...] = stacked.T


def attention_forward(length, qkv, cosine, sine):
    full_len, three = qkv.shape
    width = three // 3
    pairs = width // PAIR
    rows = min(256, full_len)

    def column(offset):
        return pl.BlockSpec((full_len, PAIR), lambda p, ln: (0, p + offset))

    table = pl.BlockSpec((full_len, PAIR), lambda p, ln: (0, 0))
    wide = jax.ShapeDtypeStruct((full_len, width), f32)
    return pl.pallas_call(
        partial(forward_kernel, rows=rows),
        name="attention_forward",
        out_shape=(wide, wide),
        grid_spec=pltpu.PrefetchScalarGridSpec(
            num_scalar_prefetch=1,
            grid=(pairs,),
            in_specs=[column(0), column(pairs), column(2 * pairs), table, table],
            out_specs=(column(0), column(0)),
            scratch_shapes=[
                pltpu.VMEM((2, full_len, 2 * PAIR), bf16),
                pltpu.VMEM((2, full_len, 2 * PAIR), bf16),
                pltpu.VMEM((2, full_len, PAIR), bf16),
                pltpu.VMEM((8, 128), f32),
            ],
        ),
        cost_estimate=pl.CostEstimate(
            flops=24 * full_len * full_len * width, bytes_accessed=20 * full_len * width, transcendentals=0
        ),
    )(length, qkv, qkv, qkv, cosine, sine)


def attention_backward(length, qkv, cosine, sine, attended, lse, out_grad):
    full_len, three = qkv.shape
    width = three // 3
    pairs = width // PAIR
    rows = min(256, full_len)

    def column(offset):
        return pl.BlockSpec((full_len, PAIR), lambda p, c, ln: (0, p + offset))

    table = pl.BlockSpec((full_len, PAIR), lambda p, c, ln: (0, 0))
    stacked = pltpu.VMEM((2, full_len, 2 * PAIR), bf16)
    turned = pltpu.VMEM((2, PAIR, full_len), bf16)
    summed = pltpu.VMEM((2, PAIR, full_len), f32)
    return pl.pallas_call(
        partial(backward_kernel, rows=rows),
        name="attention_backward",
        out_shape=jax.ShapeDtypeStruct((full_len, three), f32),
        grid_spec=pltpu.PrefetchScalarGridSpec(
            num_scalar_prefetch=1,
            grid=(pairs, 3),
            in_specs=[
                column(0),
                column(pairs),
                column(2 * pairs),
                table,
                table,
                column(0),
                column(0),
                column(0),
            ],
            out_specs=pl.BlockSpec((full_len, PAIR), lambda p, c, ln: (0, c * pairs + p)),
            scratch_shapes=[
                stacked,
                stacked,
                stacked,
                stacked,
                pltpu.VMEM((2, full_len, PAIR), bf16),
                turned,
                turned,
                pltpu.VMEM((full_len, PAIR), f32),
                summed,
                summed,
            ],
        ),
        cost_estimate=pl.CostEstimate(
            flops=60 * full_len * full_len * width, bytes_accessed=32 * full_len * width, transcendentals=0
        ),
    )(length, qkv, qkv, qkv, cosine, sine, attended, lse, out_grad)


ATTN_GAIN, ATTN_SHIFT, ATTN_SCALE, ATTN_GATE, MLP_GAIN, MLP_SHIFT, MLP_SCALE, MLP_GATE, DOWN_BIAS = range(9)
VECTORS = 16
COLUMNS = 256


def put_left(ref, u, axis):
    hi, lo = split_bf16(u)
    size = u.shape[axis]
    for place, part in enumerate((hi, lo, hi)):
        if axis == 1:
            ref[:, place * size : (place + 1) * size] = part
        else:
            ref[place * size : (place + 1) * size, :] = part


def put_right(ref, u, axis):
    hi, lo = split_bf16(u)
    size = u.shape[axis]
    for place, part in enumerate((hi, hi, lo)):
        if axis == 1:
            ref[:, place * size : (place + 1) * size] = part
        else:
            ref[place * size : (place + 1) * size, :] = part


def normalized(v):
    average = jnp.mean(v, axis=-1, keepdims=True)
    centered = v - average
    rstd = lax.rsqrt(jnp.mean(centered * centered, axis=-1, keepdims=True) + epsilon)
    return centered * rstd, rstd


def modulated(v, vec_ref, gain, shift, scale):
    xhat, _ = normalized(v)
    return xhat * row(vec_ref, gain) * (1.0 + row(vec_ref, scale)) + row(vec_ref, shift)


def row(ref, index):
    return ref[index : index + 1, :]


def column_sum(u):
    return jnp.sum(u, axis=0, keepdims=True)


def norm_backward(e_ref, v_ref, extra_ref, vec_ref, gain, scale, out_ref, sums_ref, other_ref):
    full_len = v_ref.shape[0]
    rows = min(128, full_len)
    factor = (1.0 + row(vec_ref, scale)) * row(vec_ref, gain)

    def step(block, carry):
        at = pl.ds(pl.multiple_of(block * rows, rows), rows)
        e = e_ref[at, :]
        xhat, rstd = normalized(v_ref[at, :])
        f = e * factor
        grad = rstd * (
            f
            - jnp.mean(f, axis=-1, keepdims=True)
            - xhat * jnp.mean(f * xhat, axis=-1, keepdims=True)
        )
        out = extra_ref[at, :] + grad
        out_ref[at, :] = out
        new = [column_sum(e), column_sum(e * xhat)]
        if other_ref is not None:
            new.append(column_sum(out * other_ref[at, :]))
        return tuple(c + n for c, n in zip(carry, new))

    zero = jnp.zeros((1, v_ref.shape[1]), f32)
    count = 2 if other_ref is None else 3
    total = lax.fori_loop(0, full_len // rows, step, (zero,) * count)
    sums_ref[...] = jnp.zeros_like(sums_ref)
    sums_ref[0:1, :] = total[0]
    sums_ref[1:2, :] = total[1] * row(vec_ref, gain)
    sums_ref[2:3, :] = total[1] * (1.0 + row(vec_ref, scale))
    if other_ref is not None:
        sums_ref[3:4, :] = total[2]


def qkv_kernel(x_ref, vec_ref, w_ref, out_ref, left, right):
    @pl.when(pl.program_id(0) == 0)
    def _():
        put_left(left, modulated(x_ref[...], vec_ref, ATTN_GAIN, ATTN_SHIFT, ATTN_SCALE), 1)

    put_right(right, w_ref[...], 0)
    out_ref[...] = dot_nn(left[...], right[...])


def proj_kernel(
    len_ref, att_ref, x_ref, vec_ref, w_ref, proj_ref, middle_ref, sums_ref, left, right
):
    @pl.when(pl.program_id(0) == 0)
    def _():
        put_left(left, att_ref[...], 1)

    put_right(right, w_ref[...], 0)
    proj = dot_nn(left[...], right[...])
    x = x_ref[...]
    branch = row(vec_ref, ATTN_GATE) * proj
    proj_ref[...] = proj
    middle_ref[...] = x + branch
    valid = lax.broadcasted_iota(jnp.int32, x.shape, 0) < len_ref[0]
    sums_ref[...] = jnp.zeros_like(sums_ref)
    sums_ref[0:1, :] = column_sum(jnp.where(valid, x * x, 0.0))
    sums_ref[1:2, :] = column_sum(jnp.where(valid, branch * branch, 0.0))


def up_kernel(middle_ref, vec_ref, up_ref, bias_ref, act_ref, slope_ref, left, right, *, rows):
    @pl.when(pl.program_id(0) == 0)
    def _():
        put_left(left, modulated(middle_ref[...], vec_ref, MLP_GAIN, MLP_SHIFT, MLP_SCALE), 1)

    put_right(right, up_ref[...], 0)
    for block in range(middle_ref.shape[0] // rows):
        at = pl.ds(block * rows, rows)
        pre = dot_nn(left[at, :], right[...]) + bias_ref[...]
        act_ref[at, :], slope_ref[at, :] = gelu_and_slope(pre)


def down_kernel(
    len_ref, act_ref, down_ref, middle_ref, cot_ref, vec_ref, out_ref, sums_ref, left, right, acc
):
    step = pl.program_id(0)

    @pl.when(step == 0)
    def _():
        acc[...] = jnp.zeros_like(acc)

    put_left(left, act_ref[...], 1)
    put_right(right, down_ref[...], 0)
    acc[...] += dot_nn(left[...], right[...])

    @pl.when(step == pl.num_programs(0) - 1)
    def _():
        down_out = acc[...] + row(vec_ref, DOWN_BIAS)
        branch = row(vec_ref, MLP_GATE) * down_out
        out_ref[...] = middle_ref[...] + branch
        valid = lax.broadcasted_iota(jnp.int32, branch.shape, 0) < len_ref[0]
        sums_ref[...] = jnp.zeros_like(sums_ref)
        sums_ref[0:1, :] = column_sum(jnp.where(valid, branch * branch, 0.0))
        sums_ref[1:2, :] = column_sum(cot_ref[...] * down_out)


def down_grad_kernel(cot_ref, vec_ref, act_ref, grad_ref, sums_ref, left, right):
    @pl.when(pl.program_id(0) == 0)
    def _():
        grad = cot_ref[...] * row(vec_ref, MLP_GATE)
        put_left(left, grad.T, 1)
        sums_ref[...] = jnp.zeros_like(sums_ref)
        sums_ref[0:1, :] = column_sum(grad)

    put_right(right, act_ref[...], 0)
    grad_ref[...] = dot_nn(left[...], right[...]).T


def mlp_backward_kernel(
    cot_ref,
    middle_ref,
    proj_ref,
    vec_ref,
    down_ref,
    up_ref,
    slope_ref,
    up_grad_ref,
    bias_grad_ref,
    middle_grad_ref,
    sums_ref,
    left,
    turned,
    down_cat,
    up_cat,
    pre_cat,
    pre_stack,
    acc,
    *,
    rows,
):
    step = pl.program_id(0)
    full_len = middle_ref.shape[0]

    @pl.when(step == 0)
    def _():
        put_left(left, cot_ref[...] * row(vec_ref, MLP_GATE), 1)
        normed = modulated(middle_ref[...], vec_ref, MLP_GAIN, MLP_SHIFT, MLP_SCALE)
        put_left(turned, normed.T, 1)
        acc[...] = jnp.zeros_like(acc)

    put_right(down_cat, down_ref[...], 1)
    put_right(up_cat, up_ref[...], 1)
    bias_grad = jnp.zeros_like(bias_grad_ref)
    for block in range(full_len // rows):
        at = pl.ds(block * rows, rows)
        pre_grad = dot_nt(left[at, :], down_cat[...]) * slope_ref[at, :]
        bias_grad += column_sum(pre_grad)
        hi, lo = split_bf16(pre_grad)
        columns = hi.shape[1]
        for place, part in enumerate((hi, lo, hi)):
            pre_cat[at, place * columns : (place + 1) * columns] = part
        for place, part in enumerate((hi, hi, lo)):
            pre_stack[pl.ds(place * full_len + block * rows, rows), :] = part
        acc[at, :] += dot_nt(pre_cat[at, :], up_cat[...])
    bias_grad_ref[...] = bias_grad
    up_grad_ref[...] = dot_nn(turned[...], pre_stack[...])

    @pl.when(step == pl.num_programs(0) - 1)
    def _():
        norm_backward(
            acc, middle_ref, cot_ref, vec_ref, MLP_GAIN, MLP_SCALE, middle_grad_ref, sums_ref, proj_ref
        )


def proj_backward_kernel(
    grad_ref, grad_block_ref, att_ref, vec_ref, vec_block_ref, w_ref, joined_ref, out_ref, w_grad_ref,
    left, turned, w_cat, stack,
):
    del joined_ref

    @pl.when(pl.program_id(0) == 0)
    def _():
        put_left(left, grad_ref[...] * row(vec_ref, ATTN_GATE), 1)
        put_left(turned, att_ref[...].T, 1)

    put_right(w_cat, w_ref[...], 1)
    out_ref[...] = dot_nt(left[...], w_cat[...])
    put_right(stack, grad_block_ref[...] * row(vec_block_ref, ATTN_GATE), 0)
    w_grad_ref[...] = dot_nn(turned[...], stack[...])


def tokens_grad_kernel(
    grad_ref, w_ref, x_ref, extra_ref, vec_ref, out_ref, sums_ref, left, w_cat, acc
):
    step = pl.program_id(0)

    @pl.when(step == 0)
    def _():
        acc[...] = jnp.zeros_like(acc)

    put_left(left, grad_ref[...], 1)
    put_right(w_cat, w_ref[...], 1)
    acc[...] += dot_nt(left[...], w_cat[...])

    @pl.when(step == pl.num_programs(0) - 1)
    def _():
        norm_backward(acc, x_ref, extra_ref, vec_ref, ATTN_GAIN, ATTN_SCALE, out_ref, sums_ref, None)


def qkv_grad_kernel(x_ref, vec_ref, grad_ref, out_ref, turned, stack):
    @pl.when(pl.program_id(0) == 0)
    def _():
        normed = modulated(x_ref[...], vec_ref, ATTN_GAIN, ATTN_SHIFT, ATTN_SCALE)
        put_left(turned, normed.T, 1)

    put_right(stack, grad_ref[...], 0)
    out_ref[...] = dot_nn(turned[...], stack[...])


def whole(shape):
    return pl.BlockSpec(shape, lambda *ids: (0,) * len(shape), pipeline_mode=pl.Buffered(1))


def by_columns(rows, columns, first=0):
    return pl.BlockSpec((rows, columns), lambda j, *refs: (0, first + j))


def by_rows(rows, columns, column=0):
    return pl.BlockSpec((rows, columns), lambda j, *refs: (j, column))


def dense(body, grid, in_specs, out_specs, out_shapes, scratch, products, args, scalars=0, aliases=None):
    moved = sum(a.size for a in args) + sum(o.size for o in out_shapes)
    return pl.pallas_call(
        body,
        out_shape=tuple(out_shapes),
        grid_spec=pltpu.PrefetchScalarGridSpec(
            num_scalar_prefetch=scalars,
            grid=(grid,),
            in_specs=in_specs,
            out_specs=tuple(out_specs),
            scratch_shapes=[pltpu.VMEM(shape, kind) for shape, kind in scratch],
        ),
        input_output_aliases=aliases or {},
        compiler_params=pltpu.CompilerParams(vmem_limit_bytes=60 << 20),
        cost_estimate=pl.CostEstimate(flops=6 * products, bytes_accessed=4 * moved, transcendentals=0),
    )(*args)


def array(*shape):
    return jax.ShapeDtypeStruct(shape, f32)


def mm_qkv(x, vectors, weight):
    t, d = x.shape
    n = 3 * d
    c = COLUMNS
    return dense(
        qkv_kernel,
        n // c,
        [whole((t, d)), whole((VECTORS, d)), by_columns(d, c)],
        [by_columns(t, c)],
        [array(t, n)],
        [((t, 3 * d), bf16), ((3 * d, c), bf16)],
        t * d * n,
        (x, vectors, weight),
    )[0]


def mm_proj(length, attended, x, vectors, weight):
    t, d = x.shape
    c = COLUMNS
    return dense(
        proj_kernel,
        d // c,
        [whole((t, d)), by_columns(t, c), by_columns(VECTORS, c), by_columns(d, c, 3 * d // c)],
        [by_columns(t, c), by_columns(t, c), by_columns(8, c)],
        [array(t, d), array(t, d), array(8, d)],
        [((t, 3 * d), bf16), ((3 * d, c), bf16)],
        t * d * d,
        (length, attended, x, vectors, weight),
        scalars=1,
    )


def mm_up(middle, vectors, up, up_bias):
    t, d = middle.shape
    n = up.shape[1]
    c = COLUMNS
    return dense(
        partial(up_kernel, rows=min(256, t)),
        n // c,
        [whole((t, d)), whole((VECTORS, d)), by_columns(d, c), by_columns(1, c)],
        [by_columns(t, c), by_columns(t, c)],
        [array(t, n), array(t, n)],
        [((t, 3 * d), bf16), ((3 * d, c), bf16)],
        t * d * n,
        (middle, vectors, up, up_bias),
    )


def mm_down(length, act, down, middle, cot, vectors):
    t, n = act.shape
    d = down.shape[1]
    c = 2 * COLUMNS
    return dense(
        down_kernel,
        n // c,
        [by_columns(t, c), by_rows(c, d), whole((t, d)), whole((t, d)), whole((VECTORS, d))],
        [whole((t, d)), whole((8, d))],
        [array(t, d), array(8, d)],
        [((t, 3 * c), bf16), ((3 * c, d), bf16), ((t, d), f32)],
        t * d * n,
        (length, act, down, middle, cot, vectors),
        scalars=1,
    )


def dw_down(cot, vectors, act):
    t, d = cot.shape
    n = act.shape[1]
    c = COLUMNS
    return dense(
        down_grad_kernel,
        n // c,
        [whole((t, d)), whole((VECTORS, d)), by_columns(t, c)],
        [by_rows(c, d), whole((8, d))],
        [array(n, d), array(8, d)],
        [((d, 3 * t), bf16), ((3 * t, c), bf16)],
        t * d * n,
        (cot, vectors, act),
    )


def mlp_backward(cot, middle, proj_out, vectors, down, up, slope):
    t, d = cot.shape
    n = up.shape[1]
    c = COLUMNS
    return dense(
        partial(mlp_backward_kernel, rows=min(256, t)),
        n // c,
        [
            whole((t, d)),
            whole((t, d)),
            whole((t, d)),
            whole((VECTORS, d)),
            by_rows(c, d),
            by_columns(d, c),
            by_columns(t, c),
        ],
        [by_columns(d, c), by_columns(1, c), whole((t, d)), whole((8, d))],
        [array(d, n + d), array(1, n), array(t, d), array(8, d)],
        [
            ((t, 3 * d), bf16),
            ((d, 3 * t), bf16),
            ((c, 3 * d), bf16),
            ((d, 3 * c), bf16),
            ((t, 3 * c), bf16),
            ((3 * t, c), bf16),
            ((t, d), f32),
        ],
        3 * t * d * n,
        (cot, middle, proj_out, vectors, down, up, slope),
    )


def proj_backward(middle_grad, attended, vectors, weight, joined):
    t, d = middle_grad.shape
    c = COLUMNS
    return dense(
        proj_backward_kernel,
        d // c,
        [
            whole((t, d)),
            by_columns(t, c),
            whole((t, d)),
            whole((VECTORS, d)),
            by_columns(VECTORS, c),
            by_rows(c, d, 3),
            pl.BlockSpec(memory_space=pl.ANY),
        ],
        [by_columns(t, c), by_columns(d, c, joined.shape[1] // c - d // c)],
        [array(t, d), array(*joined.shape)],
        [((t, 3 * d), bf16), ((d, 3 * t), bf16), ((c, 3 * d), bf16), ((3 * t, c), bf16)],
        2 * t * d * d,
        (middle_grad, middle_grad, attended, vectors, vectors, weight, joined),
        aliases={6: 1},
    )


def mm_tokens_grad(qkv_grad, weight, x, middle_grad, vectors):
    t, d = x.shape
    n = 3 * d
    c = COLUMNS
    return dense(
        tokens_grad_kernel,
        n // c,
        [by_columns(t, c), by_columns(d, c), whole((t, d)), whole((t, d)), whole((VECTORS, d))],
        [whole((t, d)), whole((8, d))],
        [array(t, d), array(8, d)],
        [((t, 3 * c), bf16), ((d, 3 * c), bf16), ((t, d), f32)],
        t * d * n,
        (qkv_grad, weight, x, middle_grad, vectors),
    )


def dw_qkv(x, vectors, qkv_grad):
    t, d = x.shape
    n = qkv_grad.shape[1]
    c = COLUMNS
    return dense(
        qkv_grad_kernel,
        n // c,
        [whole((t, d)), whole((VECTORS, d)), by_columns(t, c)],
        [by_columns(d, c)],
        [array(d, n)],
        [((d, 3 * t), bf16), ((3 * t, c), bf16)],
        t * d * n,
        (x, vectors, qkv_grad),
    )[0]


def padded_row(pieces):
    row = jnp.concatenate([piece.reshape(-1) for piece in pieces])
    return jnp.pad(row, (0, -row.shape[0] % 128))[None, :]


def cut(row, sizes):
    out, start = [], 0
    for size in sizes:
        out.append(row[:, start : start + size])
        start += size
    return out


def shards(
    tokens,
    time_embed,
    lengths,
    positions,
    ada_weight,
    ada_bias,
    attn_gain,
    qkv_weight,
    proj_weight,
    mlp_gain,
    up_weight,
    up_bias,
    down_weight,
    down_bias,
    cotangent,
):
    groups = lax.axis_size("seq")
    owners = lax.axis_size("fsdp")
    mine_seq = lax.axis_index("seq")
    mine_fsdp = lax.axis_index("fsdp")
    seqs_here, local_len, width = tokens.shape
    cond = time_embed.shape[1]
    full_len = local_len * groups
    hidden = up_weight.shape[1]
    assert seqs_here == groups

    def to_sequence(field):
        return lax.all_to_all(field, "seq", split_axis=0, concat_axis=1, tiled=True)[0]

    def to_tokens(field):
        pieces = field.reshape(groups, local_len, width)
        return lax.all_to_all(pieces, "seq", split_axis=0, concat_axis=0, tiled=True)

    def gather(shard):
        return lax.all_gather(shard, "fsdp", axis=0, tiled=True)

    def rows_of_all(row, axes):
        count = lax.axis_size(axes)
        sent = jnp.broadcast_to(row[None], (count,) + row.shape)
        return lax.all_to_all(sent, axes, split_axis=0, concat_axis=0, tiled=True)[:, 0]

    def exchanged(rows, axis, count, mine):
        if count > 8:
            all_rows = lax.all_gather(rows, axis, axis=0)
            return lax.dynamic_slice(all_rows, (0, mine, 0), (count, 1, rows.shape[1]))[:, 0]
        out = jnp.zeros_like(rows)
        for shift in range(count):
            target = (mine + shift) % count
            sent = lax.dynamic_slice(rows, (target, 0), (1, rows.shape[1]))
            if shift > 0:
                sent = lax.ppermute(sent, axis, [(i, (i + shift) % count) for i in range(count)])
            out = lax.dynamic_update_slice(out, sent, ((mine - shift) % count, 0))
        return out

    x = to_sequence(tokens)
    places = exchanged(positions, "seq", groups, mine_seq).reshape(full_len)
    length = lax.dynamic_slice(lengths, (mine_seq,), (1,))
    small = [time_embed, ada_bias, attn_gain, mlp_gain, up_bias, down_bias]
    small_sizes = [piece.size for piece in small]
    packed = gather(padded_row(small))
    time_all, ada_bias_full, attn_gain_full, mlp_gain_full, up_bias_full, down_bias_full = cut(
        packed, small_sizes
    )
    time_all = time_all.reshape(owners * seqs_here, cond)
    ada_bias_full, attn_gain_full, mlp_gain_full, up_bias_full, down_bias_full = (
        piece.reshape(1, -1)
        for piece in (ada_bias_full, attn_gain_full, mlp_gain_full, up_bias_full, down_bias_full)
    )
    silu_all = jax.nn.silu(time_all)
    ada_rows = ada_weight.shape[0]
    silu_cols = lax.dynamic_slice(silu_all, (0, mine_fsdp * ada_rows), (owners * seqs_here, ada_rows))
    silu_group = lax.dynamic_slice(
        silu_cols.reshape(owners, seqs_here, ada_rows), (0, mine_seq, 0), (owners, 1, ada_rows)
    )[:, 0]
    partial_rows = jnp.dot(silu_group, ada_weight, precision=highest)
    partial_rows = exchanged(partial_rows, "fsdp", owners, mine_fsdp)
    modulation = jnp.sum(partial_rows, axis=0, keepdims=True) + ada_bias_full
    shift_attn, scale_attn, gate_attn, shift_mlp, scale_mlp, gate_mlp = jnp.split(modulation, 6, axis=1)
    vectors = [
        attn_gain_full,
        shift_attn,
        scale_attn,
        gate_attn,
        mlp_gain_full,
        shift_mlp,
        scale_mlp,
        gate_mlp,
        down_bias_full,
    ]
    vectors = jnp.concatenate(vectors + [jnp.zeros((VECTORS - len(vectors), width), f32)], axis=0)
    attn_full = gather(jnp.concatenate([qkv_weight, proj_weight], axis=1))
    up_full = gather(up_weight)
    down_full = gather(down_weight)
    cosine, sine = rotary_tables(places)

    qkv = mm_qkv(x, vectors, attn_full)
    cot_in, _ = lax.optimization_barrier((cotangent, x))
    cot = to_sequence(cot_in)
    attended, lse = attention_forward(length, qkv, cosine, sine)
    proj_out, middle, attn_sums = mm_proj(length, attended, x, vectors, attn_full)
    hidden_act, gelu_slope = mm_up(middle, vectors, up_full, up_bias_full)
    down_weight_grad, down_sums = dw_down(cot, vectors, hidden_act)
    block_out, mlp_sums = mm_down(length, hidden_act, down_full, middle, cot, vectors)
    block_out = to_tokens(block_out)

    def scatter(grad):
        return lax.psum_scatter(grad, "fsdp", scatter_dimension=0, tiled=True)

    down_shard = scatter(down_weight_grad)
    up_weight_grad, up_bias_grad, middle_grad, mlp_norm_sums = mlp_backward(
        cot, middle, proj_out, vectors, down_full, up_full, gelu_slope
    )
    attended_grad, up_proj_grad = proj_backward(middle_grad, attended, vectors, attn_full, up_weight_grad)
    up_shard = scatter(up_proj_grad)
    down_total = lax.psum(down_shard, "seq")
    gate_mlp_grad, down_bias_grad = mlp_sums[1], down_sums[0]
    shift_mlp_grad, scale_mlp_grad, mlp_gain_grad, gate_attn_grad = (mlp_norm_sums[i] for i in range(4))
    sums = jnp.stack(
        [
            jnp.sum(attn_sums[0]),
            jnp.sum(attn_sums[1]),
            jnp.sum(mlp_sums[0]),
            length[0].astype(f32),
        ]
    )
    early = [
        gate_attn_grad,
        shift_mlp_grad,
        scale_mlp_grad,
        gate_mlp_grad,
        mlp_gain_grad,
        up_bias_grad,
        down_bias_grad,
        sums,
    ]
    early_all = rows_of_all(padded_row(early), ("fsdp", "seq"))
    gate_attn_rows, shift_mlp_rows, scale_mlp_rows, gate_mlp_rows, *early_rest = cut(
        early_all, [piece.size for piece in early]
    )

    qkv_grad = attention_backward(length, qkv, cosine, sine, attended, lse, attended_grad)
    tokens_grad, attn_norm_sums = mm_tokens_grad(qkv_grad, attn_full, x, middle_grad, vectors)
    shift_attn_grad, scale_attn_grad, attn_gain_grad = (attn_norm_sums[i] for i in range(3))
    tokens_grad = to_tokens(tokens_grad)
    qkv_weight_grad, down_total = lax.optimization_barrier((dw_qkv(x, vectors, qkv_grad), down_total))
    qkv_shard = scatter(qkv_weight_grad)
    late = [shift_attn_grad, scale_attn_grad, attn_gain_grad]
    late_all = lax.all_gather(padded_row(late), "fsdp", axis=0, tiled=True)
    late_all = lax.all_gather(lax.optimization_barrier(late_all), "seq", axis=0)
    late_all = jnp.swapaxes(late_all, 0, 1).reshape(owners * groups, -1)
    shift_attn_rows, scale_attn_rows, attn_gain_rows = cut(late_all, [piece.size for piece in late])
    modulation_rows = jnp.concatenate(
        [shift_attn_rows, scale_attn_rows, gate_attn_rows, shift_mlp_rows, scale_mlp_rows, gate_mlp_rows],
        axis=1,
    )

    ada_weight_grad = lax.dot_general(
        silu_cols, modulation_rows, (((0,), (0,)), ((), ())), precision=highest
    )
    time_cols = lax.dot_general(modulation_rows, ada_weight, (((1,), (1,)), ((), ())), precision=highest)
    time_cols = lax.all_gather(time_cols, "fsdp", axis=0)
    time_rows = lax.dynamic_slice(
        time_cols, (0, mine_fsdp * seqs_here, 0), (owners, seqs_here, ada_rows)
    )
    time_part = jnp.swapaxes(time_rows, 0, 1).reshape(seqs_here, cond)
    _, silu_back = jax.vjp(jax.nn.silu, time_embed)
    (time_grad,) = silu_back(time_part)

    def owned(rows):
        total = jnp.sum(rows, axis=0)
        size = total.shape[0] // owners
        return lax.dynamic_slice(total, (mine_fsdp * size,), (size,))

    mlp_gain_rows, up_bias_rows, down_bias_rows, sums_rows = early_rest
    totals = jnp.sum(sums_rows, axis=0)
    rms = jnp.sqrt(totals[:3] / (totals[3] * width))
    up_proj_total, qkv_total = lax.psum((up_shard, qkv_shard), "seq")
    up_total, proj_total = up_proj_total[:, :hidden], up_proj_total[:, hidden:]
    return (
        block_out,
        tokens_grad,
        time_grad,
        ada_weight_grad,
        owned(modulation_rows),
        owned(attn_gain_rows),
        qkv_total,
        proj_total,
        owned(mlp_gain_rows),
        up_total,
        owned(up_bias_rows),
        down_total,
        owned(down_bias_rows),
        rms[0],
        rms[1],
        rms[2],
    )


def solution(mesh):
    field = P("fsdp", "seq", None)
    matrix = P("fsdp", None)
    vector = P("fsdp")

    return jax.shard_map(
        shards,
        mesh=mesh,
        in_specs=(
            field,
            matrix,
            vector,
            P("fsdp", "seq"),
            matrix,
            vector,
            vector,
            matrix,
            matrix,
            vector,
            matrix,
            vector,
            matrix,
            vector,
            field,
        ),
        out_specs=(
            field,
            field,
            matrix,
            matrix,
            vector,
            vector,
            matrix,
            matrix,
            vector,
            matrix,
            vector,
            matrix,
            vector,
            P(),
            P(),
            P(),
        ),
        check_vma=False,
    )
```

```python
from functools import partial

import jax
import jax.numpy as jnp
from jax import lax
from jax.experimental import pallas as pl
from jax.experimental.pallas import tpu as pltpu
from jax.sharding import PartitionSpec as P


HD = 64
PAIR = 2 * HD
LOG2E = 1.4426950408889634
LN2 = 0.6931471805599453

epsilon = 1e-05
highest = lax.Precision.HIGHEST
f32 = jnp.float32
bf16 = jnp.bfloat16


def gelu_and_slope(value):
    square = value * value
    t = jnp.tanh(0.7978845608028654 * (value + 0.044715 * value * square))
    slope = 0.5 * (1.0 + t) + 0.5 * value * (1.0 - t * t) * (
        0.7978845608028654 * (1.0 + 3 * 0.044715 * square)
    )
    return 0.5 * value * (1.0 + t), slope


def rotary_tables(positions):
    inverse = 1.0 / 10000.0 ** (jnp.arange(0, HD, 2, dtype=f32) / HD)
    angles = positions.astype(f32)[:, None] * inverse
    cosine, sine = jnp.cos(angles), jnp.sin(angles)
    return jnp.tile(cosine, (1, 4)), jnp.tile(sine, (1, 4))


def rotate(u, cosine, sine, lane):
    first = (lane % HD) < (HD // 2)
    turned = jnp.where(first, -pltpu.roll(u, PAIR - HD // 2, 1), pltpu.roll(u, HD // 2, 1))
    return u * cosine + turned * sine


def rotate_back(g, cosine, sine, lane):
    first = (lane % HD) < (HD // 2)
    w = g * sine
    return g * cosine + jnp.where(first, pltpu.roll(w, PAIR - HD // 2, 1), -pltpu.roll(w, HD // 2, 1))


def parts(u):
    hi = u.astype(bf16).astype(f32)
    return hi, (u - hi).astype(bf16).astype(f32)


def both(u, head, lane):
    turned = pltpu.roll(u, HD, 1)
    return jnp.where((lane < HD) == (head == 0), u, turned)


def beside(left, right, head, lane):
    low = left if head == 0 else pltpu.roll(left, HD, 1)
    high_lanes = pltpu.roll(right, HD, 1) if head == 0 else right
    return jnp.where(lane < HD, low, high_lanes)


def three_terms(column, lane):
    a = column.astype(bf16).astype(f32)
    b = (column - a).astype(bf16).astype(f32)
    c = column - a - b
    return jnp.where(lane == HD, a, jnp.where(lane == HD + 1, b, jnp.where(lane == HD + 2, c, 0.0)))


def split_bf16(u):
    hi = u.astype(bf16)
    return hi, (u - hi.astype(f32)).astype(bf16)


def dot_nt(a, b):
    return lax.dot_general(a, b, (((1,), (1,)), ((), ())), preferred_element_type=f32)


def dot_nn(a, b):
    return lax.dot_general(a, b, (((1,), (0,)), ((), ())), preferred_element_type=f32)


def forward_kernel(
    len_ref, q_ref, k_ref, v_ref, cos_ref, sin_ref, out_ref, lse_ref, qs, ks, vs, acc, *, rows
):
    full_len = q_ref.shape[0]
    lane = lax.broadcasted_iota(jnp.int32, (full_len, PAIR), 1)
    place = lax.broadcasted_iota(jnp.int32, (full_len, PAIR), 0)
    cosine, sine = cos_ref[...], sin_ref[...]
    q = rotate(q_ref[...], cosine, sine, lane) * (HD**-0.5 * LOG2E)
    k = rotate(k_ref[...], cosine, sine, lane)
    q_hi, q_lo = parts(q)
    k_hi, k_lo = parts(k)
    v_hi, v_lo = parts(v_ref[...])
    bias = jnp.where(place < len_ref[0], 0.0, -1e30)
    for head in range(2):
        qs[head, :, :PAIR] = both(q_hi, head, lane).astype(bf16)
        qs[head, :, PAIR:] = jnp.where(
            lane < HD, beside(q_lo, q_lo, head, lane), jnp.where(lane == HD, 1.0, 0.0)
        ).astype(bf16)
        ks[head, :, :PAIR] = beside(k_hi, k_lo, head, lane).astype(bf16)
        ks[head, :, PAIR:] = jnp.where(
            lane < HD, beside(k_hi, k_hi, head, lane), jnp.where(lane == HD, bias, 0.0)
        ).astype(bf16)
        vs[head] = beside(v_hi, v_lo, head, lane).astype(bf16)

    low = lax.broadcasted_iota(jnp.int32, (rows, PAIR), 1) < HD
    units = [(block, head) for block in range(full_len // rows) for head in range(2)]

    def scores_of(unit):
        block, head = unit
        return dot_nt(qs[head, pl.ds(block * rows, rows), :], ks[head])

    following = scores_of(units[0])
    outs, lses = [], []
    for place, (block, head) in enumerate(units):
        scores = following
        if place + 1 < len(units):
            following = scores_of(units[place + 1])
        largest = jnp.max(scores, axis=1, keepdims=True)
        expo = jnp.exp2(scores - largest)
        total = jnp.sum(expo, axis=1, keepdims=True)
        hi, lo = split_bf16(expo)
        both_parts = dot_nn(hi, vs[head]) + dot_nn(lo, vs[head])
        outs.append((both_parts + pltpu.roll(both_parts, HD, 1)) / total)
        lses.append(largest + jnp.log2(total))
        if head == 1:
            at = pl.ds(block * rows, rows)
            out_ref[at, :] = jnp.where(low, outs[-2], outs[-1])
            lse_ref[at, :] = jnp.where(low, lses[-2], lses[-1])


def backward_kernel(
    len_ref,
    q_ref,
    k_ref,
    v_ref,
    cos_ref,
    sin_ref,
    out_in_ref,
    lse_ref,
    do_ref,
    grad_ref,
    qs,
    ks,
    vs,
    dos,
    kd,
    qt,
    dot_t,
    dq,
    dkt,
    dvt,
    *,
    rows,
):
    full_len = q_ref.shape[0]
    which = pl.program_id(1)
    lane = lax.broadcasted_iota(jnp.int32, (full_len, PAIR), 1)

    @pl.when(which == 0)
    def _():
        place = lax.broadcasted_iota(jnp.int32, (full_len, PAIR), 0)
        cosine, sine = cos_ref[...], sin_ref[...]
        q = rotate(q_ref[...], cosine, sine, lane) * (HD**-0.5 * LOG2E)
        k = rotate(k_ref[...], cosine, sine, lane)
        out_grad = do_ref[...]
        q_hi, q_lo = parts(q)
        k_hi, k_lo = parts(k)
        v_hi, v_lo = parts(v_ref[...])
        g_hi, g_lo = parts(out_grad)
        product = out_grad * out_in_ref[...]
        lse = lse_ref[...]
        bias = jnp.where(place < len_ref[0], 0.0, -1e30)
        ones = jnp.where((lane >= HD) & (lane < HD + 3), 1.0, 0.0)
        for head in range(2):
            mine = (lane < HD) == (head == 0)
            delta = jnp.sum(jnp.where(mine, product, 0.0), axis=1, keepdims=True)
            lse_head = jnp.max(jnp.where(mine, lse, -3e38), axis=1, keepdims=True)
            qs[head, :, :PAIR] = both(q_hi, head, lane).astype(bf16)
            qs[head, :, PAIR:] = jnp.where(
                lane < HD,
                beside(q_lo, q_lo, head, lane),
                three_terms(-lse_head, lane) + jnp.where(lane == HD + 3, 1.0, 0.0),
            ).astype(bf16)
            ks[head, :, :PAIR] = beside(k_hi, k_lo, head, lane).astype(bf16)
            ks[head, :, PAIR:] = jnp.where(
                lane < HD, beside(k_hi, k_hi, head, lane), ones + jnp.where(lane == HD + 3, bias, 0.0)
            ).astype(bf16)
            dos[head, :, :PAIR] = both(g_hi, head, lane).astype(bf16)
            dos[head, :, PAIR:] = jnp.where(
                lane < HD, beside(g_lo, g_lo, head, lane), three_terms(-delta, lane)
            ).astype(bf16)
            vs[head, :, :PAIR] = beside(v_hi, v_lo, head, lane).astype(bf16)
            vs[head, :, PAIR:] = jnp.where(lane < HD, beside(v_hi, v_hi, head, lane), ones).astype(bf16)
            kd[head] = beside(k_hi, k_lo, head, lane).astype(bf16)
            qt[head] = beside(q_hi, q_lo, head, lane).T.astype(bf16)
            dot_t[head] = beside(g_hi, g_lo, head, lane).T.astype(bf16)
        dkt[...] = jnp.zeros_like(dkt)
        dvt[...] = jnp.zeros_like(dvt)
        low = lax.broadcasted_iota(jnp.int32, (rows, PAIR), 1) < HD

        units = [(block, head) for block in range(full_len // rows) for head in range(2)]

        def products_of(unit):
            block, head = unit
            at = pl.ds(block * rows, rows)
            return dot_nt(qs[head, at, :], ks[head]), dot_nt(dos[head, at, :], vs[head])

        following = products_of(units[0])
        outs = []
        for order, (block, head) in enumerate(units):
            scores, weight_grad = following
            if order + 1 < len(units):
                following = products_of(units[order + 1])
            at = pl.ds(block * rows, rows)
            weights = jnp.exp2(scores)
            score_grad = weights * weight_grad
            w_hi, w_lo = split_bf16(weights)
            s_hi, s_lo = split_bf16(score_grad)
            both_parts = dot_nn(s_hi, kd[head]) + dot_nn(s_lo, kd[head])
            outs.append(both_parts + pltpu.roll(both_parts, HD, 1))
            q_t = qt[head, :, at]
            g_t = dot_t[head, :, at]
            dkt[head] += dot_nn(q_t, s_hi) + dot_nn(q_t, s_lo)
            dvt[head] += dot_nn(g_t, w_hi) + dot_nn(g_t, w_lo)
            if head == 1:
                dq[at, :] = jnp.where(low, outs[-2], outs[-1])
        grad_ref[...] = rotate_back(dq[...] * HD**-0.5, cosine, sine, lane)

    @pl.when(which == 1)
    def _():
        stacked = jnp.concatenate([dkt[h, :HD, :] + dkt[h, HD:, :] for h in range(2)], axis=0)
        grad_ref[...] = rotate_back(stacked.T * LN2, cos_ref[...], sin_ref[...], lane)

    @pl.when(which == 2)
    def _():
        stacked = jnp.concatenate([dvt[h, :HD, :] + dvt[h, HD:, :] for h in range(2)], axis=0)
        grad_ref[...] = stacked.T


def attention_forward(length, qkv, cosine, sine):
    full_len, three = qkv.shape
    width = three // 3
    pairs = width // PAIR
    rows = min(256, full_len)

    def column(offset):
        return pl.BlockSpec((full_len, PAIR), lambda p, ln: (0, p + offset))

    table = pl.BlockSpec((full_len, PAIR), lambda p, ln: (0, 0))
    wide = jax.ShapeDtypeStruct((full_len, width), f32)
    return pl.pallas_call(
        partial(forward_kernel, rows=rows),
        name="attention_forward",
        out_shape=(wide, wide),
        grid_spec=pltpu.PrefetchScalarGridSpec(
            num_scalar_prefetch=1,
            grid=(pairs,),
            in_specs=[column(0), column(pairs), column(2 * pairs), table, table],
            out_specs=(column(0), column(0)),
            scratch_shapes=[
                pltpu.VMEM((2, full_len, 2 * PAIR), bf16),
                pltpu.VMEM((2, full_len, 2 * PAIR), bf16),
                pltpu.VMEM((2, full_len, PAIR), bf16),
                pltpu.VMEM((8, 128), f32),
            ],
        ),
        cost_estimate=pl.CostEstimate(
            flops=24 * full_len * full_len * width, bytes_accessed=20 * full_len * width, transcendentals=0
        ),
    )(length, qkv, qkv, qkv, cosine, sine)


def attention_backward(length, qkv, cosine, sine, attended, lse, out_grad):
    full_len, three = qkv.shape
    width = three // 3
    pairs = width // PAIR
    rows = min(256, full_len)

    def column(offset):
        return pl.BlockSpec((full_len, PAIR), lambda p, c, ln: (0, p + offset))

    table = pl.BlockSpec((full_len, PAIR), lambda p, c, ln: (0, 0))
    stacked = pltpu.VMEM((2, full_len, 2 * PAIR), bf16)
    turned = pltpu.VMEM((2, PAIR, full_len), bf16)
    summed = pltpu.VMEM((2, PAIR, full_len), f32)
    return pl.pallas_call(
        partial(backward_kernel, rows=rows),
        name="attention_backward",
        out_shape=jax.ShapeDtypeStruct((full_len, three), f32),
        grid_spec=pltpu.PrefetchScalarGridSpec(
            num_scalar_prefetch=1,
            grid=(pairs, 3),
            in_specs=[
                column(0),
                column(pairs),
                column(2 * pairs),
                table,
                table,
                column(0),
                column(0),
                column(0),
            ],
            out_specs=pl.BlockSpec((full_len, PAIR), lambda p, c, ln: (0, c * pairs + p)),
            scratch_shapes=[
                stacked,
                stacked,
                stacked,
                stacked,
                pltpu.VMEM((2, full_len, PAIR), bf16),
                turned,
                turned,
                pltpu.VMEM((full_len, PAIR), f32),
                summed,
                summed,
            ],
        ),
        cost_estimate=pl.CostEstimate(
            flops=60 * full_len * full_len * width, bytes_accessed=32 * full_len * width, transcendentals=0
        ),
    )(length, qkv, qkv, qkv, cosine, sine, attended, lse, out_grad)


ATTN_GAIN, ATTN_SHIFT, ATTN_SCALE, ATTN_GATE, MLP_GAIN, MLP_SHIFT, MLP_SCALE, MLP_GATE, DOWN_BIAS = range(9)
VECTORS = 16
COLUMNS = 256


def put_left(ref, u, axis):
    hi, lo = split_bf16(u)
    size = u.shape[axis]
    for place, part in enumerate((hi, lo, hi)):
        if axis == 1:
            ref[:, place * size : (place + 1) * size] = part
        else:
            ref[place * size : (place + 1) * size, :] = part


def put_right(ref, u, axis):
    hi, lo = split_bf16(u)
    size = u.shape[axis]
    for place, part in enumerate((hi, hi, lo)):
        if axis == 1:
            ref[:, place * size : (place + 1) * size] = part
        else:
            ref[place * size : (place + 1) * size, :] = part


def normalized(v):
    average = jnp.mean(v, axis=-1, keepdims=True)
    centered = v - average
    rstd = lax.rsqrt(jnp.mean(centered * centered, axis=-1, keepdims=True) + epsilon)
    return centered * rstd, rstd


def modulated(v, vec_ref, gain, shift, scale):
    xhat, _ = normalized(v)
    return xhat * row(vec_ref, gain) * (1.0 + row(vec_ref, scale)) + row(vec_ref, shift)


def row(ref, index):
    return ref[index : index + 1, :]


def column_sum(u):
    return jnp.sum(u, axis=0, keepdims=True)


def norm_backward(e_ref, v_ref, extra_ref, vec_ref, gain, scale, out_ref, sums_ref, other_ref):
    full_len = v_ref.shape[0]
    rows = min(128, full_len)
    factor = (1.0 + row(vec_ref, scale)) * row(vec_ref, gain)

    def step(block, carry):
        at = pl.ds(pl.multiple_of(block * rows, rows), rows)
        e = e_ref[at, :]
        xhat, rstd = normalized(v_ref[at, :])
        f = e * factor
        grad = rstd * (
            f
            - jnp.mean(f, axis=-1, keepdims=True)
            - xhat * jnp.mean(f * xhat, axis=-1, keepdims=True)
        )
        out = extra_ref[at, :] + grad
        out_ref[at, :] = out
        new = [column_sum(e), column_sum(e * xhat)]
        if other_ref is not None:
            new.append(column_sum(out * other_ref[at, :]))
        return tuple(c + n for c, n in zip(carry, new))

    zero = jnp.zeros((1, v_ref.shape[1]), f32)
    count = 2 if other_ref is None else 3
    total = lax.fori_loop(0, full_len // rows, step, (zero,) * count)
    sums_ref[...] = jnp.zeros_like(sums_ref)
    sums_ref[0:1, :] = total[0]
    sums_ref[1:2, :] = total[1] * row(vec_ref, gain)
    sums_ref[2:3, :] = total[1] * (1.0 + row(vec_ref, scale))
    if other_ref is not None:
        sums_ref[3:4, :] = total[2]


def qkv_kernel(x_ref, vec_ref, w_ref, out_ref, left, right):
    @pl.when(pl.program_id(0) == 0)
    def _():
        put_left(left, modulated(x_ref[...], vec_ref, ATTN_GAIN, ATTN_SHIFT, ATTN_SCALE), 1)

    put_right(right, w_ref[...], 0)
    out_ref[...] = dot_nn(left[...], right[...])


def proj_kernel(
    len_ref, att_ref, x_ref, vec_ref, w_ref, proj_ref, middle_ref, sums_ref, left, right
):
    @pl.when(pl.program_id(0) == 0)
    def _():
        put_left(left, att_ref[...], 1)

    put_right(right, w_ref[...], 0)
    proj = dot_nn(left[...], right[...])
    x = x_ref[...]
    branch = row(vec_ref, ATTN_GATE) * proj
    proj_ref[...] = proj
    middle_ref[...] = x + branch
    valid = lax.broadcasted_iota(jnp.int32, x.shape, 0) < len_ref[0]
    sums_ref[...] = jnp.zeros_like(sums_ref)
    sums_ref[0:1, :] = column_sum(jnp.where(valid, x * x, 0.0))
    sums_ref[1:2, :] = column_sum(jnp.where(valid, branch * branch, 0.0))


def up_kernel(middle_ref, vec_ref, up_ref, bias_ref, act_ref, slope_ref, left, right, *, rows):
    @pl.when(pl.program_id(0) == 0)
    def _():
        put_left(left, modulated(middle_ref[...], vec_ref, MLP_GAIN, MLP_SHIFT, MLP_SCALE), 1)

    put_right(right, up_ref[...], 0)
    for block in range(middle_ref.shape[0] // rows):
        at = pl.ds(block * rows, rows)
        pre = dot_nn(left[at, :], right[...]) + bias_ref[...]
        act_ref[at, :], slope_ref[at, :] = gelu_and_slope(pre)


def down_kernel(
    len_ref, act_ref, down_ref, middle_ref, cot_ref, vec_ref, out_ref, sums_ref, left, right, acc
):
    step = pl.program_id(0)

    @pl.when(step == 0)
    def _():
        acc[...] = jnp.zeros_like(acc)

    put_left(left, act_ref[...], 1)
    put_right(right, down_ref[...], 0)
    acc[...] += dot_nn(left[...], right[...])

    @pl.when(step == pl.num_programs(0) - 1)
    def _():
        down_out = acc[...] + row(vec_ref, DOWN_BIAS)
        branch = row(vec_ref, MLP_GATE) * down_out
        out_ref[...] = middle_ref[...] + branch
        valid = lax.broadcasted_iota(jnp.int32, branch.shape, 0) < len_ref[0]
        sums_ref[...] = jnp.zeros_like(sums_ref)
        sums_ref[0:1, :] = column_sum(jnp.where(valid, branch * branch, 0.0))
        sums_ref[1:2, :] = column_sum(cot_ref[...] * down_out)


def down_grad_kernel(cot_ref, vec_ref, act_ref, grad_ref, sums_ref, left, right):
    @pl.when(pl.program_id(0) == 0)
    def _():
        grad = cot_ref[...] * row(vec_ref, MLP_GATE)
        put_left(left, grad.T, 1)
        sums_ref[...] = jnp.zeros_like(sums_ref)
        sums_ref[0:1, :] = column_sum(grad)

    put_right(right, act_ref[...], 0)
    chunk = COLUMNS
    count = left.shape[0] // chunk
    following = dot_nn(left[:chunk, :], right[...])
    for part in range(count):
        turned = following
        if part + 1 < count:
            following = dot_nn(left[(part + 1) * chunk : (part + 2) * chunk, :], right[...])
        grad_ref[:, part * chunk : (part + 1) * chunk] = turned.T


def mlp_backward_kernel(
    cot_ref,
    middle_ref,
    proj_ref,
    vec_ref,
    down_ref,
    up_ref,
    slope_ref,
    up_grad_ref,
    bias_grad_ref,
    middle_grad_ref,
    sums_ref,
    left,
    turned,
    down_cat,
    up_cat,
    pre_cat,
    pre_stack,
    acc,
    *,
    rows,
):
    step = pl.program_id(0)
    full_len = middle_ref.shape[0]

    @pl.when(step == 0)
    def _():
        put_left(left, cot_ref[...] * row(vec_ref, MLP_GATE), 1)
        normed = modulated(middle_ref[...], vec_ref, MLP_GAIN, MLP_SHIFT, MLP_SCALE)
        put_left(turned, normed.T, 1)
        acc[...] = jnp.zeros_like(acc)

    put_right(down_cat, down_ref[...], 1)
    put_right(up_cat, up_ref[...], 1)
    bias_grad = jnp.zeros_like(bias_grad_ref)
    blocks = [pl.ds(block * rows, rows) for block in range(full_len // rows)]

    def add_to_acc(at):
        acc[at, :] += dot_nt(pre_cat[at, :], up_cat[...])

    following = dot_nt(left[blocks[0], :], down_cat[...])
    for block, at in enumerate(blocks):
        act_grad = following
        if block + 1 < len(blocks):
            following = dot_nt(left[blocks[block + 1], :], down_cat[...])
        if block > 0:
            add_to_acc(blocks[block - 1])
        pre_grad = act_grad * slope_ref[at, :]
        bias_grad += column_sum(pre_grad)
        hi, lo = split_bf16(pre_grad)
        columns = hi.shape[1]
        for place, part in enumerate((hi, lo, hi)):
            pre_cat[at, place * columns : (place + 1) * columns] = part
        for place, part in enumerate((hi, hi, lo)):
            pre_stack[pl.ds(place * full_len + block * rows, rows), :] = part
    add_to_acc(blocks[-1])
    bias_grad_ref[...] = bias_grad
    up_grad_ref[...] = dot_nn(turned[...], pre_stack[...])

    @pl.when(step == pl.num_programs(0) - 1)
    def _():
        norm_backward(
            acc, middle_ref, cot_ref, vec_ref, MLP_GAIN, MLP_SCALE, middle_grad_ref, sums_ref, proj_ref
        )


def proj_backward_kernel(
    grad_ref, grad_block_ref, att_ref, vec_ref, vec_block_ref, w_ref, joined_ref, out_ref, w_grad_ref,
    left, turned, w_cat, stack,
):
    del joined_ref

    @pl.when(pl.program_id(0) == 0)
    def _():
        put_left(left, grad_ref[...] * row(vec_ref, ATTN_GATE), 1)
        put_left(turned, att_ref[...].T, 1)

    put_right(w_cat, w_ref[...], 1)
    out_ref[...] = dot_nt(left[...], w_cat[...])
    put_right(stack, grad_block_ref[...] * row(vec_block_ref, ATTN_GATE), 0)
    w_grad_ref[...] = dot_nn(turned[...], stack[...])


def tokens_grad_kernel(
    grad_ref, w_ref, x_ref, extra_ref, vec_ref, out_ref, sums_ref, left, w_cat, acc
):
    step = pl.program_id(0)

    @pl.when(step == 0)
    def _():
        acc[...] = jnp.zeros_like(acc)

    put_left(left, grad_ref[...], 1)
    put_right(w_cat, w_ref[...], 1)
    acc[...] += dot_nt(left[...], w_cat[...])

    @pl.when(step == pl.num_programs(0) - 1)
    def _():
        norm_backward(acc, x_ref, extra_ref, vec_ref, ATTN_GAIN, ATTN_SCALE, out_ref, sums_ref, None)


def qkv_grad_kernel(x_ref, vec_ref, grad_ref, out_ref, turned, stack):
    @pl.when(pl.program_id(0) == 0)
    def _():
        normed = modulated(x_ref[...], vec_ref, ATTN_GAIN, ATTN_SHIFT, ATTN_SCALE)
        put_left(turned, normed.T, 1)

    put_right(stack, grad_ref[...], 0)
    out_ref[...] = dot_nn(turned[...], stack[...])


def whole(shape):
    return pl.BlockSpec(shape, lambda *ids: (0,) * len(shape), pipeline_mode=pl.Buffered(1))


def by_columns(rows, columns, first=0):
    return pl.BlockSpec((rows, columns), lambda j, *refs: (0, first + j))


def by_rows(rows, columns, column=0):
    return pl.BlockSpec((rows, columns), lambda j, *refs: (j, column))


def dense(body, grid, in_specs, out_specs, out_shapes, scratch, products, args, scalars=0, aliases=None):
    moved = sum(a.size for a in args) + sum(o.size for o in out_shapes)
    return pl.pallas_call(
        body,
        out_shape=tuple(out_shapes),
        grid_spec=pltpu.PrefetchScalarGridSpec(
            num_scalar_prefetch=scalars,
            grid=(grid,),
            in_specs=in_specs,
            out_specs=tuple(out_specs),
            scratch_shapes=[pltpu.VMEM(shape, kind) for shape, kind in scratch],
        ),
        input_output_aliases=aliases or {},
        compiler_params=pltpu.CompilerParams(vmem_limit_bytes=60 << 20),
        cost_estimate=pl.CostEstimate(flops=6 * products, bytes_accessed=4 * moved, transcendentals=0),
    )(*args)


def array(*shape):
    return jax.ShapeDtypeStruct(shape, f32)


def mm_qkv(x, vectors, weight):
    t, d = x.shape
    n = 3 * d
    c = COLUMNS
    return dense(
        qkv_kernel,
        n // c,
        [whole((t, d)), whole((VECTORS, d)), by_columns(d, c)],
        [by_columns(t, c)],
        [array(t, n)],
        [((t, 3 * d), bf16), ((3 * d, c), bf16)],
        t * d * n,
        (x, vectors, weight),
    )[0]


def mm_proj(length, attended, x, vectors, weight):
    t, d = x.shape
    c = COLUMNS
    return dense(
        proj_kernel,
        d // c,
        [whole((t, d)), by_columns(t, c), by_columns(VECTORS, c), by_columns(d, c, 3 * d // c)],
        [by_columns(t, c), by_columns(t, c), by_columns(8, c)],
        [array(t, d), array(t, d), array(8, d)],
        [((t, 3 * d), bf16), ((3 * d, c), bf16)],
        t * d * d,
        (length, attended, x, vectors, weight),
        scalars=1,
    )


def mm_up(middle, vectors, up, up_bias):
    t, d = middle.shape
    n = up.shape[1]
    c = COLUMNS
    return dense(
        partial(up_kernel, rows=min(256, t)),
        n // c,
        [whole((t, d)), whole((VECTORS, d)), by_columns(d, c), by_columns(1, c)],
        [by_columns(t, c), by_columns(t, c)],
        [array(t, n), array(t, n)],
        [((t, 3 * d), bf16), ((3 * d, c), bf16)],
        t * d * n,
        (middle, vectors, up, up_bias),
    )


def mm_down(length, act, down, middle, cot, vectors):
    t, n = act.shape
    d = down.shape[1]
    c = 2 * COLUMNS
    return dense(
        down_kernel,
        n // c,
        [by_columns(t, c), by_rows(c, d), whole((t, d)), whole((t, d)), whole((VECTORS, d))],
        [whole((t, d)), whole((8, d))],
        [array(t, d), array(8, d)],
        [((t, 3 * c), bf16), ((3 * c, d), bf16), ((t, d), f32)],
        t * d * n,
        (length, act, down, middle, cot, vectors),
        scalars=1,
    )


def dw_down(cot, vectors, act):
    t, d = cot.shape
    n = act.shape[1]
    c = 2 * COLUMNS
    return dense(
        down_grad_kernel,
        n // c,
        [whole((t, d)), whole((VECTORS, d)), by_columns(t, c)],
        [by_rows(c, d), whole((8, d))],
        [array(n, d), array(8, d)],
        [((d, 3 * t), bf16), ((3 * t, c), bf16)],
        t * d * n,
        (cot, vectors, act),
    )


def mlp_backward(cot, middle, proj_out, vectors, down, up, slope):
    t, d = cot.shape
    n = up.shape[1]
    c = COLUMNS
    return dense(
        partial(mlp_backward_kernel, rows=min(256, t)),
        n // c,
        [
            whole((t, d)),
            whole((t, d)),
            whole((t, d)),
            whole((VECTORS, d)),
            by_rows(c, d),
            by_columns(d, c),
            by_columns(t, c),
        ],
        [by_columns(d, c), by_columns(1, c), whole((t, d)), whole((8, d))],
        [array(d, n + d), array(1, n), array(t, d), array(8, d)],
        [
            ((t, 3 * d), bf16),
            ((d, 3 * t), bf16),
            ((c, 3 * d), bf16),
            ((d, 3 * c), bf16),
            ((t, 3 * c), bf16),
            ((3 * t, c), bf16),
            ((t, d), f32),
        ],
        3 * t * d * n,
        (cot, middle, proj_out, vectors, down, up, slope),
    )


def proj_backward(middle_grad, attended, vectors, weight, joined):
    t, d = middle_grad.shape
    c = COLUMNS
    return dense(
        proj_backward_kernel,
        d // c,
        [
            whole((t, d)),
            by_columns(t, c),
            whole((t, d)),
            whole((VECTORS, d)),
            by_columns(VECTORS, c),
            by_rows(c, d, 3),
            pl.BlockSpec(memory_space=pl.ANY),
        ],
        [by_columns(t, c), by_columns(d, c, joined.shape[1] // c - d // c)],
        [array(t, d), array(*joined.shape)],
        [((t, 3 * d), bf16), ((d, 3 * t), bf16), ((c, 3 * d), bf16), ((3 * t, c), bf16)],
        2 * t * d * d,
        (middle_grad, middle_grad, attended, vectors, vectors, weight, joined),
        aliases={6: 1},
    )


def mm_tokens_grad(qkv_grad, weight, x, middle_grad, vectors):
    t, d = x.shape
    n = 3 * d
    c = COLUMNS
    return dense(
        tokens_grad_kernel,
        n // c,
        [by_columns(t, c), by_columns(d, c), whole((t, d)), whole((t, d)), whole((VECTORS, d))],
        [whole((t, d)), whole((8, d))],
        [array(t, d), array(8, d)],
        [((t, 3 * c), bf16), ((d, 3 * c), bf16), ((t, d), f32)],
        t * d * n,
        (qkv_grad, weight, x, middle_grad, vectors),
    )


def dw_qkv(x, vectors, qkv_grad):
    t, d = x.shape
    n = qkv_grad.shape[1]
    c = COLUMNS
    return dense(
        qkv_grad_kernel,
        n // c,
        [whole((t, d)), whole((VECTORS, d)), by_columns(t, c)],
        [by_columns(d, c)],
        [array(d, n)],
        [((d, 3 * t), bf16), ((3 * t, c), bf16)],
        t * d * n,
        (x, vectors, qkv_grad),
    )[0]


def padded_row(pieces):
    row = jnp.concatenate([piece.reshape(-1) for piece in pieces])
    return jnp.pad(row, (0, -row.shape[0] % 128))[None, :]


def cut(row, sizes):
    out, start = [], 0
    for size in sizes:
        out.append(row[:, start : start + size])
        start += size
    return out


def shards(
    tokens,
    time_embed,
    lengths,
    positions,
    ada_weight,
    ada_bias,
    attn_gain,
    qkv_weight,
    proj_weight,
    mlp_gain,
    up_weight,
    up_bias,
    down_weight,
    down_bias,
    cotangent,
):
    groups = lax.axis_size("seq")
    owners = lax.axis_size("fsdp")
    mine_seq = lax.axis_index("seq")
    mine_fsdp = lax.axis_index("fsdp")
    seqs_here, local_len, width = tokens.shape
    cond = time_embed.shape[1]
    full_len = local_len * groups
    hidden = up_weight.shape[1]
    assert seqs_here == groups

    def to_sequence(field):
        return lax.all_to_all(field, "seq", split_axis=0, concat_axis=1, tiled=True)[0]

    def to_tokens(field):
        pieces = field.reshape(groups, local_len, width)
        return lax.all_to_all(pieces, "seq", split_axis=0, concat_axis=0, tiled=True)

    def gather(shard):
        return lax.all_gather(shard, "fsdp", axis=0, tiled=True)

    def rows_of_all(row, axes):
        count = lax.axis_size(axes)
        sent = jnp.broadcast_to(row[None], (count,) + row.shape)
        return lax.all_to_all(sent, axes, split_axis=0, concat_axis=0, tiled=True)[:, 0]

    def exchanged(rows, axis, count, mine):
        if count > 8:
            all_rows = lax.all_gather(rows, axis, axis=0)
            return lax.dynamic_slice(all_rows, (0, mine, 0), (count, 1, rows.shape[1]))[:, 0]
        out = jnp.zeros_like(rows)
        for shift in range(count):
            target = (mine + shift) % count
            sent = lax.dynamic_slice(rows, (target, 0), (1, rows.shape[1]))
            if shift > 0:
                sent = lax.ppermute(sent, axis, [(i, (i + shift) % count) for i in range(count)])
            out = lax.dynamic_update_slice(out, sent, ((mine - shift) % count, 0))
        return out

    x = to_sequence(tokens)
    places = exchanged(positions, "seq", groups, mine_seq).reshape(full_len)
    length = lax.dynamic_slice(lengths, (mine_seq,), (1,))
    small = [time_embed, ada_bias, attn_gain, mlp_gain, up_bias, down_bias]
    small_sizes = [piece.size for piece in small]
    packed = gather(padded_row(small))
    time_all, ada_bias_full, attn_gain_full, mlp_gain_full, up_bias_full, down_bias_full = cut(
        packed, small_sizes
    )
    time_all = time_all.reshape(owners * seqs_here, cond)
    ada_bias_full, attn_gain_full, mlp_gain_full, up_bias_full, down_bias_full = (
        piece.reshape(1, -1)
        for piece in (ada_bias_full, attn_gain_full, mlp_gain_full, up_bias_full, down_bias_full)
    )
    silu_all = jax.nn.silu(time_all)
    ada_rows = ada_weight.shape[0]
    silu_cols = lax.dynamic_slice(silu_all, (0, mine_fsdp * ada_rows), (owners * seqs_here, ada_rows))
    silu_group = lax.dynamic_slice(
        silu_cols.reshape(owners, seqs_here, ada_rows), (0, mine_seq, 0), (owners, 1, ada_rows)
    )[:, 0]
    partial_rows = jnp.dot(silu_group, ada_weight, precision=highest)
    partial_rows = exchanged(partial_rows, "fsdp", owners, mine_fsdp)
    modulation = jnp.sum(partial_rows, axis=0, keepdims=True) + ada_bias_full
    shift_attn, scale_attn, gate_attn, shift_mlp, scale_mlp, gate_mlp = jnp.split(modulation, 6, axis=1)
    vectors = [
        attn_gain_full,
        shift_attn,
        scale_attn,
        gate_attn,
        mlp_gain_full,
        shift_mlp,
        scale_mlp,
        gate_mlp,
        down_bias_full,
    ]
    vectors = jnp.concatenate(vectors + [jnp.zeros((VECTORS - len(vectors), width), f32)], axis=0)
    attn_full = gather(jnp.concatenate([qkv_weight, proj_weight], axis=1))
    up_full = gather(up_weight)
    down_full = gather(down_weight)
    cosine, sine = rotary_tables(places)

    qkv = mm_qkv(x, vectors, attn_full)
    cot_in, _ = lax.optimization_barrier((cotangent, x))
    cot = to_sequence(cot_in)
    attended, lse = attention_forward(length, qkv, cosine, sine)
    proj_out, middle, attn_sums = mm_proj(length, attended, x, vectors, attn_full)
    hidden_act, gelu_slope = mm_up(middle, vectors, up_full, up_bias_full)
    block_out, mlp_sums = mm_down(length, hidden_act, down_full, middle, cot, vectors)
    block_out = to_tokens(block_out)

    def scatter(grad):
        return lax.psum_scatter(grad, "fsdp", scatter_dimension=0, tiled=True)

    down_weight_grad, down_sums = dw_down(cot, vectors, hidden_act)
    down_shard = scatter(down_weight_grad)
    up_weight_grad, up_bias_grad, middle_grad, mlp_norm_sums = mlp_backward(
        cot, middle, proj_out, vectors, down_full, up_full, gelu_slope
    )
    attended_grad, up_proj_grad = proj_backward(middle_grad, attended, vectors, attn_full, up_weight_grad)
    up_shard = scatter(up_proj_grad)
    down_total = lax.psum(down_shard, "seq")
    gate_mlp_grad, down_bias_grad = mlp_sums[1], down_sums[0]
    shift_mlp_grad, scale_mlp_grad, mlp_gain_grad, gate_attn_grad = (mlp_norm_sums[i] for i in range(4))
    sums = jnp.stack(
        [
            jnp.sum(attn_sums[0]),
            jnp.sum(attn_sums[1]),
            jnp.sum(mlp_sums[0]),
            length[0].astype(f32),
        ]
    )
    early_rows = [gate_attn_grad, shift_mlp_grad, scale_mlp_grad, gate_mlp_grad]
    early_sums = [mlp_gain_grad, up_bias_grad, down_bias_grad, sums]
    early_all = rows_of_all(padded_row(early_rows + early_sums), "fsdp")
    row_width = sum(piece.size for piece in early_rows)

    qkv_grad = attention_backward(length, qkv, cosine, sine, attended, lse, attended_grad)
    tokens_grad, attn_norm_sums = mm_tokens_grad(qkv_grad, attn_full, x, middle_grad, vectors)
    shift_attn_grad, scale_attn_grad, attn_gain_grad = (attn_norm_sums[i] for i in range(3))
    tokens_grad = to_tokens(tokens_grad)
    qkv_weight_grad, down_total = lax.optimization_barrier((dw_qkv(x, vectors, qkv_grad), down_total))
    qkv_shard = scatter(qkv_weight_grad)
    late_rows = [shift_attn_grad, scale_attn_grad]
    late_all = lax.all_gather(padded_row(late_rows + [attn_gain_grad]), "fsdp", axis=0, tiled=True)
    group_rows = jnp.concatenate([late_all[:, : 2 * width], early_all[:, :row_width]], axis=1)
    group_sums = jnp.concatenate(
        [jnp.sum(early_all[:, row_width:], axis=0), jnp.sum(late_all[:, 2 * width :], axis=0)]
    )
    group_all = lax.all_gather(
        jnp.concatenate([group_rows.reshape(-1), group_sums])[None, :], "seq", axis=0, tiled=True
    )
    all_rows, all_sums = cut(group_all, [group_rows.size, group_sums.size])
    all_rows = all_rows.reshape(groups, owners, group_rows.shape[1])
    all_rows = jnp.swapaxes(all_rows, 0, 1).reshape(owners * groups, group_rows.shape[1])
    shift_attn_rows, scale_attn_rows, gate_attn_rows, shift_mlp_rows, scale_mlp_rows, gate_mlp_rows = cut(
        all_rows, [width] * 6
    )
    totals = jnp.sum(all_sums, axis=0, keepdims=True)
    early_size = early_all.shape[1] - row_width
    mlp_gain_total, up_bias_total, down_bias_total, sums_total = cut(
        totals, [piece.size for piece in early_sums]
    )
    attn_gain_total = totals[:, early_size : early_size + width]
    modulation_rows = jnp.concatenate(
        [shift_attn_rows, scale_attn_rows, gate_attn_rows, shift_mlp_rows, scale_mlp_rows, gate_mlp_rows],
        axis=1,
    )

    ada_weight_grad = lax.dot_general(
        silu_cols, modulation_rows, (((0,), (0,)), ((), ())), precision=highest
    )
    time_cols = lax.dot_general(modulation_rows, ada_weight, (((1,), (1,)), ((), ())), precision=highest)
    time_cols = lax.all_gather(time_cols, "fsdp", axis=0)
    time_rows = lax.dynamic_slice(
        time_cols, (0, mine_fsdp * seqs_here, 0), (owners, seqs_here, ada_rows)
    )
    time_part = jnp.swapaxes(time_rows, 0, 1).reshape(seqs_here, cond)
    _, silu_back = jax.vjp(jax.nn.silu, time_embed)
    (time_grad,) = silu_back(time_part)

    def owned(total):
        size = total.shape[1] // owners
        return lax.dynamic_slice(total[0], (mine_fsdp * size,), (size,))

    rms = jnp.sqrt(sums_total[0, :3] / (sums_total[0, 3] * width))
    up_proj_total, qkv_total = lax.psum((up_shard, qkv_shard), "seq")
    up_total, proj_total = up_proj_total[:, :hidden], up_proj_total[:, hidden:]
    return (
        block_out,
        tokens_grad,
        time_grad,
        ada_weight_grad,
        owned(jnp.sum(modulation_rows, axis=0, keepdims=True)),
        owned(attn_gain_total),
        qkv_total,
        proj_total,
        owned(mlp_gain_total),
        up_total,
        owned(up_bias_total),
        down_total,
        owned(down_bias_total),
        rms[0],
        rms[1],
        rms[2],
    )


def solution(mesh):
    field = P("fsdp", "seq", None)
    matrix = P("fsdp", None)
    vector = P("fsdp")

    return jax.shard_map(
        shards,
        mesh=mesh,
        in_specs=(
            field,
            matrix,
            vector,
            P("fsdp", "seq"),
            matrix,
            vector,
            vector,
            matrix,
            matrix,
            vector,
            matrix,
            vector,
            matrix,
            vector,
            field,
        ),
        out_specs=(
            field,
            field,
            matrix,
            matrix,
            vector,
            vector,
            matrix,
            matrix,
            vector,
            matrix,
            vector,
            matrix,
            vector,
            P(),
            P(),
            P(),
        ),
        check_vma=False,
    )
```

```python
from functools import partial

import jax
import jax.numpy as jnp
from jax import lax
from jax.experimental import pallas as pl
from jax.experimental.pallas import tpu as pltpu
from jax.sharding import PartitionSpec as P


HD = 64
PAIR = 2 * HD
LOG2E = 1.4426950408889634
LN2 = 0.6931471805599453


epsilon = 1e-05
highest = lax.Precision.HIGHEST
f32 = jnp.float32
bf16 = jnp.bfloat16


def gelu_and_slope(value):
    square = value * value
    t = jnp.tanh(0.7978845608028654 * (value + 0.044715 * value * square))
    slope = 0.5 * (1.0 + t) + 0.5 * value * (1.0 - t * t) * (
        0.7978845608028654 * (1.0 + 3 * 0.044715 * square)
    )
    return 0.5 * value * (1.0 + t), slope


def rotary_tables(positions):
    inverse = 1.0 / 10000.0 ** (jnp.arange(0, HD, 2, dtype=f32) / HD)
    angles = positions.astype(f32)[:, None] * inverse
    cosine, sine = jnp.cos(angles), jnp.sin(angles)
    return jnp.tile(cosine, (1, 4)), jnp.tile(sine, (1, 4))


def rotate(u, cosine, sine, lane):
    first = (lane % HD) < (HD // 2)
    turned = jnp.where(first, -pltpu.roll(u, PAIR - HD // 2, 1), pltpu.roll(u, HD // 2, 1))
    return u * cosine + turned * sine


def rotate_back(g, cosine, sine, lane):
    first = (lane % HD) < (HD // 2)
    w = g * sine
    return g * cosine + jnp.where(first, pltpu.roll(w, PAIR - HD // 2, 1), -pltpu.roll(w, HD // 2, 1))


def parts(u):
    hi = u.astype(bf16).astype(f32)
    return hi, (u - hi).astype(bf16).astype(f32)


def both(u, head, lane):
    turned = pltpu.roll(u, HD, 1)
    return jnp.where((lane < HD) == (head == 0), u, turned)


def beside(left, right, head, lane):
    low = left if head == 0 else pltpu.roll(left, HD, 1)
    high_lanes = pltpu.roll(right, HD, 1) if head == 0 else right
    return jnp.where(lane < HD, low, high_lanes)


def three_terms(column, lane):
    a = column.astype(bf16).astype(f32)
    b = (column - a).astype(bf16).astype(f32)
    c = column - a - b
    return jnp.where(lane == HD, a, jnp.where(lane == HD + 1, b, jnp.where(lane == HD + 2, c, 0.0)))


def split_bf16(u):
    hi = u.astype(bf16)
    return hi, (u - hi.astype(f32)).astype(bf16)


def dot_nt(a, b):
    return lax.dot_general(a, b, (((1,), (1,)), ((), ())), preferred_element_type=f32)


def dot_nn(a, b):
    return lax.dot_general(a, b, (((1,), (0,)), ((), ())), preferred_element_type=f32)


def forward_kernel(
    len_ref, q_ref, k_ref, v_ref, cos_ref, sin_ref, out_ref, lse_ref, qs, ks, vs, acc, *, rows
):
    full_len = q_ref.shape[0]
    lane = lax.broadcasted_iota(jnp.int32, (full_len, PAIR), 1)
    place = lax.broadcasted_iota(jnp.int32, (full_len, PAIR), 0)
    cosine, sine = cos_ref[...], sin_ref[...]
    q = rotate(q_ref[...], cosine, sine, lane) * (HD**-0.5 * LOG2E)
    k = rotate(k_ref[...], cosine, sine, lane)
    q_hi, q_lo = parts(q)
    k_hi, k_lo = parts(k)
    v_hi, v_lo = parts(v_ref[...])
    bias = jnp.where(place < len_ref[0], 0.0, -1e30)
    for head in range(2):
        qs[head, :, :PAIR] = both(q_hi, head, lane).astype(bf16)
        qs[head, :, PAIR:] = jnp.where(
            lane < HD, beside(q_lo, q_lo, head, lane), jnp.where(lane == HD, 1.0, 0.0)
        ).astype(bf16)
        ks[head, :, :PAIR] = beside(k_hi, k_lo, head, lane).astype(bf16)
        ks[head, :, PAIR:] = jnp.where(
            lane < HD, beside(k_hi, k_hi, head, lane), jnp.where(lane == HD, bias, 0.0)
        ).astype(bf16)
        vs[head] = beside(v_hi, v_lo, head, lane).astype(bf16)

    low = lax.broadcasted_iota(jnp.int32, (rows, PAIR), 1) < HD
    units = [(block, head) for block in range(full_len // rows) for head in range(2)]

    def scores_of(unit):
        block, head = unit
        return dot_nt(qs[head, pl.ds(block * rows, rows), :], ks[head])

    following = scores_of(units[0])
    outs, lses = [], []
    for place, (block, head) in enumerate(units):
        scores = following
        if place + 1 < len(units):
            following = scores_of(units[place + 1])
        largest = jnp.max(scores, axis=1, keepdims=True)
        expo = jnp.exp2(scores - largest)
        total = jnp.sum(expo, axis=1, keepdims=True)
        hi, lo = split_bf16(expo)
        both_parts = dot_nn(hi, vs[head]) + dot_nn(lo, vs[head])
        outs.append((both_parts + pltpu.roll(both_parts, HD, 1)) / total)
        lses.append(largest + jnp.log2(total))
        if head == 1:
            at = pl.ds(block * rows, rows)
            out_ref[at, :] = jnp.where(low, outs[-2], outs[-1])
            lse_ref[at, :] = jnp.where(low, lses[-2], lses[-1])


def backward_kernel(
    len_ref, q_ref, k_ref, v_ref, cos_ref, sin_ref, out_in_ref, lse_ref, do_ref, *rest, rows
):
    grad_ref, qs, ks, vs, dos, kd, qt, dot_t, dq, dkt, dvt = rest[-11:]
    full_len = q_ref.shape[0]
    which = pl.program_id(1)
    lane = lax.broadcasted_iota(jnp.int32, (full_len, PAIR), 1)

    @pl.when(which == 0)
    def _():
        place = lax.broadcasted_iota(jnp.int32, (full_len, PAIR), 0)
        cosine, sine = cos_ref[...], sin_ref[...]
        q = rotate(q_ref[...], cosine, sine, lane) * (HD**-0.5 * LOG2E)
        k = rotate(k_ref[...], cosine, sine, lane)
        out_grad = do_ref[...]
        q_hi, q_lo = parts(q)
        k_hi, k_lo = parts(k)
        v_hi, v_lo = parts(v_ref[...])
        g_hi, g_lo = parts(out_grad)
        product = out_grad * out_in_ref[...]
        lse = lse_ref[...]
        bias = jnp.where(place < len_ref[0], 0.0, -1e30)
        ones = jnp.where((lane >= HD) & (lane < HD + 3), 1.0, 0.0)
        for head in range(2):
            mine = (lane < HD) == (head == 0)
            delta = jnp.sum(jnp.where(mine, product, 0.0), axis=1, keepdims=True)
            lse_head = jnp.max(jnp.where(mine, lse, -3e38), axis=1, keepdims=True)
            qs[head, :, :PAIR] = both(q_hi, head, lane).astype(bf16)
            qs[head, :, PAIR:] = jnp.where(
                lane < HD,
                beside(q_lo, q_lo, head, lane),
                three_terms(-lse_head, lane) + jnp.where(lane == HD + 3, 1.0, 0.0),
            ).astype(bf16)
            ks[head, :, :PAIR] = beside(k_hi, k_lo, head, lane).astype(bf16)
            ks[head, :, PAIR:] = jnp.where(
                lane < HD, beside(k_hi, k_hi, head, lane), ones + jnp.where(lane == HD + 3, bias, 0.0)
            ).astype(bf16)
            dos[head, :, :PAIR] = both(g_hi, head, lane).astype(bf16)
            dos[head, :, PAIR:] = jnp.where(
                lane < HD, beside(g_lo, g_lo, head, lane), three_terms(-delta, lane)
            ).astype(bf16)
            vs[head, :, :PAIR] = beside(v_hi, v_lo, head, lane).astype(bf16)
            vs[head, :, PAIR:] = jnp.where(lane < HD, beside(v_hi, v_hi, head, lane), ones).astype(bf16)
            kd[head] = beside(k_hi, k_lo, head, lane).astype(bf16)
            qt[head] = beside(q_hi, q_lo, head, lane).T.astype(bf16)
            dot_t[head] = beside(g_hi, g_lo, head, lane).T.astype(bf16)
        dkt[...] = jnp.zeros_like(dkt)
        dvt[...] = jnp.zeros_like(dvt)
        low = lax.broadcasted_iota(jnp.int32, (rows, PAIR), 1) < HD

        units = [(block, head) for block in range(full_len // rows) for head in range(2)]

        def products_of(unit):
            block, head = unit
            at = pl.ds(block * rows, rows)
            return dot_nt(qs[head, at, :], ks[head]), dot_nt(dos[head, at, :], vs[head])

        following = products_of(units[0])
        outs = []
        for order, (block, head) in enumerate(units):
            scores, weight_grad = following
            if order + 1 < len(units):
                following = products_of(units[order + 1])
            at = pl.ds(block * rows, rows)
            weights = jnp.exp2(scores)
            score_grad = weights * weight_grad
            w_hi, w_lo = split_bf16(weights)
            s_hi, s_lo = split_bf16(score_grad)
            both_parts = dot_nn(s_hi, kd[head]) + dot_nn(s_lo, kd[head])
            outs.append(both_parts + pltpu.roll(both_parts, HD, 1))
            q_t = qt[head, :, at]
            g_t = dot_t[head, :, at]
            dkt[head] += dot_nn(q_t, s_hi) + dot_nn(q_t, s_lo)
            dvt[head] += dot_nn(g_t, w_hi) + dot_nn(g_t, w_lo)
            if head == 1:
                dq[at, :] = jnp.where(low, outs[-2], outs[-1])
        grad_ref[...] = rotate_back(dq[...] * HD**-0.5, cosine, sine, lane)

    @pl.when(which == 1)
    def _():
        stacked = jnp.concatenate([dkt[h, :HD, :] + dkt[h, HD:, :] for h in range(2)], axis=0)
        grad_ref[...] = rotate_back(stacked.T * LN2, cos_ref[...], sin_ref[...], lane)

    @pl.when(which == 2)
    def _():
        stacked = jnp.concatenate([dvt[h, :HD, :] + dvt[h, HD:, :] for h in range(2)], axis=0)
        grad_ref[...] = stacked.T


def attention_forward(length, qkv, cosine, sine):
    full_len, three = qkv.shape
    width = three // 3
    pairs = width // PAIR
    rows = min(256, full_len)

    def column(offset):
        return pl.BlockSpec((full_len, PAIR), lambda p, ln: (0, p + offset))

    table = pl.BlockSpec((full_len, PAIR), lambda p, ln: (0, 0))
    wide = jax.ShapeDtypeStruct((full_len, width), f32)
    return pl.pallas_call(
        partial(forward_kernel, rows=rows),
        name="attention_forward",
        out_shape=(wide, wide),
        grid_spec=pltpu.PrefetchScalarGridSpec(
            num_scalar_prefetch=1,
            grid=(pairs,),
            in_specs=[column(0), column(pairs), column(2 * pairs), table, table],
            out_specs=(column(0), column(0)),
            scratch_shapes=[
                pltpu.VMEM((2, full_len, 2 * PAIR), bf16),
                pltpu.VMEM((2, full_len, 2 * PAIR), bf16),
                pltpu.VMEM((2, full_len, PAIR), bf16),
                pltpu.VMEM((8, 128), f32),
            ],
        ),
        cost_estimate=pl.CostEstimate(
            flops=24 * full_len * full_len * width, bytes_accessed=20 * full_len * width, transcendentals=0
        ),
    )(length, qkv, qkv, qkv, cosine, sine)


def attention_backward(length, qkv, cosine, sine, attended, lse, out_grad, first, last, joined):
    full_len, three = qkv.shape
    width = three // 3
    pairs = width // PAIR
    rows = min(256, full_len)

    def column(offset):
        return pl.BlockSpec((full_len, PAIR), lambda p, c, ln: (0, first + p + offset))

    table = pl.BlockSpec((full_len, PAIR), lambda p, c, ln: (0, 0))
    stacked = pltpu.VMEM((2, full_len, 2 * PAIR), bf16)
    turned = pltpu.VMEM((2, PAIR, full_len), bf16)
    summed = pltpu.VMEM((2, PAIR, full_len), f32)
    args = [length, qkv, qkv, qkv, cosine, sine, attended, lse, out_grad]
    in_specs = [
        column(0),
        column(pairs),
        column(2 * pairs),
        table,
        table,
        column(0),
        column(0),
        column(0),
    ]
    if joined is not None:
        args.append(joined)
        in_specs.append(pl.BlockSpec(memory_space=pl.ANY))
    share = (last - first) * full_len * PAIR
    return pl.pallas_call(
        partial(backward_kernel, rows=rows),
        out_shape=jax.ShapeDtypeStruct((full_len, three), f32),
        grid_spec=pltpu.PrefetchScalarGridSpec(
            num_scalar_prefetch=1,
            grid=(last - first, 3),
            in_specs=in_specs,
            out_specs=pl.BlockSpec((full_len, PAIR), lambda p, c, ln: (0, c * pairs + first + p)),
            scratch_shapes=[
                stacked,
                stacked,
                stacked,
                stacked,
                pltpu.VMEM((2, full_len, PAIR), bf16),
                turned,
                turned,
                pltpu.VMEM((full_len, PAIR), f32),
                summed,
                summed,
            ],
        ),
        input_output_aliases={} if joined is None else {len(args) - 1: 0},
        cost_estimate=pl.CostEstimate(
            flops=60 * full_len * share, bytes_accessed=32 * share, transcendentals=0
        ),
    )(*args)


ATTN_GAIN, ATTN_SHIFT, ATTN_SCALE, ATTN_GATE, MLP_GAIN, MLP_SHIFT, MLP_SCALE, MLP_GATE, DOWN_BIAS = range(9)
VECTORS = 16
COLUMNS = 256


def put_left(ref, u, axis):
    hi, lo = split_bf16(u)
    size = u.shape[axis]
    for place, part in enumerate((hi, lo, hi)):
        if axis == 1:
            ref[:, place * size : (place + 1) * size] = part
        else:
            ref[place * size : (place + 1) * size, :] = part


def put_right(ref, u, axis):
    hi, lo = split_bf16(u)
    size = u.shape[axis]
    for place, part in enumerate((hi, hi, lo)):
        if axis == 1:
            ref[:, place * size : (place + 1) * size] = part
        else:
            ref[place * size : (place + 1) * size, :] = part


def normalized(v):
    average = jnp.mean(v, axis=-1, keepdims=True)
    centered = v - average
    rstd = lax.rsqrt(jnp.mean(centered * centered, axis=-1, keepdims=True) + epsilon)
    return centered * rstd, rstd


def modulated(v, vec_ref, gain, shift, scale):
    xhat, _ = normalized(v)
    return xhat * row(vec_ref, gain) * (1.0 + row(vec_ref, scale)) + row(vec_ref, shift)


def row(ref, index):
    return ref[index : index + 1, :]


def column_sum(u):
    return jnp.sum(u, axis=0, keepdims=True)


def norm_backward(e_ref, v_ref, extra_ref, vec_ref, gain, scale, out_ref, sums_ref, other_ref):
    full_len = v_ref.shape[0]
    rows = min(128, full_len)
    factor = (1.0 + row(vec_ref, scale)) * row(vec_ref, gain)

    def step(block, carry):
        at = pl.ds(pl.multiple_of(block * rows, rows), rows)
        e = e_ref[at, :]
        xhat, rstd = normalized(v_ref[at, :])
        f = e * factor
        grad = rstd * (
            f
            - jnp.mean(f, axis=-1, keepdims=True)
            - xhat * jnp.mean(f * xhat, axis=-1, keepdims=True)
        )
        out = extra_ref[at, :] + grad
        out_ref[at, :] = out
        new = [column_sum(e), column_sum(e * xhat)]
        if other_ref is not None:
            new.append(column_sum(out * other_ref[at, :]))
        return tuple(c + n for c, n in zip(carry, new))

    zero = jnp.zeros((1, v_ref.shape[1]), f32)
    count = 2 if other_ref is None else 3
    total = lax.fori_loop(0, full_len // rows, step, (zero,) * count)
    sums_ref[...] = jnp.zeros_like(sums_ref)
    sums_ref[0:1, :] = total[0]
    sums_ref[1:2, :] = total[1] * row(vec_ref, gain)
    sums_ref[2:3, :] = total[1] * (1.0 + row(vec_ref, scale))
    if other_ref is not None:
        sums_ref[3:4, :] = total[2]


def qkv_kernel(x_ref, vec_ref, w_ref, out_ref, left, right):
    @pl.when(pl.program_id(0) == 0)
    def _():
        put_left(left, modulated(x_ref[...], vec_ref, ATTN_GAIN, ATTN_SHIFT, ATTN_SCALE), 1)

    put_right(right, w_ref[...], 0)
    out_ref[...] = dot_nn(left[...], right[...])


def proj_kernel(
    len_ref, att_ref, x_ref, vec_ref, w_ref, proj_ref, middle_ref, sums_ref, left, right
):
    @pl.when(pl.program_id(0) == 0)
    def _():
        put_left(left, att_ref[...], 1)

    put_right(right, w_ref[...], 0)
    proj = dot_nn(left[...], right[...])
    x = x_ref[...]
    branch = row(vec_ref, ATTN_GATE) * proj
    proj_ref[...] = proj
    middle_ref[...] = x + branch
    valid = lax.broadcasted_iota(jnp.int32, x.shape, 0) < len_ref[0]
    sums_ref[...] = jnp.zeros_like(sums_ref)
    sums_ref[0:1, :] = column_sum(jnp.where(valid, x * x, 0.0))
    sums_ref[1:2, :] = column_sum(jnp.where(valid, branch * branch, 0.0))


def up_kernel(middle_ref, vec_ref, up_ref, bias_ref, act_ref, slope_ref, left, right, *, rows):
    @pl.when(pl.program_id(0) == 0)
    def _():
        put_left(left, modulated(middle_ref[...], vec_ref, MLP_GAIN, MLP_SHIFT, MLP_SCALE), 1)

    put_right(right, up_ref[...], 0)
    for block in range(middle_ref.shape[0] // rows):
        at = pl.ds(block * rows, rows)
        pre = dot_nn(left[at, :], right[...]) + bias_ref[...]
        act_ref[at, :], slope_ref[at, :] = gelu_and_slope(pre)


def down_kernel(
    len_ref, act_ref, down_ref, middle_ref, cot_ref, vec_ref, out_ref, sums_ref, left, right, acc
):
    step = pl.program_id(0)

    @pl.when(step == 0)
    def _():
        acc[...] = jnp.zeros_like(acc)

    put_left(left, act_ref[...], 1)
    put_right(right, down_ref[...], 0)
    acc[...] += dot_nn(left[...], right[...])

    @pl.when(step == pl.num_programs(0) - 1)
    def _():
        down_out = acc[...] + row(vec_ref, DOWN_BIAS)
        branch = row(vec_ref, MLP_GATE) * down_out
        out_ref[...] = middle_ref[...] + branch
        valid = lax.broadcasted_iota(jnp.int32, branch.shape, 0) < len_ref[0]
        sums_ref[...] = jnp.zeros_like(sums_ref)
        sums_ref[0:1, :] = column_sum(jnp.where(valid, branch * branch, 0.0))
        sums_ref[1:2, :] = column_sum(cot_ref[...] * down_out)


def down_grad_kernel(cot_ref, vec_ref, act_ref, grad_ref, sums_ref, left, right):
    @pl.when(pl.program_id(0) == 0)
    def _():
        grad = cot_ref[...] * row(vec_ref, MLP_GATE)
        put_left(left, grad.T, 1)
        sums_ref[...] = jnp.zeros_like(sums_ref)
        sums_ref[0:1, :] = column_sum(grad)

    put_right(right, act_ref[...], 0)
    chunk = COLUMNS
    count = left.shape[0] // chunk
    following = dot_nn(left[:chunk, :], right[...])
    for part in range(count):
        turned = following
        if part + 1 < count:
            following = dot_nn(left[(part + 1) * chunk : (part + 2) * chunk, :], right[...])
        grad_ref[:, part * chunk : (part + 1) * chunk] = turned.T


def mlp_backward_kernel(
    cot_ref,
    middle_ref,
    proj_ref,
    vec_ref,
    down_ref,
    up_ref,
    slope_ref,
    up_grad_ref,
    bias_grad_ref,
    middle_grad_ref,
    sums_ref,
    left,
    turned,
    down_cat,
    up_cat,
    pre_cat,
    pre_stack,
    acc,
    *,
    rows,
):
    step = pl.program_id(0)
    full_len = middle_ref.shape[0]

    @pl.when(step == 0)
    def _():
        put_left(left, cot_ref[...] * row(vec_ref, MLP_GATE), 1)
        normed = modulated(middle_ref[...], vec_ref, MLP_GAIN, MLP_SHIFT, MLP_SCALE)
        put_left(turned, normed.T, 1)
        acc[...] = jnp.zeros_like(acc)

    put_right(down_cat, down_ref[...], 1)
    put_right(up_cat, up_ref[...], 1)
    bias_grad = jnp.zeros_like(bias_grad_ref)
    blocks = [pl.ds(block * rows, rows) for block in range(full_len // rows)]

    def add_to_acc(at):
        acc[at, :] += dot_nt(pre_cat[at, :], up_cat[...])

    following = dot_nt(left[blocks[0], :], down_cat[...])
    for block, at in enumerate(blocks):
        act_grad = following
        if block + 1 < len(blocks):
            following = dot_nt(left[blocks[block + 1], :], down_cat[...])
        if block > 0:
            add_to_acc(blocks[block - 1])
        pre_grad = act_grad * slope_ref[at, :]
        bias_grad += column_sum(pre_grad)
        hi, lo = split_bf16(pre_grad)
        columns = hi.shape[1]
        for place, part in enumerate((hi, lo, hi)):
            pre_cat[at, place * columns : (place + 1) * columns] = part
        for place, part in enumerate((hi, hi, lo)):
            pre_stack[pl.ds(place * full_len + block * rows, rows), :] = part
    add_to_acc(blocks[-1])
    bias_grad_ref[...] = bias_grad
    up_grad_ref[...] = dot_nn(turned[...], pre_stack[...])

    @pl.when(step == pl.num_programs(0) - 1)
    def _():
        norm_backward(
            acc, middle_ref, cot_ref, vec_ref, MLP_GAIN, MLP_SCALE, middle_grad_ref, sums_ref, proj_ref
        )


def proj_backward_kernel(
    grad_ref, grad_block_ref, att_ref, vec_ref, vec_block_ref, w_ref, joined_ref, out_ref, w_grad_ref,
    left, turned, w_cat, stack,
):
    del joined_ref

    @pl.when(pl.program_id(0) == 0)
    def _():
        put_left(left, grad_ref[...] * row(vec_ref, ATTN_GATE), 1)
        put_left(turned, att_ref[...].T, 1)

    put_right(w_cat, w_ref[...], 1)
    out_ref[...] = dot_nt(left[...], w_cat[...])
    put_right(stack, grad_block_ref[...] * row(vec_block_ref, ATTN_GATE), 0)
    w_grad_ref[...] = dot_nn(turned[...], stack[...])


def tokens_grad_kernel(
    grad_ref, w_ref, x_ref, extra_ref, vec_ref, out_ref, sums_ref, left, w_cat, acc
):
    step = pl.program_id(0)

    @pl.when(step == 0)
    def _():
        acc[...] = jnp.zeros_like(acc)

    put_left(left, grad_ref[...], 1)
    put_right(w_cat, w_ref[...], 1)
    acc[...] += dot_nt(left[...], w_cat[...])

    @pl.when(step == pl.num_programs(0) - 1)
    def _():
        norm_backward(acc, x_ref, extra_ref, vec_ref, ATTN_GAIN, ATTN_SCALE, out_ref, sums_ref, None)


def qkv_grad_kernel(x_ref, vec_ref, grad_ref, out_ref, turned, stack):
    @pl.when(pl.program_id(0) == 0)
    def _():
        normed = modulated(x_ref[...], vec_ref, ATTN_GAIN, ATTN_SHIFT, ATTN_SCALE)
        put_left(turned, normed.T, 1)

    put_right(stack, grad_ref[...], 0)
    out_ref[...] = dot_nn(turned[...], stack[...])


def whole(shape):
    return pl.BlockSpec(shape, lambda *ids: (0,) * len(shape), pipeline_mode=pl.Buffered(1))


def by_columns(rows, columns, first=0):
    return pl.BlockSpec((rows, columns), lambda j, *refs: (0, first + j))


def by_rows(rows, columns, column=0):
    return pl.BlockSpec((rows, columns), lambda j, *refs: (j, column))


def dense(body, grid, in_specs, out_specs, out_shapes, scratch, products, args, scalars=0, aliases=None):
    moved = sum(a.size for a in args) + sum(o.size for o in out_shapes)
    return pl.pallas_call(
        body,
        out_shape=tuple(out_shapes),
        grid_spec=pltpu.PrefetchScalarGridSpec(
            num_scalar_prefetch=scalars,
            grid=(grid,),
            in_specs=in_specs,
            out_specs=tuple(out_specs),
            scratch_shapes=[pltpu.VMEM(shape, kind) for shape, kind in scratch],
        ),
        input_output_aliases=aliases or {},
        compiler_params=pltpu.CompilerParams(vmem_limit_bytes=60 << 20),
        cost_estimate=pl.CostEstimate(flops=6 * products, bytes_accessed=4 * moved, transcendentals=0),
    )(*args)


def array(*shape):
    return jax.ShapeDtypeStruct(shape, f32)


def mm_qkv(x, vectors, weight):
    t, d = x.shape
    n = 3 * d
    c = COLUMNS
    return dense(
        qkv_kernel,
        n // c,
        [whole((t, d)), whole((VECTORS, d)), by_columns(d, c)],
        [by_columns(t, c)],
        [array(t, n)],
        [((t, 3 * d), bf16), ((3 * d, c), bf16)],
        t * d * n,
        (x, vectors, weight),
    )[0]


def mm_proj(length, attended, x, vectors, weight):
    t, d = x.shape
    c = COLUMNS
    return dense(
        proj_kernel,
        d // c,
        [whole((t, d)), by_columns(t, c), by_columns(VECTORS, c), by_columns(d, c, 3 * d // c)],
        [by_columns(t, c), by_columns(t, c), by_columns(8, c)],
        [array(t, d), array(t, d), array(8, d)],
        [((t, 3 * d), bf16), ((3 * d, c), bf16)],
        t * d * d,
        (length, attended, x, vectors, weight),
        scalars=1,
    )


def mm_up(middle, vectors, up, up_bias):
    t, d = middle.shape
    n = up.shape[1]
    c = COLUMNS
    return dense(
        partial(up_kernel, rows=min(256, t)),
        n // c,
        [whole((t, d)), whole((VECTORS, d)), by_columns(d, c), by_columns(1, c)],
        [by_columns(t, c), by_columns(t, c)],
        [array(t, n), array(t, n)],
        [((t, 3 * d), bf16), ((3 * d, c), bf16)],
        t * d * n,
        (middle, vectors, up, up_bias),
    )


def mm_down(length, act, down, middle, cot, vectors):
    t, n = act.shape
    d = down.shape[1]
    c = 2 * COLUMNS
    return dense(
        down_kernel,
        n // c,
        [by_columns(t, c), by_rows(c, d), whole((t, d)), whole((t, d)), whole((VECTORS, d))],
        [whole((t, d)), whole((8, d))],
        [array(t, d), array(8, d)],
        [((t, 3 * c), bf16), ((3 * c, d), bf16), ((t, d), f32)],
        t * d * n,
        (length, act, down, middle, cot, vectors),
        scalars=1,
    )


def dw_down(cot, vectors, act):
    t, d = cot.shape
    n = act.shape[1]
    c = 2 * COLUMNS
    return dense(
        down_grad_kernel,
        n // c,
        [whole((t, d)), whole((VECTORS, d)), by_columns(t, c)],
        [by_rows(c, d), whole((8, d))],
        [array(n, d), array(8, d)],
        [((d, 3 * t), bf16), ((3 * t, c), bf16)],
        t * d * n,
        (cot, vectors, act),
    )


def mlp_backward(cot, middle, proj_out, vectors, down, up, slope):
    t, d = cot.shape
    n = up.shape[1]
    c = COLUMNS
    return dense(
        partial(mlp_backward_kernel, rows=min(256, t)),
        n // c,
        [
            whole((t, d)),
            whole((t, d)),
            whole((t, d)),
            whole((VECTORS, d)),
            by_rows(c, d),
            by_columns(d, c),
            by_columns(t, c),
        ],
        [by_columns(d, c), by_columns(1, c), whole((t, d)), whole((8, d))],
        [array(d, n + d), array(1, n), array(t, d), array(8, d)],
        [
            ((t, 3 * d), bf16),
            ((d, 3 * t), bf16),
            ((c, 3 * d), bf16),
            ((d, 3 * c), bf16),
            ((t, 3 * c), bf16),
            ((3 * t, c), bf16),
            ((t, d), f32),
        ],
        3 * t * d * n,
        (cot, middle, proj_out, vectors, down, up, slope),
    )


def proj_backward(middle_grad, attended, vectors, weight, joined):
    t, d = middle_grad.shape
    c = COLUMNS
    return dense(
        proj_backward_kernel,
        d // c,
        [
            whole((t, d)),
            by_columns(t, c),
            whole((t, d)),
            whole((VECTORS, d)),
            by_columns(VECTORS, c),
            by_rows(c, d, 3),
            pl.BlockSpec(memory_space=pl.ANY),
        ],
        [by_columns(t, c), by_columns(d, c, joined.shape[1] // c - d // c)],
        [array(t, d), array(*joined.shape)],
        [((t, 3 * d), bf16), ((d, 3 * t), bf16), ((c, 3 * d), bf16), ((3 * t, c), bf16)],
        2 * t * d * d,
        (middle_grad, middle_grad, attended, vectors, vectors, weight, joined),
        aliases={6: 1},
    )


def mm_tokens_grad(qkv_grad, weight, x, middle_grad, vectors):
    t, d = x.shape
    n = 3 * d
    c = COLUMNS
    return dense(
        tokens_grad_kernel,
        n // c,
        [by_columns(t, c), by_columns(d, c), whole((t, d)), whole((t, d)), whole((VECTORS, d))],
        [whole((t, d)), whole((8, d))],
        [array(t, d), array(8, d)],
        [((t, 3 * c), bf16), ((d, 3 * c), bf16), ((t, d), f32)],
        t * d * n,
        (qkv_grad, weight, x, middle_grad, vectors),
    )


def dw_qkv(x, vectors, qkv_grad):
    t, d = x.shape
    n = qkv_grad.shape[1]
    c = COLUMNS
    return dense(
        qkv_grad_kernel,
        n // c,
        [whole((t, d)), whole((VECTORS, d)), by_columns(t, c)],
        [by_columns(d, c)],
        [array(d, n)],
        [((d, 3 * t), bf16), ((3 * t, c), bf16)],
        t * d * n,
        (x, vectors, qkv_grad),
    )[0]


def padded_row(pieces):
    row = jnp.concatenate([piece.reshape(-1) for piece in pieces])
    return jnp.pad(row, (0, -row.shape[0] % 128))[None, :]


def cut(row, sizes):
    out, start = [], 0
    for size in sizes:
        out.append(row[:, start : start + size])
        start += size
    return out


def shards(
    tokens,
    time_embed,
    lengths,
    positions,
    ada_weight,
    ada_bias,
    attn_gain,
    qkv_weight,
    proj_weight,
    mlp_gain,
    up_weight,
    up_bias,
    down_weight,
    down_bias,
    cotangent,
):
    groups = lax.axis_size("seq")
    owners = lax.axis_size("fsdp")
    mine_seq = lax.axis_index("seq")
    mine_fsdp = lax.axis_index("fsdp")
    seqs_here, local_len, width = tokens.shape
    cond = time_embed.shape[1]
    full_len = local_len * groups
    hidden = up_weight.shape[1]
    assert seqs_here == groups

    def to_sequence(field):
        return lax.all_to_all(field, "seq", split_axis=0, concat_axis=1, tiled=True)[0]

    def to_tokens(field):
        pieces = field.reshape(groups, local_len, width)
        return lax.all_to_all(pieces, "seq", split_axis=0, concat_axis=0, tiled=True)

    def gather(shard):
        return lax.all_gather(shard, "fsdp", axis=0, tiled=True)

    def rows_of_all(row, axes):
        count = lax.axis_size(axes)
        sent = jnp.broadcast_to(row[None], (count,) + row.shape)
        return lax.all_to_all(sent, axes, split_axis=0, concat_axis=0, tiled=True)[:, 0]

    def exchanged(rows, axis, count, mine):
        if count > 8:
            all_rows = lax.all_gather(rows, axis, axis=0)
            return lax.dynamic_slice(all_rows, (0, mine, 0), (count, 1, rows.shape[1]))[:, 0]
        out = jnp.zeros_like(rows)
        for shift in range(count):
            target = (mine + shift) % count
            sent = lax.dynamic_slice(rows, (target, 0), (1, rows.shape[1]))
            if shift > 0:
                sent = lax.ppermute(sent, axis, [(i, (i + shift) % count) for i in range(count)])
            out = lax.dynamic_update_slice(out, sent, ((mine - shift) % count, 0))
        return out

    def seq_shift(piece, shift):
        return lax.ppermute(piece, "seq", [(i, (i + shift) % groups) for i in range(groups)])

    def seq_gather(piece):
        pieces = jnp.stack([piece] + [seq_shift(piece, shift) for shift in range(1, groups)])
        order = [(mine_seq - place) % groups for place in range(groups)]
        return jnp.concatenate([lax.dynamic_slice_in_dim(pieces, at, 1, 0) for at in order], axis=0)

    def seq_partial(shard):
        pieces = shard.reshape((groups, -1) + shard.shape[1:])
        total = lax.dynamic_slice_in_dim(pieces, mine_seq, 1, 0)[0]
        for shift in range(1, groups):
            sent = lax.dynamic_slice_in_dim(pieces, (mine_seq + shift) % groups, 1, 0)[0]
            total = total + seq_shift(sent, shift)
        return total

    x = to_sequence(tokens)
    places = exchanged(positions, "seq", groups, mine_seq).reshape(full_len)
    length = lax.dynamic_slice(lengths, (mine_seq,), (1,))
    small = [time_embed, ada_bias, attn_gain, mlp_gain, up_bias, down_bias]
    small_sizes = [piece.size for piece in small]
    packed = gather(padded_row(small))
    time_all, ada_bias_full, attn_gain_full, mlp_gain_full, up_bias_full, down_bias_full = cut(
        packed, small_sizes
    )
    time_all = time_all.reshape(owners * seqs_here, cond)
    ada_bias_full, attn_gain_full, mlp_gain_full, up_bias_full, down_bias_full = (
        piece.reshape(1, -1)
        for piece in (ada_bias_full, attn_gain_full, mlp_gain_full, up_bias_full, down_bias_full)
    )
    silu_all = jax.nn.silu(time_all)
    ada_rows = ada_weight.shape[0]
    silu_cols = lax.dynamic_slice(silu_all, (0, mine_fsdp * ada_rows), (owners * seqs_here, ada_rows))
    silu_group = lax.dynamic_slice(
        silu_cols.reshape(owners, seqs_here, ada_rows), (0, mine_seq, 0), (owners, 1, ada_rows)
    )[:, 0]
    partial_rows = jnp.dot(silu_group, ada_weight, precision=highest)
    partial_rows = exchanged(partial_rows, "fsdp", owners, mine_fsdp)
    modulation = jnp.sum(partial_rows, axis=0, keepdims=True) + ada_bias_full
    shift_attn, scale_attn, gate_attn, shift_mlp, scale_mlp, gate_mlp = jnp.split(modulation, 6, axis=1)
    vectors = [
        attn_gain_full,
        shift_attn,
        scale_attn,
        gate_attn,
        mlp_gain_full,
        shift_mlp,
        scale_mlp,
        gate_mlp,
        down_bias_full,
    ]
    vectors = jnp.concatenate(vectors + [jnp.zeros((VECTORS - len(vectors), width), f32)], axis=0)
    attn_full = gather(jnp.concatenate([qkv_weight, proj_weight], axis=1))
    up_full = gather(up_weight)
    down_full = gather(down_weight)
    cosine, sine = rotary_tables(places)

    qkv = mm_qkv(x, vectors, attn_full)
    cot_in, _ = lax.optimization_barrier((cotangent, x))
    cot = to_sequence(cot_in)
    attended, lse = attention_forward(length, qkv, cosine, sine)
    proj_out, middle, attn_sums = mm_proj(length, attended, x, vectors, attn_full)
    hidden_act, gelu_slope = mm_up(middle, vectors, up_full, up_bias_full)
    block_out, mlp_sums = mm_down(length, hidden_act, down_full, middle, cot, vectors)
    block_out = to_tokens(block_out)

    def scatter(grad):
        return lax.psum_scatter(grad, "fsdp", scatter_dimension=0, tiled=True)

    down_weight_grad, down_sums = dw_down(cot, vectors, hidden_act)
    down_shard = scatter(down_weight_grad)
    up_weight_grad, up_bias_grad, middle_grad, mlp_norm_sums = mlp_backward(
        cot, middle, proj_out, vectors, down_full, up_full, gelu_slope
    )
    attended_grad, up_proj_grad = proj_backward(middle_grad, attended, vectors, attn_full, up_weight_grad)
    up_shard = scatter(up_proj_grad)
    down_part = seq_partial(down_shard)
    down_total = seq_gather(down_part).reshape(down_shard.shape)
    up_proj_total = lax.psum(up_shard, "seq")
    gate_mlp_grad, down_bias_grad = mlp_sums[1], down_sums[0]
    shift_mlp_grad, scale_mlp_grad, mlp_gain_grad, gate_attn_grad = (mlp_norm_sums[i] for i in range(4))
    sums = jnp.stack(
        [
            jnp.sum(attn_sums[0]),
            jnp.sum(attn_sums[1]),
            jnp.sum(mlp_sums[0]),
            length[0].astype(f32),
        ]
    )
    early_rows = [gate_attn_grad, shift_mlp_grad, scale_mlp_grad, gate_mlp_grad]
    early_sums = [mlp_gain_grad, up_bias_grad, down_bias_grad, sums]
    early_all = rows_of_all(padded_row(early_rows + early_sums), "fsdp")
    row_width = sum(piece.size for piece in early_rows)

    pairs = width // PAIR
    back_args = (length, qkv, cosine, sine, attended, lse, attended_grad)
    qkv_grad = attention_backward(*back_args, 0, pairs // 2, None)
    qkv_grad = attention_backward(*back_args, pairs // 2, pairs, qkv_grad)
    tokens_grad, attn_norm_sums = mm_tokens_grad(qkv_grad, attn_full, x, middle_grad, vectors)
    shift_attn_grad, scale_attn_grad, attn_gain_grad = (attn_norm_sums[i] for i in range(3))
    tokens_grad = to_tokens(tokens_grad)
    qkv_weight_grad, up_proj_total = lax.optimization_barrier(
        (dw_qkv(x, vectors, qkv_grad), up_proj_total)
    )
    up_total, proj_total = up_proj_total[:, :hidden], up_proj_total[:, hidden:]
    qkv_shard = scatter(qkv_weight_grad)
    late_rows = [shift_attn_grad, scale_attn_grad]
    late_all = gather(padded_row(late_rows + [attn_gain_grad]))
    group_rows = jnp.concatenate([late_all[:, : 2 * width], early_all[:, :row_width]], axis=1)
    group_sums = jnp.concatenate(
        [jnp.sum(early_all[:, row_width:], axis=0), jnp.sum(late_all[:, 2 * width :], axis=0)]
    )
    group_all = seq_gather(jnp.concatenate([group_rows.reshape(-1), group_sums]))
    all_rows, all_sums = cut(group_all, [group_rows.size, group_sums.size])
    all_rows = all_rows.reshape(groups, owners, group_rows.shape[1])
    all_rows = jnp.swapaxes(all_rows, 0, 1).reshape(owners * groups, group_rows.shape[1])
    shift_attn_rows, scale_attn_rows, gate_attn_rows, shift_mlp_rows, scale_mlp_rows, gate_mlp_rows = cut(
        all_rows, [width] * 6
    )
    totals = jnp.sum(all_sums, axis=0, keepdims=True)
    early_size = early_all.shape[1] - row_width
    mlp_gain_total, up_bias_total, down_bias_total, sums_total = cut(
        totals, [piece.size for piece in early_sums]
    )
    attn_gain_total = totals[:, early_size : early_size + width]
    modulation_rows = jnp.concatenate(
        [shift_attn_rows, scale_attn_rows, gate_attn_rows, shift_mlp_rows, scale_mlp_rows, gate_mlp_rows],
        axis=1,
    )

    ada_weight_grad = lax.dot_general(
        silu_cols, modulation_rows, (((0,), (0,)), ((), ())), precision=highest
    )
    time_cols = lax.dot_general(modulation_rows, ada_weight, (((1,), (1,)), ((), ())), precision=highest)
    time_cols = lax.all_gather(time_cols, "fsdp", axis=0)
    time_rows = lax.dynamic_slice(
        time_cols, (0, mine_fsdp * seqs_here, 0), (owners, seqs_here, ada_rows)
    )
    time_part = jnp.swapaxes(time_rows, 0, 1).reshape(seqs_here, cond)
    _, silu_back = jax.vjp(jax.nn.silu, time_embed)
    (time_grad,) = silu_back(time_part)

    def owned(total):
        size = total.shape[1] // owners
        return lax.dynamic_slice(total[0], (mine_fsdp * size,), (size,))

    rms = jnp.sqrt(sums_total[0, :3] / (sums_total[0, 3] * width))
    qkv_total = lax.psum(qkv_shard, "seq")
    return (
        block_out,
        tokens_grad,
        time_grad,
        ada_weight_grad,
        owned(jnp.sum(modulation_rows, axis=0, keepdims=True)),
        owned(attn_gain_total),
        qkv_total,
        proj_total,
        owned(mlp_gain_total),
        up_total,
        owned(up_bias_total),
        down_total,
        owned(down_bias_total),
        rms[0],
        rms[1],
        rms[2],
    )


def solution(mesh):
    field = P("fsdp", "seq", None)
    matrix = P("fsdp", None)
    vector = P("fsdp")

    return jax.shard_map(
        shards,
        mesh=mesh,
        in_specs=(
            field,
            matrix,
            vector,
            P("fsdp", "seq"),
            matrix,
            vector,
            vector,
            matrix,
            matrix,
            vector,
            matrix,
            vector,
            matrix,
            vector,
            field,
        ),
        out_specs=(
            field,
            field,
            matrix,
            matrix,
            vector,
            vector,
            matrix,
            matrix,
            vector,
            matrix,
            vector,
            matrix,
            vector,
            P(),
            P(),
            P(),
        ),
        check_vma=False,
    )
```

```python
from functools import partial

import jax
import jax.numpy as jnp
from jax import lax
from jax.experimental import pallas as pl
from jax.experimental.pallas import tpu as pltpu
from jax.sharding import PartitionSpec as P


HD = 64
PAIR = 2 * HD
LOG2E = 1.4426950408889634
LN2 = 0.6931471805599453


epsilon = 1e-05
highest = lax.Precision.HIGHEST
f32 = jnp.float32
bf16 = jnp.bfloat16


def gelu_and_slope(value):
    square = value * value
    t = jnp.tanh(0.7978845608028654 * (value + 0.044715 * value * square))
    slope = 0.5 * (1.0 + t) + 0.5 * value * (1.0 - t * t) * (
        0.7978845608028654 * (1.0 + 3 * 0.044715 * square)
    )
    return 0.5 * value * (1.0 + t), slope


def rotary_tables(positions):
    inverse = 1.0 / 10000.0 ** (jnp.arange(0, HD, 2, dtype=f32) / HD)
    angles = positions.astype(f32)[:, None] * inverse
    cosine, sine = jnp.cos(angles), jnp.sin(angles)
    return jnp.tile(cosine, (1, 4)), jnp.tile(sine, (1, 4))


def rotate(u, cosine, sine, lane):
    first = (lane % HD) < (HD // 2)
    turned = jnp.where(first, -pltpu.roll(u, PAIR - HD // 2, 1), pltpu.roll(u, HD // 2, 1))
    return u * cosine + turned * sine


def rotate_back(g, cosine, sine, lane):
    first = (lane % HD) < (HD // 2)
    w = g * sine
    return g * cosine + jnp.where(first, pltpu.roll(w, PAIR - HD // 2, 1), -pltpu.roll(w, HD // 2, 1))


def parts(u):
    hi = u.astype(bf16).astype(f32)
    return hi, (u - hi).astype(bf16).astype(f32)


def both(u, head, lane):
    turned = pltpu.roll(u, HD, 1)
    return jnp.where((lane < HD) == (head == 0), u, turned)


def beside(left, right, head, lane):
    low = left if head == 0 else pltpu.roll(left, HD, 1)
    high_lanes = pltpu.roll(right, HD, 1) if head == 0 else right
    return jnp.where(lane < HD, low, high_lanes)


def three_terms(column, lane):
    a = column.astype(bf16).astype(f32)
    b = (column - a).astype(bf16).astype(f32)
    c = column - a - b
    return jnp.where(lane == HD, a, jnp.where(lane == HD + 1, b, jnp.where(lane == HD + 2, c, 0.0)))


def split_bf16(u):
    hi = u.astype(bf16)
    return hi, (u - hi.astype(f32)).astype(bf16)


def dot_nt(a, b):
    return lax.dot_general(a, b, (((1,), (1,)), ((), ())), preferred_element_type=f32)


def dot_nn(a, b):
    return lax.dot_general(a, b, (((1,), (0,)), ((), ())), preferred_element_type=f32)


def forward_kernel(
    len_ref, q_ref, k_ref, v_ref, cos_ref, sin_ref, out_ref, lse_ref, qs, ks, vs, acc, *, rows
):
    full_len = q_ref.shape[0]
    lane = lax.broadcasted_iota(jnp.int32, (full_len, PAIR), 1)
    place = lax.broadcasted_iota(jnp.int32, (full_len, PAIR), 0)
    cosine, sine = cos_ref[...], sin_ref[...]
    q = rotate(q_ref[...], cosine, sine, lane) * (HD**-0.5 * LOG2E)
    k = rotate(k_ref[...], cosine, sine, lane)
    q_hi, q_lo = parts(q)
    k_hi, k_lo = parts(k)
    v_hi, v_lo = parts(v_ref[...])
    bias = jnp.where(place < len_ref[0], 0.0, -1e30)
    for head in range(2):
        qs[head, :, :PAIR] = both(q_hi, head, lane).astype(bf16)
        qs[head, :, PAIR:] = jnp.where(
            lane < HD, beside(q_lo, q_lo, head, lane), jnp.where(lane == HD, 1.0, 0.0)
        ).astype(bf16)
        ks[head, :, :PAIR] = beside(k_hi, k_lo, head, lane).astype(bf16)
        ks[head, :, PAIR:] = jnp.where(
            lane < HD, beside(k_hi, k_hi, head, lane), jnp.where(lane == HD, bias, 0.0)
        ).astype(bf16)
        vs[head] = beside(v_hi, v_lo, head, lane).astype(bf16)

    low = lax.broadcasted_iota(jnp.int32, (rows, PAIR), 1) < HD
    units = [(block, head) for block in range(full_len // rows) for head in range(2)]

    def scores_of(unit):
        block, head = unit
        return dot_nt(qs[head, pl.ds(block * rows, rows), :], ks[head])

    following = scores_of(units[0])
    outs, lses = [], []
    for place, (block, head) in enumerate(units):
        scores = following
        if place + 1 < len(units):
            following = scores_of(units[place + 1])
        largest = jnp.max(scores, axis=1, keepdims=True)
        expo = jnp.exp2(scores - largest)
        total = jnp.sum(expo, axis=1, keepdims=True)
        hi, lo = split_bf16(expo)
        both_parts = dot_nn(hi, vs[head]) + dot_nn(lo, vs[head])
        outs.append((both_parts + pltpu.roll(both_parts, HD, 1)) / total)
        lses.append(largest + jnp.log2(total))
        if head == 1:
            at = pl.ds(block * rows, rows)
            out_ref[at, :] = jnp.where(low, outs[-2], outs[-1])
            lse_ref[at, :] = jnp.where(low, lses[-2], lses[-1])


def backward_kernel(
    len_ref, q_ref, k_ref, v_ref, cos_ref, sin_ref, out_in_ref, lse_ref, do_ref, *rest, rows
):
    grad_ref, qs, ks, vs, dos, kd, qt, dot_t, dq, dkt, dvt = rest[-11:]
    full_len = q_ref.shape[0]
    which = pl.program_id(1)
    lane = lax.broadcasted_iota(jnp.int32, (full_len, PAIR), 1)

    @pl.when(which == 0)
    def _():
        place = lax.broadcasted_iota(jnp.int32, (full_len, PAIR), 0)
        cosine, sine = cos_ref[...], sin_ref[...]
        q = rotate(q_ref[...], cosine, sine, lane) * (HD**-0.5 * LOG2E)
        k = rotate(k_ref[...], cosine, sine, lane)
        out_grad = do_ref[...]
        q_hi, q_lo = parts(q)
        k_hi, k_lo = parts(k)
        v_hi, v_lo = parts(v_ref[...])
        g_hi, g_lo = parts(out_grad)
        product = out_grad * out_in_ref[...]
        lse = lse_ref[...]
        bias = jnp.where(place < len_ref[0], 0.0, -1e30)
        ones = jnp.where((lane >= HD) & (lane < HD + 3), 1.0, 0.0)
        for head in range(2):
            mine = (lane < HD) == (head == 0)
            delta = jnp.sum(jnp.where(mine, product, 0.0), axis=1, keepdims=True)
            lse_head = jnp.max(jnp.where(mine, lse, -3e38), axis=1, keepdims=True)
            qs[head, :, :PAIR] = both(q_hi, head, lane).astype(bf16)
            qs[head, :, PAIR:] = jnp.where(
                lane < HD,
                beside(q_lo, q_lo, head, lane),
                three_terms(-lse_head, lane) + jnp.where(lane == HD + 3, 1.0, 0.0),
            ).astype(bf16)
            ks[head, :, :PAIR] = beside(k_hi, k_lo, head, lane).astype(bf16)
            ks[head, :, PAIR:] = jnp.where(
                lane < HD, beside(k_hi, k_hi, head, lane), ones + jnp.where(lane == HD + 3, bias, 0.0)
            ).astype(bf16)
            dos[head, :, :PAIR] = both(g_hi, head, lane).astype(bf16)
            dos[head, :, PAIR:] = jnp.where(
                lane < HD, beside(g_lo, g_lo, head, lane), three_terms(-delta, lane)
            ).astype(bf16)
            vs[head, :, :PAIR] = beside(v_hi, v_lo, head, lane).astype(bf16)
            vs[head, :, PAIR:] = jnp.where(lane < HD, beside(v_hi, v_hi, head, lane), ones).astype(bf16)
            kd[head] = beside(k_hi, k_lo, head, lane).astype(bf16)
            qt[head] = beside(q_hi, q_lo, head, lane).T.astype(bf16)
            dot_t[head] = beside(g_hi, g_lo, head, lane).T.astype(bf16)
        dkt[...] = jnp.zeros_like(dkt)
        dvt[...] = jnp.zeros_like(dvt)
        low = lax.broadcasted_iota(jnp.int32, (rows, PAIR), 1) < HD

        units = [(block, head) for block in range(full_len // rows) for head in range(2)]

        def products_of(unit):
            block, head = unit
            at = pl.ds(block * rows, rows)
            return dot_nt(qs[head, at, :], ks[head]), dot_nt(dos[head, at, :], vs[head])

        following = products_of(units[0])
        outs = []
        for order, (block, head) in enumerate(units):
            scores, weight_grad = following
            if order + 1 < len(units):
                following = products_of(units[order + 1])
            at = pl.ds(block * rows, rows)
            weights = jnp.exp2(scores)
            score_grad = weights * weight_grad
            w_hi, w_lo = split_bf16(weights)
            s_hi, s_lo = split_bf16(score_grad)
            both_parts = dot_nn(s_hi, kd[head]) + dot_nn(s_lo, kd[head])
            outs.append(both_parts + pltpu.roll(both_parts, HD, 1))
            q_t = qt[head, :, at]
            g_t = dot_t[head, :, at]
            dkt[head] += dot_nn(q_t, s_hi) + dot_nn(q_t, s_lo)
            dvt[head] += dot_nn(g_t, w_hi) + dot_nn(g_t, w_lo)
            if head == 1:
                dq[at, :] = jnp.where(low, outs[-2], outs[-1])
        grad_ref[...] = rotate_back(dq[...] * HD**-0.5, cosine, sine, lane)

    @pl.when(which == 1)
    def _():
        stacked = jnp.concatenate([dkt[h, :HD, :] + dkt[h, HD:, :] for h in range(2)], axis=0)
        grad_ref[...] = rotate_back(stacked.T * LN2, cos_ref[...], sin_ref[...], lane)

    @pl.when(which == 2)
    def _():
        stacked = jnp.concatenate([dvt[h, :HD, :] + dvt[h, HD:, :] for h in range(2)], axis=0)
        grad_ref[...] = stacked.T


def attention_forward(length, qkv, cosine, sine):
    full_len, three = qkv.shape
    width = three // 3
    pairs = width // PAIR
    rows = min(256, full_len)

    def column(offset):
        return pl.BlockSpec((full_len, PAIR), lambda p, ln: (0, p + offset))

    table = pl.BlockSpec((full_len, PAIR), lambda p, ln: (0, 0))
    wide = jax.ShapeDtypeStruct((full_len, width), f32)
    return pl.pallas_call(
        partial(forward_kernel, rows=rows),
        name="attention_forward",
        out_shape=(wide, wide),
        grid_spec=pltpu.PrefetchScalarGridSpec(
            num_scalar_prefetch=1,
            grid=(pairs,),
            in_specs=[column(0), column(pairs), column(2 * pairs), table, table],
            out_specs=(column(0), column(0)),
            scratch_shapes=[
                pltpu.VMEM((2, full_len, 2 * PAIR), bf16),
                pltpu.VMEM((2, full_len, 2 * PAIR), bf16),
                pltpu.VMEM((2, full_len, PAIR), bf16),
                pltpu.VMEM((8, 128), f32),
            ],
        ),
        cost_estimate=pl.CostEstimate(
            flops=24 * full_len * full_len * width, bytes_accessed=20 * full_len * width, transcendentals=0
        ),
    )(length, qkv, qkv, qkv, cosine, sine)


def attention_backward(length, qkv, cosine, sine, attended, lse, out_grad, first, last, joined):
    full_len, three = qkv.shape
    width = three // 3
    pairs = width // PAIR
    rows = min(256, full_len)

    def column(offset):
        return pl.BlockSpec((full_len, PAIR), lambda p, c, ln: (0, first + p + offset))

    table = pl.BlockSpec((full_len, PAIR), lambda p, c, ln: (0, 0))
    stacked = pltpu.VMEM((2, full_len, 2 * PAIR), bf16)
    turned = pltpu.VMEM((2, PAIR, full_len), bf16)
    summed = pltpu.VMEM((2, PAIR, full_len), f32)
    args = [length, qkv, qkv, qkv, cosine, sine, attended, lse, out_grad]
    in_specs = [
        column(0),
        column(pairs),
        column(2 * pairs),
        table,
        table,
        column(0),
        column(0),
        column(0),
    ]
    if joined is not None:
        args.append(joined)
        in_specs.append(pl.BlockSpec(memory_space=pl.ANY))
    share = (last - first) * full_len * PAIR
    return pl.pallas_call(
        partial(backward_kernel, rows=rows),
        out_shape=jax.ShapeDtypeStruct((full_len, three), f32),
        grid_spec=pltpu.PrefetchScalarGridSpec(
            num_scalar_prefetch=1,
            grid=(last - first, 3),
            in_specs=in_specs,
            out_specs=pl.BlockSpec((full_len, PAIR), lambda p, c, ln: (0, c * pairs + first + p)),
            scratch_shapes=[
                stacked,
                stacked,
                stacked,
                stacked,
                pltpu.VMEM((2, full_len, PAIR), bf16),
                turned,
                turned,
                pltpu.VMEM((full_len, PAIR), f32),
                summed,
                summed,
            ],
        ),
        input_output_aliases={} if joined is None else {len(args) - 1: 0},
        cost_estimate=pl.CostEstimate(
            flops=60 * full_len * share, bytes_accessed=32 * share, transcendentals=0
        ),
    )(*args)


ATTN_GAIN, ATTN_SHIFT, ATTN_SCALE, ATTN_GATE, MLP_GAIN, MLP_SHIFT, MLP_SCALE, MLP_GATE, DOWN_BIAS = range(9)
VECTORS = 16
COLUMNS = 256


def put_left(ref, u, axis):
    hi, lo = split_bf16(u)
    size = u.shape[axis]
    for place, part in enumerate((hi, lo, hi)):
        if axis == 1:
            ref[:, place * size : (place + 1) * size] = part
        else:
            ref[place * size : (place + 1) * size, :] = part


def put_right(ref, u, axis):
    hi, lo = split_bf16(u)
    size = u.shape[axis]
    for place, part in enumerate((hi, hi, lo)):
        if axis == 1:
            ref[:, place * size : (place + 1) * size] = part
        else:
            ref[place * size : (place + 1) * size, :] = part


def normalized(v):
    average = jnp.mean(v, axis=-1, keepdims=True)
    centered = v - average
    rstd = lax.rsqrt(jnp.mean(centered * centered, axis=-1, keepdims=True) + epsilon)
    return centered * rstd, rstd


def modulated(v, vec_ref, gain, shift, scale):
    xhat, _ = normalized(v)
    return xhat * row(vec_ref, gain) * (1.0 + row(vec_ref, scale)) + row(vec_ref, shift)


def row(ref, index):
    return ref[index : index + 1, :]


def column_sum(u):
    return jnp.sum(u, axis=0, keepdims=True)


def norm_backward(e_ref, v_ref, extra_ref, vec_ref, gain, scale, out_ref, sums_ref, other_ref):
    full_len = v_ref.shape[0]
    rows = min(128, full_len)
    factor = (1.0 + row(vec_ref, scale)) * row(vec_ref, gain)

    def step(block, carry):
        at = pl.ds(pl.multiple_of(block * rows, rows), rows)
        e = e_ref[at, :]
        xhat, rstd = normalized(v_ref[at, :])
        f = e * factor
        grad = rstd * (
            f
            - jnp.mean(f, axis=-1, keepdims=True)
            - xhat * jnp.mean(f * xhat, axis=-1, keepdims=True)
        )
        out = extra_ref[at, :] + grad
        out_ref[at, :] = out
        new = [column_sum(e), column_sum(e * xhat)]
        if other_ref is not None:
            new.append(column_sum(out * other_ref[at, :]))
        return tuple(c + n for c, n in zip(carry, new))

    zero = jnp.zeros((1, v_ref.shape[1]), f32)
    count = 2 if other_ref is None else 3
    total = lax.fori_loop(0, full_len // rows, step, (zero,) * count)
    sums_ref[...] = jnp.zeros_like(sums_ref)
    sums_ref[0:1, :] = total[0]
    sums_ref[1:2, :] = total[1] * row(vec_ref, gain)
    sums_ref[2:3, :] = total[1] * (1.0 + row(vec_ref, scale))
    if other_ref is not None:
        sums_ref[3:4, :] = total[2]


def qkv_kernel(x_ref, vec_ref, w_ref, out_ref, left, right):
    @pl.when(pl.program_id(0) == 0)
    def _():
        put_left(left, modulated(x_ref[...], vec_ref, ATTN_GAIN, ATTN_SHIFT, ATTN_SCALE), 1)

    put_right(right, w_ref[...], 0)
    out_ref[...] = dot_nn(left[...], right[...])


def proj_kernel(
    len_ref, att_ref, x_ref, vec_ref, w_ref, proj_ref, middle_ref, sums_ref, left, right
):
    @pl.when(pl.program_id(0) == 0)
    def _():
        put_left(left, att_ref[...], 1)

    put_right(right, w_ref[...], 0)
    proj = dot_nn(left[...], right[...])
    x = x_ref[...]
    branch = row(vec_ref, ATTN_GATE) * proj
    proj_ref[...] = proj
    middle_ref[...] = x + branch
    valid = lax.broadcasted_iota(jnp.int32, x.shape, 0) < len_ref[0]
    sums_ref[...] = jnp.zeros_like(sums_ref)
    sums_ref[0:1, :] = column_sum(jnp.where(valid, x * x, 0.0))
    sums_ref[1:2, :] = column_sum(jnp.where(valid, branch * branch, 0.0))


def up_kernel(middle_ref, vec_ref, up_ref, bias_ref, act_ref, slope_ref, left, right, *, rows):
    @pl.when(pl.program_id(0) == 0)
    def _():
        put_left(left, modulated(middle_ref[...], vec_ref, MLP_GAIN, MLP_SHIFT, MLP_SCALE), 1)

    put_right(right, up_ref[...], 0)
    for block in range(middle_ref.shape[0] // rows):
        at = pl.ds(block * rows, rows)
        pre = dot_nn(left[at, :], right[...]) + bias_ref[...]
        act_ref[at, :], slope_ref[at, :] = gelu_and_slope(pre)


def down_kernel(
    len_ref, act_ref, down_ref, middle_ref, cot_ref, vec_ref, out_ref, sums_ref, left, right, acc
):
    step = pl.program_id(0)

    @pl.when(step == 0)
    def _():
        acc[...] = jnp.zeros_like(acc)

    put_left(left, act_ref[...], 1)
    put_right(right, down_ref[...], 0)
    acc[...] += dot_nn(left[...], right[...])

    @pl.when(step == pl.num_programs(0) - 1)
    def _():
        down_out = acc[...] + row(vec_ref, DOWN_BIAS)
        branch = row(vec_ref, MLP_GATE) * down_out
        out_ref[...] = middle_ref[...] + branch
        valid = lax.broadcasted_iota(jnp.int32, branch.shape, 0) < len_ref[0]
        sums_ref[...] = jnp.zeros_like(sums_ref)
        sums_ref[0:1, :] = column_sum(jnp.where(valid, branch * branch, 0.0))
        sums_ref[1:2, :] = column_sum(cot_ref[...] * down_out)


def down_grad_kernel(cot_ref, vec_ref, act_ref, grad_ref, sums_ref, left, right):
    @pl.when(pl.program_id(0) == 0)
    def _():
        grad = cot_ref[...] * row(vec_ref, MLP_GATE)
        put_left(left, grad.T, 1)
        sums_ref[...] = jnp.zeros_like(sums_ref)
        sums_ref[0:1, :] = column_sum(grad)

    put_right(right, act_ref[...], 0)
    chunk = COLUMNS
    count = left.shape[0] // chunk
    following = dot_nn(left[:chunk, :], right[...])
    for part in range(count):
        turned = following
        if part + 1 < count:
            following = dot_nn(left[(part + 1) * chunk : (part + 2) * chunk, :], right[...])
        grad_ref[:, part * chunk : (part + 1) * chunk] = turned.T


def mlp_backward_kernel(
    cot_ref,
    middle_ref,
    proj_ref,
    vec_ref,
    down_ref,
    up_ref,
    slope_ref,
    up_grad_ref,
    bias_grad_ref,
    middle_grad_ref,
    sums_ref,
    left,
    turned,
    down_cat,
    up_cat,
    pre_cat,
    pre_stack,
    acc,
    *,
    rows,
):
    step = pl.program_id(0)
    full_len = middle_ref.shape[0]

    @pl.when(step == 0)
    def _():
        put_left(left, cot_ref[...] * row(vec_ref, MLP_GATE), 1)
        normed = modulated(middle_ref[...], vec_ref, MLP_GAIN, MLP_SHIFT, MLP_SCALE)
        put_left(turned, normed.T, 1)
        acc[...] = jnp.zeros_like(acc)

    put_right(down_cat, down_ref[...], 1)
    put_right(up_cat, up_ref[...], 1)
    bias_grad = jnp.zeros_like(bias_grad_ref)
    blocks = [pl.ds(block * rows, rows) for block in range(full_len // rows)]

    def add_to_acc(at):
        acc[at, :] += dot_nt(pre_cat[at, :], up_cat[...])

    following = dot_nt(left[blocks[0], :], down_cat[...])
    for block, at in enumerate(blocks):
        act_grad = following
        if block + 1 < len(blocks):
            following = dot_nt(left[blocks[block + 1], :], down_cat[...])
        if block > 0:
            add_to_acc(blocks[block - 1])
        pre_grad = act_grad * slope_ref[at, :]
        bias_grad += column_sum(pre_grad)
        hi, lo = split_bf16(pre_grad)
        columns = hi.shape[1]
        for place, part in enumerate((hi, lo, hi)):
            pre_cat[at, place * columns : (place + 1) * columns] = part
        for place, part in enumerate((hi, hi, lo)):
            pre_stack[pl.ds(place * full_len + block * rows, rows), :] = part
    add_to_acc(blocks[-1])
    bias_grad_ref[...] = bias_grad
    up_grad_ref[...] = dot_nn(turned[...], pre_stack[...])

    @pl.when(step == pl.num_programs(0) - 1)
    def _():
        norm_backward(
            acc, middle_ref, cot_ref, vec_ref, MLP_GAIN, MLP_SCALE, middle_grad_ref, sums_ref, proj_ref
        )


def proj_backward_kernel(
    grad_ref, grad_block_ref, att_ref, vec_ref, vec_block_ref, w_ref, joined_ref, out_ref, w_grad_ref,
    left, turned, w_cat, stack,
):
    del joined_ref

    @pl.when(pl.program_id(0) == 0)
    def _():
        put_left(left, grad_ref[...] * row(vec_ref, ATTN_GATE), 1)
        put_left(turned, att_ref[...].T, 1)

    put_right(w_cat, w_ref[...], 1)
    out_ref[...] = dot_nt(left[...], w_cat[...])
    put_right(stack, grad_block_ref[...] * row(vec_block_ref, ATTN_GATE), 0)
    w_grad_ref[...] = dot_nn(turned[...], stack[...])


def tokens_grad_kernel(
    grad_ref, w_ref, x_ref, extra_ref, vec_ref, out_ref, sums_ref, left, w_cat, acc
):
    step = pl.program_id(0)

    @pl.when(step == 0)
    def _():
        acc[...] = jnp.zeros_like(acc)

    put_left(left, grad_ref[...], 1)
    put_right(w_cat, w_ref[...], 1)
    acc[...] += dot_nt(left[...], w_cat[...])

    @pl.when(step == pl.num_programs(0) - 1)
    def _():
        norm_backward(acc, x_ref, extra_ref, vec_ref, ATTN_GAIN, ATTN_SCALE, out_ref, sums_ref, None)


def qkv_grad_kernel(x_ref, vec_ref, grad_ref, out_ref, turned, stack):
    @pl.when(pl.program_id(0) == 0)
    def _():
        normed = modulated(x_ref[...], vec_ref, ATTN_GAIN, ATTN_SHIFT, ATTN_SCALE)
        put_left(turned, normed.T, 1)

    put_right(stack, grad_ref[...], 0)
    out_ref[...] = dot_nn(turned[...], stack[...])


def whole(shape):
    return pl.BlockSpec(shape, lambda *ids: (0,) * len(shape), pipeline_mode=pl.Buffered(1))


def by_columns(rows, columns, first=0):
    return pl.BlockSpec((rows, columns), lambda j, *refs: (0, first + j))


def by_rows(rows, columns, column=0):
    return pl.BlockSpec((rows, columns), lambda j, *refs: (j, column))


def dense(body, grid, in_specs, out_specs, out_shapes, scratch, products, args, scalars=0, aliases=None):
    moved = sum(a.size for a in args) + sum(o.size for o in out_shapes)
    return pl.pallas_call(
        body,
        out_shape=tuple(out_shapes),
        grid_spec=pltpu.PrefetchScalarGridSpec(
            num_scalar_prefetch=scalars,
            grid=(grid,),
            in_specs=in_specs,
            out_specs=tuple(out_specs),
            scratch_shapes=[pltpu.VMEM(shape, kind) for shape, kind in scratch],
        ),
        input_output_aliases=aliases or {},
        compiler_params=pltpu.CompilerParams(vmem_limit_bytes=60 << 20),
        cost_estimate=pl.CostEstimate(flops=6 * products, bytes_accessed=4 * moved, transcendentals=0),
    )(*args)


def array(*shape):
    return jax.ShapeDtypeStruct(shape, f32)


def mm_qkv(x, vectors, weight):
    t, d = x.shape
    n = 3 * d
    c = COLUMNS
    return dense(
        qkv_kernel,
        n // c,
        [whole((t, d)), whole((VECTORS, d)), by_columns(d, c)],
        [by_columns(t, c)],
        [array(t, n)],
        [((t, 3 * d), bf16), ((3 * d, c), bf16)],
        t * d * n,
        (x, vectors, weight),
    )[0]


def mm_proj(length, attended, x, vectors, weight):
    t, d = x.shape
    c = COLUMNS
    return dense(
        proj_kernel,
        d // c,
        [whole((t, d)), by_columns(t, c), by_columns(VECTORS, c), by_columns(d, c, 3 * d // c)],
        [by_columns(t, c), by_columns(t, c), by_columns(8, c)],
        [array(t, d), array(t, d), array(8, d)],
        [((t, 3 * d), bf16), ((3 * d, c), bf16)],
        t * d * d,
        (length, attended, x, vectors, weight),
        scalars=1,
    )


def mm_up(middle, vectors, up, up_bias):
    t, d = middle.shape
    n = up.shape[1]
    c = COLUMNS
    return dense(
        partial(up_kernel, rows=min(256, t)),
        n // c,
        [whole((t, d)), whole((VECTORS, d)), by_columns(d, c), by_columns(1, c)],
        [by_columns(t, c), by_columns(t, c)],
        [array(t, n), array(t, n)],
        [((t, 3 * d), bf16), ((3 * d, c), bf16)],
        t * d * n,
        (middle, vectors, up, up_bias),
    )


def mm_down(length, act, down, middle, cot, vectors):
    t, n = act.shape
    d = down.shape[1]
    c = 2 * COLUMNS
    return dense(
        down_kernel,
        n // c,
        [by_columns(t, c), by_rows(c, d), whole((t, d)), whole((t, d)), whole((VECTORS, d))],
        [whole((t, d)), whole((8, d))],
        [array(t, d), array(8, d)],
        [((t, 3 * c), bf16), ((3 * c, d), bf16), ((t, d), f32)],
        t * d * n,
        (length, act, down, middle, cot, vectors),
        scalars=1,
    )


def dw_down(cot, vectors, act):
    t, d = cot.shape
    n = act.shape[1]
    c = 2 * COLUMNS
    return dense(
        down_grad_kernel,
        n // c,
        [whole((t, d)), whole((VECTORS, d)), by_columns(t, c)],
        [by_rows(c, d), whole((8, d))],
        [array(n, d), array(8, d)],
        [((d, 3 * t), bf16), ((3 * t, c), bf16)],
        t * d * n,
        (cot, vectors, act),
    )


def mlp_backward(cot, middle, proj_out, vectors, down, up, slope):
    t, d = cot.shape
    n = up.shape[1]
    c = COLUMNS
    return dense(
        partial(mlp_backward_kernel, rows=min(256, t)),
        n // c,
        [
            whole((t, d)),
            whole((t, d)),
            whole((t, d)),
            whole((VECTORS, d)),
            by_rows(c, d),
            by_columns(d, c),
            by_columns(t, c),
        ],
        [by_columns(d, c), by_columns(1, c), whole((t, d)), whole((8, d))],
        [array(d, n + d), array(1, n), array(t, d), array(8, d)],
        [
            ((t, 3 * d), bf16),
            ((d, 3 * t), bf16),
            ((c, 3 * d), bf16),
            ((d, 3 * c), bf16),
            ((t, 3 * c), bf16),
            ((3 * t, c), bf16),
            ((t, d), f32),
        ],
        3 * t * d * n,
        (cot, middle, proj_out, vectors, down, up, slope),
    )


def proj_backward(middle_grad, attended, vectors, weight, joined):
    t, d = middle_grad.shape
    c = COLUMNS
    return dense(
        proj_backward_kernel,
        d // c,
        [
            whole((t, d)),
            by_columns(t, c),
            whole((t, d)),
            whole((VECTORS, d)),
            by_columns(VECTORS, c),
            by_rows(c, d, 3),
            pl.BlockSpec(memory_space=pl.ANY),
        ],
        [by_columns(t, c), by_columns(d, c, joined.shape[1] // c - d // c)],
        [array(t, d), array(*joined.shape)],
        [((t, 3 * d), bf16), ((d, 3 * t), bf16), ((c, 3 * d), bf16), ((3 * t, c), bf16)],
        2 * t * d * d,
        (middle_grad, middle_grad, attended, vectors, vectors, weight, joined),
        aliases={6: 1},
    )


def mm_tokens_grad(qkv_grad, weight, x, middle_grad, vectors):
    t, d = x.shape
    n = 3 * d
    c = COLUMNS
    return dense(
        tokens_grad_kernel,
        n // c,
        [by_columns(t, c), by_columns(d, c), whole((t, d)), whole((t, d)), whole((VECTORS, d))],
        [whole((t, d)), whole((8, d))],
        [array(t, d), array(8, d)],
        [((t, 3 * c), bf16), ((d, 3 * c), bf16), ((t, d), f32)],
        t * d * n,
        (qkv_grad, weight, x, middle_grad, vectors),
    )


def dw_qkv(x, vectors, qkv_grad):
    t, d = x.shape
    n = qkv_grad.shape[1]
    c = COLUMNS
    return dense(
        qkv_grad_kernel,
        n // c,
        [whole((t, d)), whole((VECTORS, d)), by_columns(t, c)],
        [by_columns(d, c)],
        [array(d, n)],
        [((d, 3 * t), bf16), ((3 * t, c), bf16)],
        t * d * n,
        (x, vectors, qkv_grad),
    )[0]


def padded_row(pieces):
    row = jnp.concatenate([piece.reshape(-1) for piece in pieces])
    return jnp.pad(row, (0, -row.shape[0] % 128))[None, :]


def cut(row, sizes):
    out, start = [], 0
    for size in sizes:
        out.append(row[:, start : start + size])
        start += size
    return out


def shards(
    tokens,
    time_embed,
    lengths,
    positions,
    ada_weight,
    ada_bias,
    attn_gain,
    qkv_weight,
    proj_weight,
    mlp_gain,
    up_weight,
    up_bias,
    down_weight,
    down_bias,
    cotangent,
):
    groups = lax.axis_size("seq")
    owners = lax.axis_size("fsdp")
    mine_seq = lax.axis_index("seq")
    mine_fsdp = lax.axis_index("fsdp")
    seqs_here, local_len, width = tokens.shape
    cond = time_embed.shape[1]
    full_len = local_len * groups
    hidden = up_weight.shape[1]
    assert seqs_here == groups

    def to_sequence(field):
        return lax.all_to_all(field, "seq", split_axis=0, concat_axis=1, tiled=True)[0]

    def to_tokens(field):
        pieces = field.reshape(groups, local_len, width)
        return lax.all_to_all(pieces, "seq", split_axis=0, concat_axis=0, tiled=True)

    def gather(shard):
        return lax.all_gather(shard, "fsdp", axis=0, tiled=True)

    def exchanged(rows, axis, count, mine):
        if count > 8:
            all_rows = lax.all_gather(rows, axis, axis=0)
            return lax.dynamic_slice(all_rows, (0, mine, 0), (count, 1, rows.shape[1]))[:, 0]
        out = jnp.zeros_like(rows)
        for shift in range(count):
            target = (mine + shift) % count
            sent = lax.dynamic_slice(rows, (target, 0), (1, rows.shape[1]))
            if shift > 0:
                sent = lax.ppermute(sent, axis, [(i, (i + shift) % count) for i in range(count)])
            out = lax.dynamic_update_slice(out, sent, ((mine - shift) % count, 0))
        return out

    def seq_shift(piece, shift):
        return lax.ppermute(piece, "seq", [(i, (i + shift) % groups) for i in range(groups)])

    def seq_gather(piece):
        pieces = jnp.stack([piece] + [seq_shift(piece, shift) for shift in range(1, groups)])
        order = [(mine_seq - place) % groups for place in range(groups)]
        return jnp.concatenate([lax.dynamic_slice_in_dim(pieces, at, 1, 0) for at in order], axis=0)

    def seq_partial(shard):
        pieces = shard.reshape((groups, -1) + shard.shape[1:])
        total = lax.dynamic_slice_in_dim(pieces, mine_seq, 1, 0)[0]
        for shift in range(1, groups):
            sent = lax.dynamic_slice_in_dim(pieces, (mine_seq + shift) % groups, 1, 0)[0]
            total = total + seq_shift(sent, shift)
        return total

    x = to_sequence(tokens)
    places = exchanged(positions, "seq", groups, mine_seq).reshape(full_len)
    length = lax.dynamic_slice(lengths, (mine_seq,), (1,))
    small = [time_embed, ada_bias, attn_gain, mlp_gain, up_bias, down_bias]
    small_sizes = [piece.size for piece in small]
    packed = gather(padded_row(small))
    time_all, ada_bias_full, attn_gain_full, mlp_gain_full, up_bias_full, down_bias_full = cut(
        packed, small_sizes
    )
    time_all = time_all.reshape(owners * seqs_here, cond)
    ada_bias_full, attn_gain_full, mlp_gain_full, up_bias_full, down_bias_full = (
        piece.reshape(1, -1)
        for piece in (ada_bias_full, attn_gain_full, mlp_gain_full, up_bias_full, down_bias_full)
    )
    silu_all = jax.nn.silu(time_all)
    ada_rows = ada_weight.shape[0]
    silu_cols = lax.dynamic_slice(silu_all, (0, mine_fsdp * ada_rows), (owners * seqs_here, ada_rows))
    silu_group = lax.dynamic_slice(
        silu_cols.reshape(owners, seqs_here, ada_rows), (0, mine_seq, 0), (owners, 1, ada_rows)
    )[:, 0]
    partial_rows = jnp.dot(silu_group, ada_weight, precision=highest)
    partial_rows = exchanged(partial_rows, "fsdp", owners, mine_fsdp)
    modulation = jnp.sum(partial_rows, axis=0, keepdims=True) + ada_bias_full
    shift_attn, scale_attn, gate_attn, shift_mlp, scale_mlp, gate_mlp = jnp.split(modulation, 6, axis=1)
    vectors = [
        attn_gain_full,
        shift_attn,
        scale_attn,
        gate_attn,
        mlp_gain_full,
        shift_mlp,
        scale_mlp,
        gate_mlp,
        down_bias_full,
    ]
    vectors = jnp.concatenate(vectors + [jnp.zeros((VECTORS - len(vectors), width), f32)], axis=0)
    attn_full = gather(jnp.concatenate([qkv_weight, proj_weight], axis=1))
    up_full = gather(up_weight)
    down_full = gather(down_weight)
    cosine, sine = rotary_tables(places)

    qkv = mm_qkv(x, vectors, attn_full)
    cot_in, _ = lax.optimization_barrier((cotangent, x))
    cot = to_sequence(cot_in)
    attended, lse = attention_forward(length, qkv, cosine, sine)
    proj_out, middle, attn_sums = mm_proj(length, attended, x, vectors, attn_full)
    hidden_act, gelu_slope = mm_up(middle, vectors, up_full, up_bias_full)
    block_out, mlp_sums = mm_down(length, hidden_act, down_full, middle, cot, vectors)
    block_out = to_tokens(block_out)

    def scatter(grad):
        return lax.psum_scatter(grad, "fsdp", scatter_dimension=0, tiled=True)

    down_weight_grad, down_sums = dw_down(cot, vectors, hidden_act)
    down_shard = scatter(down_weight_grad)
    up_weight_grad, up_bias_grad, middle_grad, mlp_norm_sums = mlp_backward(
        cot, middle, proj_out, vectors, down_full, up_full, gelu_slope
    )
    attended_grad, up_proj_grad = proj_backward(middle_grad, attended, vectors, attn_full, up_weight_grad)
    up_shard = scatter(up_proj_grad)
    down_part = seq_partial(down_shard)
    down_total = seq_gather(down_part).reshape(down_shard.shape)
    up_proj_total = lax.psum(up_shard, "seq")
    gate_mlp_grad, down_bias_grad = mlp_sums[1], down_sums[0]
    shift_mlp_grad, scale_mlp_grad, mlp_gain_grad, gate_attn_grad = (mlp_norm_sums[i] for i in range(4))
    sums = jnp.stack(
        [
            jnp.sum(attn_sums[0]),
            jnp.sum(attn_sums[1]),
            jnp.sum(mlp_sums[0]),
            length[0].astype(f32),
        ]
    )
    pairs = width // PAIR
    back_args = (length, qkv, cosine, sine, attended, lse, attended_grad)
    qkv_grad = attention_backward(*back_args, 0, pairs // 2, None)
    qkv_grad = attention_backward(*back_args, pairs // 2, pairs, qkv_grad)
    tokens_grad, attn_norm_sums = mm_tokens_grad(qkv_grad, attn_full, x, middle_grad, vectors)
    shift_attn_grad, scale_attn_grad, attn_gain_grad = (attn_norm_sums[i] for i in range(3))
    tokens_grad = to_tokens(tokens_grad)
    qkv_weight_grad, up_proj_total = lax.optimization_barrier(
        (dw_qkv(x, vectors, qkv_grad), up_proj_total)
    )
    up_total, proj_total = up_proj_total[:, :hidden], up_proj_total[:, hidden:]
    qkv_shard = scatter(qkv_weight_grad)
    modulation_rows = [
        shift_attn_grad,
        scale_attn_grad,
        gate_attn_grad,
        shift_mlp_grad,
        scale_mlp_grad,
        gate_mlp_grad,
    ]
    vector_grads = [attn_gain_grad, mlp_gain_grad, up_bias_grad, down_bias_grad]
    late_all = gather(padded_row(modulation_rows + vector_grads + [sums]))
    modulation_grad = late_all[:, : 6 * width]
    group_sum = jnp.sum(late_all, axis=0, keepdims=True)
    ada_bias_sum, *vector_sums, sums_sum = cut(
        group_sum, [6 * width] + [piece.size for piece in vector_grads] + [sums.size]
    )

    def owned(total):
        size = total.shape[1] // owners
        return lax.dynamic_slice(total, (0, mine_fsdp * size), (1, size))

    time_cols = lax.dot_general(modulation_grad, ada_weight, (((1,), (1,)), ((), ())), precision=highest)
    time_cols = lax.all_gather(time_cols, "fsdp", axis=0)
    time_part = lax.dynamic_slice(time_cols, (0, mine_fsdp, 0), (owners, 1, ada_rows)).reshape(1, cond)
    time_part = jnp.where(jnp.arange(seqs_here)[:, None] == mine_seq, time_part, 0.0)
    ada_part = lax.dot_general(silu_group, modulation_grad, (((0,), (0,)), ((), ())), precision=highest)
    owned_sums = [owned(piece) for piece in [ada_bias_sum] + vector_sums]
    vector_part = padded_row(owned_sums + [sums_sum, time_part])
    qkv_total, ada_weight_grad, vector_total = lax.psum((qkv_shard, ada_part, vector_part), "seq")
    ada_bias_total, attn_gain_total, mlp_gain_total, up_bias_total, down_bias_total, sums_total, time_total = (
        piece[0]
        for piece in cut(vector_total, [piece.size for piece in owned_sums] + [sums.size, time_part.size])
    )
    _, silu_back = jax.vjp(jax.nn.silu, time_embed)
    (time_grad,) = silu_back(time_total.reshape(seqs_here, cond))
    rms = jnp.sqrt(sums_total[:3] / (sums_total[3] * width))
    return (
        block_out,
        tokens_grad,
        time_grad,
        ada_weight_grad,
        ada_bias_total,
        attn_gain_total,
        qkv_total,
        proj_total,
        mlp_gain_total,
        up_total,
        up_bias_total,
        down_total,
        down_bias_total,
        rms[0],
        rms[1],
        rms[2],
    )


def solution(mesh):
    field = P("fsdp", "seq", None)
    matrix = P("fsdp", None)
    vector = P("fsdp")

    return jax.shard_map(
        shards,
        mesh=mesh,
        in_specs=(
            field,
            matrix,
            vector,
            P("fsdp", "seq"),
            matrix,
            vector,
            vector,
            matrix,
            matrix,
            vector,
            matrix,
            vector,
            matrix,
            vector,
            field,
        ),
        out_specs=(
            field,
            field,
            matrix,
            matrix,
            vector,
            vector,
            matrix,
            matrix,
            vector,
            matrix,
            vector,
            matrix,
            vector,
            P(),
            P(),
            P(),
        ),
        check_vma=False,
    )
```

```python
from functools import partial

import jax
import jax.numpy as jnp
from jax import lax
from jax.experimental import pallas as pl
from jax.experimental.pallas import tpu as pltpu
from jax.sharding import PartitionSpec as P


HD = 64
PAIR = 2 * HD
LOG2E = 1.4426950408889634
LN2 = 0.6931471805599453


epsilon = 1e-05
highest = lax.Precision.HIGHEST
f32 = jnp.float32
bf16 = jnp.bfloat16


def gelu_and_slope(value):
    square = value * value
    t = jnp.tanh(0.7978845608028654 * (value + 0.044715 * value * square))
    slope = 0.5 * (1.0 + t) + 0.5 * value * (1.0 - t * t) * (
        0.7978845608028654 * (1.0 + 3 * 0.044715 * square)
    )
    return 0.5 * value * (1.0 + t), slope


def rotary_tables(positions):
    inverse = 1.0 / 10000.0 ** (jnp.arange(0, HD, 2, dtype=f32) / HD)
    angles = positions.astype(f32)[:, None] * inverse
    cosine, sine = jnp.cos(angles), jnp.sin(angles)
    return jnp.tile(cosine, (1, 4)), jnp.tile(sine, (1, 4))


def rotate(u, cosine, sine, lane):
    first = (lane % HD) < (HD // 2)
    turned = jnp.where(first, -pltpu.roll(u, PAIR - HD // 2, 1), pltpu.roll(u, HD // 2, 1))
    return u * cosine + turned * sine


def rotate_back(g, cosine, sine, lane):
    first = (lane % HD) < (HD // 2)
    w = g * sine
    return g * cosine + jnp.where(first, pltpu.roll(w, PAIR - HD // 2, 1), -pltpu.roll(w, HD // 2, 1))


def parts(u):
    hi = u.astype(bf16).astype(f32)
    return hi, (u - hi).astype(bf16).astype(f32)


def both(u, head, lane):
    turned = pltpu.roll(u, HD, 1)
    return jnp.where((lane < HD) == (head == 0), u, turned)


def beside(left, right, head, lane):
    low = left if head == 0 else pltpu.roll(left, HD, 1)
    high_lanes = pltpu.roll(right, HD, 1) if head == 0 else right
    return jnp.where(lane < HD, low, high_lanes)


def three_terms(column, lane):
    a = column.astype(bf16).astype(f32)
    b = (column - a).astype(bf16).astype(f32)
    c = column - a - b
    return jnp.where(lane == HD, a, jnp.where(lane == HD + 1, b, jnp.where(lane == HD + 2, c, 0.0)))


def split_bf16(u):
    hi = u.astype(bf16)
    return hi, (u - hi.astype(f32)).astype(bf16)


def dot_nt(a, b):
    return lax.dot_general(a, b, (((1,), (1,)), ((), ())), preferred_element_type=f32)


def dot_nn(a, b):
    return lax.dot_general(a, b, (((1,), (0,)), ((), ())), preferred_element_type=f32)


def forward_kernel(
    len_ref, q_ref, k_ref, v_ref, cos_ref, sin_ref, out_ref, lse_ref, qs, ks, vs, acc, *, rows
):
    full_len = q_ref.shape[0]
    lane = lax.broadcasted_iota(jnp.int32, (full_len, PAIR), 1)
    place = lax.broadcasted_iota(jnp.int32, (full_len, PAIR), 0)
    cosine, sine = cos_ref[...], sin_ref[...]
    q = rotate(q_ref[...], cosine, sine, lane) * (HD**-0.5 * LOG2E)
    k = rotate(k_ref[...], cosine, sine, lane)
    q_hi, q_lo = parts(q)
    k_hi, k_lo = parts(k)
    v_hi, v_lo = parts(v_ref[...])
    bias = jnp.where(place < len_ref[0], 0.0, -1e30)
    for head in range(2):
        qs[head, :, :PAIR] = both(q_hi, head, lane).astype(bf16)
        qs[head, :, PAIR:] = jnp.where(
            lane < HD, beside(q_lo, q_lo, head, lane), jnp.where(lane == HD, 1.0, 0.0)
        ).astype(bf16)
        ks[head, :, :PAIR] = beside(k_hi, k_lo, head, lane).astype(bf16)
        ks[head, :, PAIR:] = jnp.where(
            lane < HD, beside(k_hi, k_hi, head, lane), jnp.where(lane == HD, bias, 0.0)
        ).astype(bf16)
        vs[head] = beside(v_hi, v_lo, head, lane).astype(bf16)

    low = lax.broadcasted_iota(jnp.int32, (rows, PAIR), 1) < HD
    units = [(block, head) for block in range(full_len // rows) for head in range(2)]

    def scores_of(unit):
        block, head = unit
        return dot_nt(qs[head, pl.ds(block * rows, rows), :], ks[head])

    following = scores_of(units[0])
    outs, lses = [], []
    for place, (block, head) in enumerate(units):
        scores = following
        if place + 1 < len(units):
            following = scores_of(units[place + 1])
        largest = jnp.max(scores, axis=1, keepdims=True)
        expo = jnp.exp2(scores - largest)
        total = jnp.sum(expo, axis=1, keepdims=True)
        hi, lo = split_bf16(expo)
        both_parts = dot_nn(hi, vs[head]) + dot_nn(lo, vs[head])
        outs.append((both_parts + pltpu.roll(both_parts, HD, 1)) / total)
        lses.append(largest + jnp.log2(total))
        if head == 1:
            at = pl.ds(block * rows, rows)
            out_ref[at, :] = jnp.where(low, outs[-2], outs[-1])
            lse_ref[at, :] = jnp.where(low, lses[-2], lses[-1])


def backward_kernel(
    len_ref, q_ref, k_ref, v_ref, cos_ref, sin_ref, out_in_ref, lse_ref, do_ref, *rest, rows
):
    grad_ref, qs, ks, vs, dos, kd, qt, dot_t, dq, dkt, dvt = rest[-11:]
    full_len = q_ref.shape[0]
    which = pl.program_id(1)
    lane = lax.broadcasted_iota(jnp.int32, (full_len, PAIR), 1)

    @pl.when(which == 0)
    def _():
        place = lax.broadcasted_iota(jnp.int32, (full_len, PAIR), 0)
        cosine, sine = cos_ref[...], sin_ref[...]
        q = rotate(q_ref[...], cosine, sine, lane) * (HD**-0.5 * LOG2E)
        k = rotate(k_ref[...], cosine, sine, lane)
        out_grad = do_ref[...]
        q_hi, q_lo = parts(q)
        k_hi, k_lo = parts(k)
        v_hi, v_lo = parts(v_ref[...])
        g_hi, g_lo = parts(out_grad)
        product = out_grad * out_in_ref[...]
        lse = lse_ref[...]
        bias = jnp.where(place < len_ref[0], 0.0, -1e30)
        ones = jnp.where((lane >= HD) & (lane < HD + 3), 1.0, 0.0)
        for head in range(2):
            mine = (lane < HD) == (head == 0)
            delta = jnp.sum(jnp.where(mine, product, 0.0), axis=1, keepdims=True)
            lse_head = jnp.max(jnp.where(mine, lse, -3e38), axis=1, keepdims=True)
            qs[head, :, :PAIR] = both(q_hi, head, lane).astype(bf16)
            qs[head, :, PAIR:] = jnp.where(
                lane < HD,
                beside(q_lo, q_lo, head, lane),
                three_terms(-lse_head, lane) + jnp.where(lane == HD + 3, 1.0, 0.0),
            ).astype(bf16)
            ks[head, :, :PAIR] = beside(k_hi, k_lo, head, lane).astype(bf16)
            ks[head, :, PAIR:] = jnp.where(
                lane < HD, beside(k_hi, k_hi, head, lane), ones + jnp.where(lane == HD + 3, bias, 0.0)
            ).astype(bf16)
            dos[head, :, :PAIR] = both(g_hi, head, lane).astype(bf16)
            dos[head, :, PAIR:] = jnp.where(
                lane < HD, beside(g_lo, g_lo, head, lane), three_terms(-delta, lane)
            ).astype(bf16)
            vs[head, :, :PAIR] = beside(v_hi, v_lo, head, lane).astype(bf16)
            vs[head, :, PAIR:] = jnp.where(lane < HD, beside(v_hi, v_hi, head, lane), ones).astype(bf16)
            kd[head] = beside(k_hi, k_lo, head, lane).astype(bf16)
            qt[head] = beside(q_hi, q_lo, head, lane).T.astype(bf16)
            dot_t[head] = beside(g_hi, g_lo, head, lane).T.astype(bf16)
        dkt[...] = jnp.zeros_like(dkt)
        dvt[...] = jnp.zeros_like(dvt)
        low = lax.broadcasted_iota(jnp.int32, (rows, PAIR), 1) < HD

        units = [(block, head) for block in range(full_len // rows) for head in range(2)]

        def products_of(unit):
            block, head = unit
            at = pl.ds(block * rows, rows)
            return dot_nt(qs[head, at, :], ks[head]), dot_nt(dos[head, at, :], vs[head])

        following = products_of(units[0])
        outs = []
        for order, (block, head) in enumerate(units):
            scores, weight_grad = following
            if order + 1 < len(units):
                following = products_of(units[order + 1])
            at = pl.ds(block * rows, rows)
            weights = jnp.exp2(scores)
            score_grad = weights * weight_grad
            w_hi, w_lo = split_bf16(weights)
            s_hi, s_lo = split_bf16(score_grad)
            both_parts = dot_nn(s_hi, kd[head]) + dot_nn(s_lo, kd[head])
            outs.append(both_parts + pltpu.roll(both_parts, HD, 1))
            q_t = qt[head, :, at]
            g_t = dot_t[head, :, at]
            dkt[head] += dot_nn(q_t, s_hi) + dot_nn(q_t, s_lo)
            dvt[head] += dot_nn(g_t, w_hi) + dot_nn(g_t, w_lo)
            if head == 1:
                dq[at, :] = jnp.where(low, outs[-2], outs[-1])
        grad_ref[...] = rotate_back(dq[...] * HD**-0.5, cosine, sine, lane)

    @pl.when(which == 1)
    def _():
        stacked = jnp.concatenate([dkt[h, :HD, :] + dkt[h, HD:, :] for h in range(2)], axis=0)
        grad_ref[...] = rotate_back(stacked.T * LN2, cos_ref[...], sin_ref[...], lane)

    @pl.when(which == 2)
    def _():
        stacked = jnp.concatenate([dvt[h, :HD, :] + dvt[h, HD:, :] for h in range(2)], axis=0)
        grad_ref[...] = stacked.T


def attention_forward(length, qkv, cosine, sine):
    full_len, three = qkv.shape
    width = three // 3
    pairs = width // PAIR
    rows = min(256, full_len)

    def column(offset):
        return pl.BlockSpec((full_len, PAIR), lambda p, ln: (0, p + offset))

    table = pl.BlockSpec((full_len, PAIR), lambda p, ln: (0, 0))
    wide = jax.ShapeDtypeStruct((full_len, width), f32)
    return pl.pallas_call(
        partial(forward_kernel, rows=rows),
        name="attention_forward",
        out_shape=(wide, wide),
        grid_spec=pltpu.PrefetchScalarGridSpec(
            num_scalar_prefetch=1,
            grid=(pairs,),
            in_specs=[column(0), column(pairs), column(2 * pairs), table, table],
            out_specs=(column(0), column(0)),
            scratch_shapes=[
                pltpu.VMEM((2, full_len, 2 * PAIR), bf16),
                pltpu.VMEM((2, full_len, 2 * PAIR), bf16),
                pltpu.VMEM((2, full_len, PAIR), bf16),
                pltpu.VMEM((8, 128), f32),
            ],
        ),
        cost_estimate=pl.CostEstimate(
            flops=24 * full_len * full_len * width, bytes_accessed=20 * full_len * width, transcendentals=0
        ),
    )(length, qkv, qkv, qkv, cosine, sine)


def attention_backward(length, qkv, cosine, sine, attended, lse, out_grad, first, last, joined):
    full_len, three = qkv.shape
    width = three // 3
    pairs = width // PAIR
    rows = min(256, full_len)

    def column(offset):
        return pl.BlockSpec((full_len, PAIR), lambda p, c, ln: (0, first + p + offset))

    table = pl.BlockSpec((full_len, PAIR), lambda p, c, ln: (0, 0))
    stacked = pltpu.VMEM((2, full_len, 2 * PAIR), bf16)
    turned = pltpu.VMEM((2, PAIR, full_len), bf16)
    summed = pltpu.VMEM((2, PAIR, full_len), f32)
    args = [length, qkv, qkv, qkv, cosine, sine, attended, lse, out_grad]
    in_specs = [
        column(0),
        column(pairs),
        column(2 * pairs),
        table,
        table,
        column(0),
        column(0),
        column(0),
    ]
    if joined is not None:
        args.append(joined)
        in_specs.append(pl.BlockSpec(memory_space=pl.ANY))
    share = (last - first) * full_len * PAIR
    return pl.pallas_call(
        partial(backward_kernel, rows=rows),
        out_shape=jax.ShapeDtypeStruct((full_len, three), f32),
        grid_spec=pltpu.PrefetchScalarGridSpec(
            num_scalar_prefetch=1,
            grid=(last - first, 3),
            in_specs=in_specs,
            out_specs=pl.BlockSpec((full_len, PAIR), lambda p, c, ln: (0, c * pairs + first + p)),
            scratch_shapes=[
                stacked,
                stacked,
                stacked,
                stacked,
                pltpu.VMEM((2, full_len, PAIR), bf16),
                turned,
                turned,
                pltpu.VMEM((full_len, PAIR), f32),
                summed,
                summed,
            ],
        ),
        input_output_aliases={} if joined is None else {len(args) - 1: 0},
        cost_estimate=pl.CostEstimate(
            flops=60 * full_len * share, bytes_accessed=32 * share, transcendentals=0
        ),
    )(*args)


ATTN_GAIN, ATTN_SHIFT, ATTN_SCALE, ATTN_GATE, MLP_GAIN, MLP_SHIFT, MLP_SCALE, MLP_GATE, DOWN_BIAS = range(9)
VECTORS = 16
COLUMNS = 256


def put_left(ref, u, axis):
    hi, lo = split_bf16(u)
    size = u.shape[axis]
    for place, part in enumerate((hi, lo, hi)):
        if axis == 1:
            ref[:, place * size : (place + 1) * size] = part
        else:
            ref[place * size : (place + 1) * size, :] = part


def put_right(ref, u, axis):
    hi, lo = split_bf16(u)
    size = u.shape[axis]
    for place, part in enumerate((hi, hi, lo)):
        if axis == 1:
            ref[:, place * size : (place + 1) * size] = part
        else:
            ref[place * size : (place + 1) * size, :] = part


def normalized(v):
    average = jnp.mean(v, axis=-1, keepdims=True)
    centered = v - average
    rstd = lax.rsqrt(jnp.mean(centered * centered, axis=-1, keepdims=True) + epsilon)
    return centered * rstd, rstd


def modulated(v, vec_ref, gain, shift, scale):
    xhat, _ = normalized(v)
    return xhat * row(vec_ref, gain) * (1.0 + row(vec_ref, scale)) + row(vec_ref, shift)


def row(ref, index):
    return ref[index : index + 1, :]


def column_sum(u):
    return jnp.sum(u, axis=0, keepdims=True)


def norm_backward(e_ref, v_ref, extra_ref, vec_ref, gain, scale, out_ref, sums_ref, other_ref):
    full_len = v_ref.shape[0]
    rows = min(128, full_len)
    factor = (1.0 + row(vec_ref, scale)) * row(vec_ref, gain)

    def step(block, carry):
        at = pl.ds(pl.multiple_of(block * rows, rows), rows)
        e = e_ref[at, :]
        xhat, rstd = normalized(v_ref[at, :])
        f = e * factor
        grad = rstd * (
            f
            - jnp.mean(f, axis=-1, keepdims=True)
            - xhat * jnp.mean(f * xhat, axis=-1, keepdims=True)
        )
        out = extra_ref[at, :] + grad
        out_ref[at, :] = out
        new = [column_sum(e), column_sum(e * xhat)]
        if other_ref is not None:
            new.append(column_sum(out * other_ref[at, :]))
        return tuple(c + n for c, n in zip(carry, new))

    zero = jnp.zeros((1, v_ref.shape[1]), f32)
    count = 2 if other_ref is None else 3
    total = lax.fori_loop(0, full_len // rows, step, (zero,) * count)
    sums_ref[...] = jnp.zeros_like(sums_ref)
    sums_ref[0:1, :] = total[0]
    sums_ref[1:2, :] = total[1] * row(vec_ref, gain)
    sums_ref[2:3, :] = total[1] * (1.0 + row(vec_ref, scale))
    if other_ref is not None:
        sums_ref[3:4, :] = total[2]


def qkv_kernel(x_ref, vec_ref, w_ref, out_ref, left, right):
    @pl.when(pl.program_id(0) == 0)
    def _():
        put_left(left, modulated(x_ref[...], vec_ref, ATTN_GAIN, ATTN_SHIFT, ATTN_SCALE), 1)

    put_right(right, w_ref[...], 0)
    out_ref[...] = dot_nn(left[...], right[...])


def proj_kernel(
    len_ref, att_ref, x_ref, vec_ref, w_ref, proj_ref, middle_ref, sums_ref, left, right
):
    @pl.when(pl.program_id(0) == 0)
    def _():
        put_left(left, att_ref[...], 1)

    put_right(right, w_ref[...], 0)
    proj = dot_nn(left[...], right[...])
    x = x_ref[...]
    branch = row(vec_ref, ATTN_GATE) * proj
    proj_ref[...] = proj
    middle_ref[...] = x + branch
    valid = lax.broadcasted_iota(jnp.int32, x.shape, 0) < len_ref[0]
    sums_ref[...] = jnp.zeros_like(sums_ref)
    sums_ref[0:1, :] = column_sum(jnp.where(valid, x * x, 0.0))
    sums_ref[1:2, :] = column_sum(jnp.where(valid, branch * branch, 0.0))


def up_kernel(middle_ref, vec_ref, up_ref, bias_ref, act_ref, slope_ref, left, right, *, rows):
    @pl.when(pl.program_id(0) == 0)
    def _():
        put_left(left, modulated(middle_ref[...], vec_ref, MLP_GAIN, MLP_SHIFT, MLP_SCALE), 1)

    put_right(right, up_ref[...], 0)
    for block in range(middle_ref.shape[0] // rows):
        at = pl.ds(block * rows, rows)
        pre = dot_nn(left[at, :], right[...]) + bias_ref[...]
        act_ref[at, :], slope_ref[at, :] = gelu_and_slope(pre)


def down_kernel(
    len_ref, act_ref, down_ref, middle_ref, cot_ref, vec_ref, out_ref, sums_ref, left, right, acc
):
    step = pl.program_id(0)

    @pl.when(step == 0)
    def _():
        acc[...] = jnp.zeros_like(acc)

    put_left(left, act_ref[...], 1)
    put_right(right, down_ref[...], 0)
    acc[...] += dot_nn(left[...], right[...])

    @pl.when(step == pl.num_programs(0) - 1)
    def _():
        down_out = acc[...] + row(vec_ref, DOWN_BIAS)
        branch = row(vec_ref, MLP_GATE) * down_out
        out_ref[...] = middle_ref[...] + branch
        valid = lax.broadcasted_iota(jnp.int32, branch.shape, 0) < len_ref[0]
        sums_ref[...] = jnp.zeros_like(sums_ref)
        sums_ref[0:1, :] = column_sum(jnp.where(valid, branch * branch, 0.0))
        sums_ref[1:2, :] = column_sum(cot_ref[...] * down_out)


def down_grad_kernel(cot_ref, vec_ref, act_ref, grad_ref, sums_ref, left, right):
    @pl.when(pl.program_id(0) == 0)
    def _():
        grad = cot_ref[...] * row(vec_ref, MLP_GATE)
        put_left(left, grad.T, 1)
        sums_ref[...] = jnp.zeros_like(sums_ref)
        sums_ref[0:1, :] = column_sum(grad)

    put_right(right, act_ref[...], 0)
    chunk = COLUMNS
    count = left.shape[0] // chunk
    following = dot_nn(left[:chunk, :], right[...])
    for part in range(count):
        turned = following
        if part + 1 < count:
            following = dot_nn(left[(part + 1) * chunk : (part + 2) * chunk, :], right[...])
        grad_ref[:, part * chunk : (part + 1) * chunk] = turned.T


def mlp_backward_kernel(
    cot_ref,
    middle_ref,
    proj_ref,
    vec_ref,
    down_ref,
    up_ref,
    slope_ref,
    up_grad_ref,
    bias_grad_ref,
    middle_grad_ref,
    sums_ref,
    left,
    turned,
    down_cat,
    up_cat,
    pre_cat,
    pre_stack,
    acc,
    *,
    rows,
):
    step = pl.program_id(0)
    full_len = middle_ref.shape[0]

    @pl.when(step == 0)
    def _():
        put_left(left, cot_ref[...] * row(vec_ref, MLP_GATE), 1)
        normed = modulated(middle_ref[...], vec_ref, MLP_GAIN, MLP_SHIFT, MLP_SCALE)
        put_left(turned, normed.T, 1)
        acc[...] = jnp.zeros_like(acc)

    put_right(down_cat, down_ref[...], 1)
    put_right(up_cat, up_ref[...], 1)
    bias_grad = jnp.zeros_like(bias_grad_ref)
    blocks = [pl.ds(block * rows, rows) for block in range(full_len // rows)]

    def add_to_acc(at):
        acc[at, :] += dot_nt(pre_cat[at, :], up_cat[...])

    following = dot_nt(left[blocks[0], :], down_cat[...])
    for block, at in enumerate(blocks):
        act_grad = following
        if block + 1 < len(blocks):
            following = dot_nt(left[blocks[block + 1], :], down_cat[...])
        if block > 0:
            add_to_acc(blocks[block - 1])
        pre_grad = act_grad * slope_ref[at, :]
        bias_grad += column_sum(pre_grad)
        hi, lo = split_bf16(pre_grad)
        columns = hi.shape[1]
        for place, part in enumerate((hi, lo, hi)):
            pre_cat[at, place * columns : (place + 1) * columns] = part
        for place, part in enumerate((hi, hi, lo)):
            pre_stack[pl.ds(place * full_len + block * rows, rows), :] = part
    add_to_acc(blocks[-1])
    bias_grad_ref[...] = bias_grad
    up_grad_ref[...] = dot_nn(turned[...], pre_stack[...])

    @pl.when(step == pl.num_programs(0) - 1)
    def _():
        norm_backward(
            acc, middle_ref, cot_ref, vec_ref, MLP_GAIN, MLP_SCALE, middle_grad_ref, sums_ref, proj_ref
        )


def proj_backward_kernel(
    grad_ref, grad_block_ref, att_ref, vec_ref, vec_block_ref, w_ref, out_ref, w_grad_ref,
    left, turned, w_cat, stack,
):
    @pl.when(pl.program_id(0) == 0)
    def _():
        put_left(left, grad_ref[...] * row(vec_ref, ATTN_GATE), 1)
        put_left(turned, att_ref[...].T, 1)

    put_right(w_cat, w_ref[...], 1)
    out_ref[...] = dot_nt(left[...], w_cat[...])
    put_right(stack, grad_block_ref[...] * row(vec_block_ref, ATTN_GATE), 0)
    w_grad_ref[...] = dot_nn(turned[...], stack[...])


def tokens_grad_kernel(
    grad_ref, w_ref, x_ref, extra_ref, vec_ref, out_ref, sums_ref, left, w_cat, acc
):
    step = pl.program_id(0)

    @pl.when(step == 0)
    def _():
        acc[...] = jnp.zeros_like(acc)

    put_left(left, grad_ref[...], 1)
    put_right(w_cat, w_ref[...], 1)
    acc[...] += dot_nt(left[...], w_cat[...])

    @pl.when(step == pl.num_programs(0) - 1)
    def _():
        norm_backward(acc, x_ref, extra_ref, vec_ref, ATTN_GAIN, ATTN_SCALE, out_ref, sums_ref, None)


def qkv_grad_kernel(x_ref, vec_ref, grad_ref, joined_ref, out_ref, turned, stack):
    del joined_ref

    @pl.when(pl.program_id(0) == 0)
    def _():
        normed = modulated(x_ref[...], vec_ref, ATTN_GAIN, ATTN_SHIFT, ATTN_SCALE)
        put_left(turned, normed.T, 1)

    put_right(stack, grad_ref[...], 0)
    out_ref[...] = dot_nn(turned[...], stack[...])


def whole(shape):
    return pl.BlockSpec(shape, lambda *ids: (0,) * len(shape), pipeline_mode=pl.Buffered(1))


def by_columns(rows, columns, first=0):
    return pl.BlockSpec((rows, columns), lambda j, *refs: (0, first + j))


def by_rows(rows, columns, column=0):
    return pl.BlockSpec((rows, columns), lambda j, *refs: (j, column))


def dense(body, grid, in_specs, out_specs, out_shapes, scratch, products, args, scalars=0, aliases=None):
    moved = sum(a.size for a in args) + sum(o.size for o in out_shapes)
    return pl.pallas_call(
        body,
        out_shape=tuple(out_shapes),
        grid_spec=pltpu.PrefetchScalarGridSpec(
            num_scalar_prefetch=scalars,
            grid=(grid,),
            in_specs=in_specs,
            out_specs=tuple(out_specs),
            scratch_shapes=[pltpu.VMEM(shape, kind) for shape, kind in scratch],
        ),
        input_output_aliases=aliases or {},
        compiler_params=pltpu.CompilerParams(vmem_limit_bytes=60 << 20),
        cost_estimate=pl.CostEstimate(flops=6 * products, bytes_accessed=4 * moved, transcendentals=0),
    )(*args)


def array(*shape):
    return jax.ShapeDtypeStruct(shape, f32)


def mm_qkv(x, vectors, weight):
    t, d = x.shape
    n = 3 * d
    c = COLUMNS
    return dense(
        qkv_kernel,
        n // c,
        [whole((t, d)), whole((VECTORS, d)), by_columns(d, c)],
        [by_columns(t, c)],
        [array(t, n)],
        [((t, 3 * d), bf16), ((3 * d, c), bf16)],
        t * d * n,
        (x, vectors, weight),
    )[0]


def mm_proj(length, attended, x, vectors, weight):
    t, d = x.shape
    c = COLUMNS
    return dense(
        proj_kernel,
        d // c,
        [whole((t, d)), by_columns(t, c), by_columns(VECTORS, c), by_columns(d, c, 3 * d // c)],
        [by_columns(t, c), by_columns(t, c), by_columns(8, c)],
        [array(t, d), array(t, d), array(8, d)],
        [((t, 3 * d), bf16), ((3 * d, c), bf16)],
        t * d * d,
        (length, attended, x, vectors, weight),
        scalars=1,
    )


def mm_up(middle, vectors, up, up_bias):
    t, d = middle.shape
    n = up.shape[1]
    c = COLUMNS
    return dense(
        partial(up_kernel, rows=min(256, t)),
        n // c,
        [whole((t, d)), whole((VECTORS, d)), by_columns(d, c), by_columns(1, c)],
        [by_columns(t, c), by_columns(t, c)],
        [array(t, n), array(t, n)],
        [((t, 3 * d), bf16), ((3 * d, c), bf16)],
        t * d * n,
        (middle, vectors, up, up_bias),
    )


def mm_down(length, act, down, middle, cot, vectors):
    t, n = act.shape
    d = down.shape[1]
    c = 2 * COLUMNS
    return dense(
        down_kernel,
        n // c,
        [by_columns(t, c), by_rows(c, d), whole((t, d)), whole((t, d)), whole((VECTORS, d))],
        [whole((t, d)), whole((8, d))],
        [array(t, d), array(8, d)],
        [((t, 3 * c), bf16), ((3 * c, d), bf16), ((t, d), f32)],
        t * d * n,
        (length, act, down, middle, cot, vectors),
        scalars=1,
    )


def dw_down(cot, vectors, act):
    t, d = cot.shape
    n = act.shape[1]
    c = 2 * COLUMNS
    return dense(
        down_grad_kernel,
        n // c,
        [whole((t, d)), whole((VECTORS, d)), by_columns(t, c)],
        [by_rows(c, d), whole((8, d))],
        [array(n, d), array(8, d)],
        [((d, 3 * t), bf16), ((3 * t, c), bf16)],
        t * d * n,
        (cot, vectors, act),
    )


def mlp_backward(cot, middle, proj_out, vectors, down, up, slope):
    t, d = cot.shape
    n = up.shape[1]
    c = COLUMNS
    return dense(
        partial(mlp_backward_kernel, rows=min(256, t)),
        n // c,
        [
            whole((t, d)),
            whole((t, d)),
            whole((t, d)),
            whole((VECTORS, d)),
            by_rows(c, d),
            by_columns(d, c),
            by_columns(t, c),
        ],
        [by_columns(d, c), by_columns(1, c), whole((t, d)), whole((8, d))],
        [array(d, n), array(1, n), array(t, d), array(8, d)],
        [
            ((t, 3 * d), bf16),
            ((d, 3 * t), bf16),
            ((c, 3 * d), bf16),
            ((d, 3 * c), bf16),
            ((t, 3 * c), bf16),
            ((3 * t, c), bf16),
            ((t, d), f32),
        ],
        3 * t * d * n,
        (cot, middle, proj_out, vectors, down, up, slope),
    )


def proj_backward(middle_grad, attended, vectors, weight):
    t, d = middle_grad.shape
    c = COLUMNS
    return dense(
        proj_backward_kernel,
        d // c,
        [
            whole((t, d)),
            by_columns(t, c),
            whole((t, d)),
            whole((VECTORS, d)),
            by_columns(VECTORS, c),
            by_rows(c, d, 3),
        ],
        [by_columns(t, c), by_columns(d, c, 3 * d // c)],
        [array(t, d), array(d, 4 * d)],
        [((t, 3 * d), bf16), ((d, 3 * t), bf16), ((c, 3 * d), bf16), ((3 * t, c), bf16)],
        2 * t * d * d,
        (middle_grad, middle_grad, attended, vectors, vectors, weight),
    )


def mm_tokens_grad(qkv_grad, weight, x, middle_grad, vectors):
    t, d = x.shape
    n = 3 * d
    c = COLUMNS
    return dense(
        tokens_grad_kernel,
        n // c,
        [by_columns(t, c), by_columns(d, c), whole((t, d)), whole((t, d)), whole((VECTORS, d))],
        [whole((t, d)), whole((8, d))],
        [array(t, d), array(8, d)],
        [((t, 3 * c), bf16), ((d, 3 * c), bf16), ((t, d), f32)],
        t * d * n,
        (qkv_grad, weight, x, middle_grad, vectors),
    )


def dw_qkv(x, vectors, qkv_grad, joined):
    t, d = x.shape
    n = qkv_grad.shape[1]
    c = COLUMNS
    return dense(
        qkv_grad_kernel,
        n // c,
        [
            whole((t, d)),
            whole((VECTORS, d)),
            by_columns(t, c),
            pl.BlockSpec(memory_space=pl.ANY),
        ],
        [by_columns(d, c)],
        [array(*joined.shape)],
        [((d, 3 * t), bf16), ((3 * t, c), bf16)],
        t * d * n,
        (x, vectors, qkv_grad, joined),
        aliases={3: 0},
    )[0]


def padded_row(pieces):
    row = jnp.concatenate([piece.reshape(-1) for piece in pieces])
    return jnp.pad(row, (0, -row.shape[0] % 128))[None, :]


def cut(row, sizes):
    out, start = [], 0
    for size in sizes:
        out.append(row[:, start : start + size])
        start += size
    return out


def shards(
    tokens,
    time_embed,
    lengths,
    positions,
    ada_weight,
    ada_bias,
    attn_gain,
    qkv_weight,
    proj_weight,
    mlp_gain,
    up_weight,
    up_bias,
    down_weight,
    down_bias,
    cotangent,
):
    groups = lax.axis_size("seq")
    owners = lax.axis_size("fsdp")
    mine_seq = lax.axis_index("seq")
    mine_fsdp = lax.axis_index("fsdp")
    seqs_here, local_len, width = tokens.shape
    cond = time_embed.shape[1]
    full_len = local_len * groups
    assert seqs_here == groups

    def to_sequence(field):
        return lax.all_to_all(field, "seq", split_axis=0, concat_axis=1, tiled=True)[0]

    def to_tokens(field):
        pieces = field.reshape(groups, local_len, width)
        return lax.all_to_all(pieces, "seq", split_axis=0, concat_axis=0, tiled=True)

    def gather(shard):
        return lax.all_gather(shard, "fsdp", axis=0, tiled=True)

    def exchanged(rows, axis, count, mine):
        if count > 8:
            all_rows = lax.all_gather(rows, axis, axis=0)
            return lax.dynamic_slice(all_rows, (0, mine, 0), (count, 1, rows.shape[1]))[:, 0]
        out = jnp.zeros_like(rows)
        for shift in range(count):
            target = (mine + shift) % count
            sent = lax.dynamic_slice(rows, (target, 0), (1, rows.shape[1]))
            if shift > 0:
                sent = lax.ppermute(sent, axis, [(i, (i + shift) % count) for i in range(count)])
            out = lax.dynamic_update_slice(out, sent, ((mine - shift) % count, 0))
        return out

    def seq_shift(piece, shift):
        return lax.ppermute(piece, "seq", [(i, (i + shift) % groups) for i in range(groups)])

    def seq_gather(piece):
        pieces = jnp.stack([piece] + [seq_shift(piece, shift) for shift in range(1, groups)])
        order = [(mine_seq - place) % groups for place in range(groups)]
        return jnp.concatenate([lax.dynamic_slice_in_dim(pieces, at, 1, 0) for at in order], axis=0)

    def seq_partial(shard):
        pieces = shard.reshape((groups, -1) + shard.shape[1:])
        total = lax.dynamic_slice_in_dim(pieces, mine_seq, 1, 0)[0]
        for shift in range(1, groups):
            sent = lax.dynamic_slice_in_dim(pieces, (mine_seq + shift) % groups, 1, 0)[0]
            total = total + seq_shift(sent, shift)
        return total

    x = to_sequence(tokens)
    places = exchanged(positions, "seq", groups, mine_seq).reshape(full_len)
    length = lax.dynamic_slice(lengths, (mine_seq,), (1,))
    small = [time_embed, ada_bias, attn_gain, mlp_gain, up_bias, down_bias]
    small_sizes = [piece.size for piece in small]
    packed = gather(padded_row(small))
    time_all, ada_bias_full, attn_gain_full, mlp_gain_full, up_bias_full, down_bias_full = cut(
        packed, small_sizes
    )
    time_all = time_all.reshape(owners * seqs_here, cond)
    ada_bias_full, attn_gain_full, mlp_gain_full, up_bias_full, down_bias_full = (
        piece.reshape(1, -1)
        for piece in (ada_bias_full, attn_gain_full, mlp_gain_full, up_bias_full, down_bias_full)
    )
    silu_all = jax.nn.silu(time_all)
    ada_rows = ada_weight.shape[0]
    silu_cols = lax.dynamic_slice(silu_all, (0, mine_fsdp * ada_rows), (owners * seqs_here, ada_rows))
    silu_group = lax.dynamic_slice(
        silu_cols.reshape(owners, seqs_here, ada_rows), (0, mine_seq, 0), (owners, 1, ada_rows)
    )[:, 0]
    partial_rows = jnp.dot(silu_group, ada_weight, precision=highest)
    partial_rows = exchanged(partial_rows, "fsdp", owners, mine_fsdp)
    modulation = jnp.sum(partial_rows, axis=0, keepdims=True) + ada_bias_full
    shift_attn, scale_attn, gate_attn, shift_mlp, scale_mlp, gate_mlp = jnp.split(modulation, 6, axis=1)
    vectors = [
        attn_gain_full,
        shift_attn,
        scale_attn,
        gate_attn,
        mlp_gain_full,
        shift_mlp,
        scale_mlp,
        gate_mlp,
        down_bias_full,
    ]
    vectors = jnp.concatenate(vectors + [jnp.zeros((VECTORS - len(vectors), width), f32)], axis=0)
    attn_full = gather(jnp.concatenate([qkv_weight, proj_weight], axis=1))
    up_full = gather(up_weight)
    down_full = gather(down_weight)
    cosine, sine = rotary_tables(places)

    qkv = mm_qkv(x, vectors, attn_full)
    cot_in, _ = lax.optimization_barrier((cotangent, x))
    cot = to_sequence(cot_in)
    attended, lse = attention_forward(length, qkv, cosine, sine)
    proj_out, middle, attn_sums = mm_proj(length, attended, x, vectors, attn_full)
    hidden_act, gelu_slope = mm_up(middle, vectors, up_full, up_bias_full)
    down_weight_grad, down_sums = dw_down(cot, vectors, hidden_act)
    block_out, mlp_sums = mm_down(length, hidden_act, down_full, middle, cot, vectors)
    block_out = to_tokens(block_out)

    def scatter(grad):
        return lax.psum_scatter(grad, "fsdp", scatter_dimension=0, tiled=True)

    down_shard = scatter(down_weight_grad)
    up_weight_grad, up_bias_grad, middle_grad, mlp_norm_sums = mlp_backward(
        cot, middle, proj_out, vectors, down_full, up_full, gelu_slope
    )
    up_shard = scatter(up_weight_grad)
    up_total = lax.psum(up_shard, "seq")
    attended_grad, joined_grad = proj_backward(middle_grad, attended, vectors, attn_full)
    down_part = seq_partial(down_shard)
    down_total = seq_gather(down_part).reshape(down_shard.shape)
    gate_mlp_grad, down_bias_grad = mlp_sums[1], down_sums[0]
    shift_mlp_grad, scale_mlp_grad, mlp_gain_grad, gate_attn_grad = (mlp_norm_sums[i] for i in range(4))
    sums = jnp.stack(
        [
            jnp.sum(attn_sums[0]),
            jnp.sum(attn_sums[1]),
            jnp.sum(mlp_sums[0]),
            length[0].astype(f32),
        ]
    )
    pairs = width // PAIR
    back_args = (length, qkv, cosine, sine, attended, lse, attended_grad)
    qkv_grad = None
    for part in range(3):
        first, last = pairs * part // 3, pairs * (part + 1) // 3
        qkv_grad = attention_backward(*back_args, first, last, qkv_grad)
    tokens_grad, attn_norm_sums = mm_tokens_grad(qkv_grad, attn_full, x, middle_grad, vectors)
    shift_attn_grad, scale_attn_grad, attn_gain_grad = (attn_norm_sums[i] for i in range(3))
    tokens_grad = to_tokens(tokens_grad)
    joined_grad, up_total = lax.optimization_barrier(
        (dw_qkv(x, vectors, qkv_grad, joined_grad), up_total)
    )
    attn_shard = scatter(joined_grad)
    modulation_rows = [
        shift_attn_grad,
        scale_attn_grad,
        gate_attn_grad,
        shift_mlp_grad,
        scale_mlp_grad,
        gate_mlp_grad,
    ]
    vector_grads = [attn_gain_grad, mlp_gain_grad, up_bias_grad, down_bias_grad]
    late_all = gather(padded_row(modulation_rows + vector_grads + [sums]))
    modulation_grad = late_all[:, : 6 * width]
    group_sum = jnp.sum(late_all, axis=0, keepdims=True)
    ada_bias_sum, *vector_sums, sums_sum = cut(
        group_sum, [6 * width] + [piece.size for piece in vector_grads] + [sums.size]
    )

    def owned(total):
        size = total.shape[1] // owners
        return lax.dynamic_slice(total, (0, mine_fsdp * size), (1, size))

    time_cols = lax.dot_general(modulation_grad, ada_weight, (((1,), (1,)), ((), ())), precision=highest)
    time_cols = lax.all_gather(time_cols, "fsdp", axis=0)
    time_part = lax.dynamic_slice(time_cols, (0, mine_fsdp, 0), (owners, 1, ada_rows)).reshape(1, cond)
    time_part = jnp.where(jnp.arange(seqs_here)[:, None] == mine_seq, time_part, 0.0)
    ada_part = lax.dot_general(silu_group, modulation_grad, (((0,), (0,)), ((), ())), precision=highest)
    owned_sums = [owned(piece) for piece in [ada_bias_sum] + vector_sums]
    vector_part = padded_row(owned_sums + [sums_sum, time_part])
    attn_total, ada_weight_grad, vector_total = lax.psum((attn_shard, ada_part, vector_part), "seq")
    qkv_total, proj_total = attn_total[:, : 3 * width], attn_total[:, 3 * width :]
    ada_bias_total, attn_gain_total, mlp_gain_total, up_bias_total, down_bias_total, sums_total, time_total = (
        piece[0]
        for piece in cut(vector_total, [piece.size for piece in owned_sums] + [sums.size, time_part.size])
    )
    _, silu_back = jax.vjp(jax.nn.silu, time_embed)
    (time_grad,) = silu_back(time_total.reshape(seqs_here, cond))
    rms = jnp.sqrt(sums_total[:3] / (sums_total[3] * width))
    return (
        block_out,
        tokens_grad,
        time_grad,
        ada_weight_grad,
        ada_bias_total,
        attn_gain_total,
        qkv_total,
        proj_total,
        mlp_gain_total,
        up_total,
        up_bias_total,
        down_total,
        down_bias_total,
        rms[0],
        rms[1],
        rms[2],
    )


def solution(mesh):
    field = P("fsdp", "seq", None)
    matrix = P("fsdp", None)
    vector = P("fsdp")

    return jax.shard_map(
        shards,
        mesh=mesh,
        in_specs=(
            field,
            matrix,
            vector,
            P("fsdp", "seq"),
            matrix,
            vector,
            vector,
            matrix,
            matrix,
            vector,
            matrix,
            vector,
            matrix,
            vector,
            field,
        ),
        out_specs=(
            field,
            field,
            matrix,
            matrix,
            vector,
            vector,
            matrix,
            matrix,
            vector,
            matrix,
            vector,
            matrix,
            vector,
            P(),
            P(),
            P(),
        ),
        check_vma=False,
    )
```

```python
from functools import partial

import jax
import jax.numpy as jnp
from jax import lax
from jax.experimental import pallas as pl
from jax.experimental.pallas import tpu as pltpu
from jax.sharding import PartitionSpec as P


HD = 64
PAIR = 2 * HD
LOG2E = 1.4426950408889634
LN2 = 0.6931471805599453


epsilon = 1e-05
highest = lax.Precision.HIGHEST
f32 = jnp.float32
bf16 = jnp.bfloat16


def gelu_and_slope(value):
    square = value * value
    t = jnp.tanh(0.7978845608028654 * (value + 0.044715 * value * square))
    slope = 0.5 * (1.0 + t) + 0.5 * value * (1.0 - t * t) * (
        0.7978845608028654 * (1.0 + 3 * 0.044715 * square)
    )
    return 0.5 * value * (1.0 + t), slope


def rotary_tables(positions):
    inverse = 1.0 / 10000.0 ** (jnp.arange(0, HD, 2, dtype=f32) / HD)
    angles = positions.astype(f32)[:, None] * inverse
    cosine, sine = jnp.cos(angles), jnp.sin(angles)
    return jnp.tile(cosine, (1, 4)), jnp.tile(sine, (1, 4))


def rotate(u, cosine, sine, lane):
    first = (lane % HD) < (HD // 2)
    turned = jnp.where(first, -pltpu.roll(u, PAIR - HD // 2, 1), pltpu.roll(u, HD // 2, 1))
    return u * cosine + turned * sine


def rotate_back(g, cosine, sine, lane):
    first = (lane % HD) < (HD // 2)
    w = g * sine
    return g * cosine + jnp.where(first, pltpu.roll(w, PAIR - HD // 2, 1), -pltpu.roll(w, HD // 2, 1))


def parts(u):
    hi = u.astype(bf16).astype(f32)
    return hi, (u - hi).astype(bf16).astype(f32)


def both(u, head, lane):
    turned = pltpu.roll(u, HD, 1)
    return jnp.where((lane < HD) == (head == 0), u, turned)


def beside(left, right, head, lane):
    low = left if head == 0 else pltpu.roll(left, HD, 1)
    high_lanes = pltpu.roll(right, HD, 1) if head == 0 else right
    return jnp.where(lane < HD, low, high_lanes)


def three_terms(column, lane):
    a = column.astype(bf16).astype(f32)
    b = (column - a).astype(bf16).astype(f32)
    c = column - a - b
    return jnp.where(lane == HD, a, jnp.where(lane == HD + 1, b, jnp.where(lane == HD + 2, c, 0.0)))


def split_bf16(u):
    hi = u.astype(bf16)
    return hi, (u - hi.astype(f32)).astype(bf16)


def dot_nt(a, b):
    return lax.dot_general(a, b, (((1,), (1,)), ((), ())), preferred_element_type=f32)


def dot_nn(a, b):
    return lax.dot_general(a, b, (((1,), (0,)), ((), ())), preferred_element_type=f32)


def forward_kernel(
    len_ref, q_ref, k_ref, v_ref, cos_ref, sin_ref, out_ref, lse_ref, qs, ks, vs, acc, *, rows
):
    full_len = q_ref.shape[0]
    lane = lax.broadcasted_iota(jnp.int32, (full_len, PAIR), 1)
    place = lax.broadcasted_iota(jnp.int32, (full_len, PAIR), 0)
    cosine, sine = cos_ref[...], sin_ref[...]
    q = rotate(q_ref[...], cosine, sine, lane) * (HD**-0.5 * LOG2E)
    k = rotate(k_ref[...], cosine, sine, lane)
    q_hi, q_lo = parts(q)
    k_hi, k_lo = parts(k)
    v_hi, v_lo = parts(v_ref[...])
    bias = jnp.where(place < len_ref[0], 0.0, -1e30)
    for head in range(2):
        qs[head, :, :PAIR] = both(q_hi, head, lane).astype(bf16)
        qs[head, :, PAIR:] = jnp.where(
            lane < HD, beside(q_lo, q_lo, head, lane), jnp.where(lane == HD, 1.0, 0.0)
        ).astype(bf16)
        ks[head, :, :PAIR] = beside(k_hi, k_lo, head, lane).astype(bf16)
        ks[head, :, PAIR:] = jnp.where(
            lane < HD, beside(k_hi, k_hi, head, lane), jnp.where(lane == HD, bias, 0.0)
        ).astype(bf16)
        vs[head] = beside(v_hi, v_lo, head, lane).astype(bf16)

    low = lax.broadcasted_iota(jnp.int32, (rows, PAIR), 1) < HD
    units = [(block, head) for block in range(full_len // rows) for head in range(2)]

    def scores_of(unit):
        block, head = unit
        return dot_nt(qs[head, pl.ds(block * rows, rows), :], ks[head])

    following = scores_of(units[0])
    outs, lses = [], []
    for place, (block, head) in enumerate(units):
        scores = following
        if place + 1 < len(units):
            following = scores_of(units[place + 1])
        largest = jnp.max(scores, axis=1, keepdims=True)
        expo = jnp.exp2(scores - largest)
        total = jnp.sum(expo, axis=1, keepdims=True)
        hi, lo = split_bf16(expo)
        both_parts = dot_nn(hi, vs[head]) + dot_nn(lo, vs[head])
        outs.append((both_parts + pltpu.roll(both_parts, HD, 1)) / total)
        lses.append(largest + jnp.log2(total))
        if head == 1:
            at = pl.ds(block * rows, rows)
            out_ref[at, :] = jnp.where(low, outs[-2], outs[-1])
            lse_ref[at, :] = jnp.where(low, lses[-2], lses[-1])


def backward_kernel(
    len_ref, q_ref, k_ref, v_ref, cos_ref, sin_ref, out_in_ref, lse_ref, do_ref, *rest, rows
):
    grad_ref, qs, ks, vs, dos, kd, qt, dot_t, dq, dkt, dvt = rest[-11:]
    full_len = q_ref.shape[0]
    which = pl.program_id(1)
    lane = lax.broadcasted_iota(jnp.int32, (full_len, PAIR), 1)

    @pl.when(which == 0)
    def _():
        place = lax.broadcasted_iota(jnp.int32, (full_len, PAIR), 0)
        cosine, sine = cos_ref[...], sin_ref[...]
        q = rotate(q_ref[...], cosine, sine, lane) * (HD**-0.5 * LOG2E)
        k = rotate(k_ref[...], cosine, sine, lane)
        out_grad = do_ref[...]
        q_hi, q_lo = parts(q)
        k_hi, k_lo = parts(k)
        v_hi, v_lo = parts(v_ref[...])
        g_hi, g_lo = parts(out_grad)
        product = out_grad * out_in_ref[...]
        lse = lse_ref[...]
        bias = jnp.where(place < len_ref[0], 0.0, -1e30)
        ones = jnp.where((lane >= HD) & (lane < HD + 3), 1.0, 0.0)
        for head in range(2):
            mine = (lane < HD) == (head == 0)
            delta = jnp.sum(jnp.where(mine, product, 0.0), axis=1, keepdims=True)
            lse_head = jnp.max(jnp.where(mine, lse, -3e38), axis=1, keepdims=True)
            qs[head, :, :PAIR] = both(q_hi, head, lane).astype(bf16)
            qs[head, :, PAIR:] = jnp.where(
                lane < HD,
                beside(q_lo, q_lo, head, lane),
                three_terms(-lse_head, lane) + jnp.where(lane == HD + 3, 1.0, 0.0),
            ).astype(bf16)
            ks[head, :, :PAIR] = beside(k_hi, k_lo, head, lane).astype(bf16)
            ks[head, :, PAIR:] = jnp.where(
                lane < HD, beside(k_hi, k_hi, head, lane), ones + jnp.where(lane == HD + 3, bias, 0.0)
            ).astype(bf16)
            dos[head, :, :PAIR] = both(g_hi, head, lane).astype(bf16)
            dos[head, :, PAIR:] = jnp.where(
                lane < HD, beside(g_lo, g_lo, head, lane), three_terms(-delta, lane)
            ).astype(bf16)
            vs[head, :, :PAIR] = beside(v_hi, v_lo, head, lane).astype(bf16)
            vs[head, :, PAIR:] = jnp.where(lane < HD, beside(v_hi, v_hi, head, lane), ones).astype(bf16)
            kd[head] = beside(k_hi, k_lo, head, lane).astype(bf16)
            qt[head] = beside(q_hi, q_lo, head, lane).T.astype(bf16)
            dot_t[head] = beside(g_hi, g_lo, head, lane).T.astype(bf16)
        dkt[...] = jnp.zeros_like(dkt)
        dvt[...] = jnp.zeros_like(dvt)
        low = lax.broadcasted_iota(jnp.int32, (rows, PAIR), 1) < HD

        units = [(block, head) for block in range(full_len // rows) for head in range(2)]

        def products_of(unit):
            block, head = unit
            at = pl.ds(block * rows, rows)
            return dot_nt(qs[head, at, :], ks[head]), dot_nt(dos[head, at, :], vs[head])

        following = products_of(units[0])
        outs = []
        for order, (block, head) in enumerate(units):
            scores, weight_grad = following
            if order + 1 < len(units):
                following = products_of(units[order + 1])
            at = pl.ds(block * rows, rows)
            weights = jnp.exp2(scores)
            score_grad = weights * weight_grad
            w_hi, w_lo = split_bf16(weights)
            s_hi, s_lo = split_bf16(score_grad)
            both_parts = dot_nn(s_hi, kd[head]) + dot_nn(s_lo, kd[head])
            outs.append(both_parts + pltpu.roll(both_parts, HD, 1))
            q_t = qt[head, :, at]
            g_t = dot_t[head, :, at]
            dkt[head] += dot_nn(q_t, s_hi) + dot_nn(q_t, s_lo)
            dvt[head] += dot_nn(g_t, w_hi) + dot_nn(g_t, w_lo)
            if head == 1:
                dq[at, :] = jnp.where(low, outs[-2], outs[-1])
        grad_ref[...] = rotate_back(dq[...] * HD**-0.5, cosine, sine, lane)

    @pl.when(which == 1)
    def _():
        stacked = jnp.concatenate([dkt[h, :HD, :] + dkt[h, HD:, :] for h in range(2)], axis=0)
        grad_ref[...] = rotate_back(stacked.T * LN2, cos_ref[...], sin_ref[...], lane)

    @pl.when(which == 2)
    def _():
        stacked = jnp.concatenate([dvt[h, :HD, :] + dvt[h, HD:, :] for h in range(2)], axis=0)
        grad_ref[...] = stacked.T


def attention_forward(length, qkv, cosine, sine):
    full_len, three = qkv.shape
    width = three // 3
    pairs = width // PAIR
    rows = min(256, full_len)

    def column(offset):
        return pl.BlockSpec((full_len, PAIR), lambda p, ln: (0, p + offset))

    table = pl.BlockSpec((full_len, PAIR), lambda p, ln: (0, 0))
    wide = jax.ShapeDtypeStruct((full_len, width), f32)
    return pl.pallas_call(
        partial(forward_kernel, rows=rows),
        name="attention_forward",
        out_shape=(wide, wide),
        grid_spec=pltpu.PrefetchScalarGridSpec(
            num_scalar_prefetch=1,
            grid=(pairs,),
            in_specs=[column(0), column(pairs), column(2 * pairs), table, table],
            out_specs=(column(0), column(0)),
            scratch_shapes=[
                pltpu.VMEM((2, full_len, 2 * PAIR), bf16),
                pltpu.VMEM((2, full_len, 2 * PAIR), bf16),
                pltpu.VMEM((2, full_len, PAIR), bf16),
                pltpu.VMEM((8, 128), f32),
            ],
        ),
        cost_estimate=pl.CostEstimate(
            flops=24 * full_len * full_len * width, bytes_accessed=20 * full_len * width, transcendentals=0
        ),
    )(length, qkv, qkv, qkv, cosine, sine)


def attention_backward(length, qkv, cosine, sine, attended, lse, out_grad, first, last, joined):
    full_len, three = qkv.shape
    width = three // 3
    pairs = width // PAIR
    rows = min(256, full_len)

    def column(offset):
        return pl.BlockSpec((full_len, PAIR), lambda p, c, ln: (0, first + p + offset))

    table = pl.BlockSpec((full_len, PAIR), lambda p, c, ln: (0, 0))
    stacked = pltpu.VMEM((2, full_len, 2 * PAIR), bf16)
    turned = pltpu.VMEM((2, PAIR, full_len), bf16)
    summed = pltpu.VMEM((2, PAIR, full_len), f32)
    args = [length, qkv, qkv, qkv, cosine, sine, attended, lse, out_grad]
    in_specs = [
        column(0),
        column(pairs),
        column(2 * pairs),
        table,
        table,
        column(0),
        column(0),
        column(0),
    ]
    if joined is not None:
        args.append(joined)
        in_specs.append(pl.BlockSpec(memory_space=pl.ANY))
    share = (last - first) * full_len * PAIR
    return pl.pallas_call(
        partial(backward_kernel, rows=rows),
        out_shape=jax.ShapeDtypeStruct((full_len, three), f32),
        grid_spec=pltpu.PrefetchScalarGridSpec(
            num_scalar_prefetch=1,
            grid=(last - first, 3),
            in_specs=in_specs,
            out_specs=pl.BlockSpec((full_len, PAIR), lambda p, c, ln: (0, c * pairs + first + p)),
            scratch_shapes=[
                stacked,
                stacked,
                stacked,
                stacked,
                pltpu.VMEM((2, full_len, PAIR), bf16),
                turned,
                turned,
                pltpu.VMEM((full_len, PAIR), f32),
                summed,
                summed,
            ],
        ),
        input_output_aliases={} if joined is None else {len(args) - 1: 0},
        cost_estimate=pl.CostEstimate(
            flops=60 * full_len * share, bytes_accessed=32 * share, transcendentals=0
        ),
    )(*args)


ATTN_GAIN, ATTN_SHIFT, ATTN_SCALE, ATTN_GATE, MLP_GAIN, MLP_SHIFT, MLP_SCALE, MLP_GATE, DOWN_BIAS = range(9)
VECTORS = 16
COLUMNS = 256


def put_left(ref, u, axis):
    hi, lo = split_bf16(u)
    size = u.shape[axis]
    for place, part in enumerate((hi, lo, hi)):
        if axis == 1:
            ref[:, place * size : (place + 1) * size] = part
        else:
            ref[place * size : (place + 1) * size, :] = part


def put_right(ref, u, axis):
    hi, lo = split_bf16(u)
    size = u.shape[axis]
    for place, part in enumerate((hi, hi, lo)):
        if axis == 1:
            ref[:, place * size : (place + 1) * size] = part
        else:
            ref[place * size : (place + 1) * size, :] = part


def normalized(v):
    average = jnp.mean(v, axis=-1, keepdims=True)
    centered = v - average
    rstd = lax.rsqrt(jnp.mean(centered * centered, axis=-1, keepdims=True) + epsilon)
    return centered * rstd, rstd


def modulated(v, vec_ref, gain, shift, scale):
    xhat, _ = normalized(v)
    return xhat * row(vec_ref, gain) * (1.0 + row(vec_ref, scale)) + row(vec_ref, shift)


def row(ref, index):
    return ref[index : index + 1, :]


def column_sum(u):
    return jnp.sum(u, axis=0, keepdims=True)


def norm_backward(e_ref, v_ref, extra_ref, vec_ref, gain, scale, out_ref, sums_ref, other_ref):
    full_len = v_ref.shape[0]
    rows = min(128, full_len)
    factor = (1.0 + row(vec_ref, scale)) * row(vec_ref, gain)

    def step(block, carry):
        at = pl.ds(pl.multiple_of(block * rows, rows), rows)
        e = e_ref[at, :]
        xhat, rstd = normalized(v_ref[at, :])
        f = e * factor
        grad = rstd * (
            f
            - jnp.mean(f, axis=-1, keepdims=True)
            - xhat * jnp.mean(f * xhat, axis=-1, keepdims=True)
        )
        out = extra_ref[at, :] + grad
        out_ref[at, :] = out
        new = [column_sum(e), column_sum(e * xhat)]
        if other_ref is not None:
            new.append(column_sum(out * other_ref[at, :]))
        return tuple(c + n for c, n in zip(carry, new))

    zero = jnp.zeros((1, v_ref.shape[1]), f32)
    count = 2 if other_ref is None else 3
    total = lax.fori_loop(0, full_len // rows, step, (zero,) * count)
    sums_ref[...] = jnp.zeros_like(sums_ref)
    sums_ref[0:1, :] = total[0]
    sums_ref[1:2, :] = total[1] * row(vec_ref, gain)
    sums_ref[2:3, :] = total[1] * (1.0 + row(vec_ref, scale))
    if other_ref is not None:
        sums_ref[3:4, :] = total[2]


def qkv_kernel(x_ref, vec_ref, w_ref, out_ref, left, right):
    @pl.when(pl.program_id(0) == 0)
    def _():
        put_left(left, modulated(x_ref[...], vec_ref, ATTN_GAIN, ATTN_SHIFT, ATTN_SCALE), 1)

    put_right(right, w_ref[...], 0)
    out_ref[...] = dot_nn(left[...], right[...])


def proj_kernel(
    len_ref, att_ref, x_ref, vec_ref, w_ref, proj_ref, middle_ref, sums_ref, left, right
):
    @pl.when(pl.program_id(0) == 0)
    def _():
        put_left(left, att_ref[...], 1)

    put_right(right, w_ref[...], 0)
    proj = dot_nn(left[...], right[...])
    x = x_ref[...]
    branch = row(vec_ref, ATTN_GATE) * proj
    proj_ref[...] = proj
    middle_ref[...] = x + branch
    valid = lax.broadcasted_iota(jnp.int32, x.shape, 0) < len_ref[0]
    sums_ref[...] = jnp.zeros_like(sums_ref)
    sums_ref[0:1, :] = column_sum(jnp.where(valid, x * x, 0.0))
    sums_ref[1:2, :] = column_sum(jnp.where(valid, branch * branch, 0.0))


def up_kernel(middle_ref, vec_ref, up_ref, bias_ref, act_ref, slope_ref, left, right, *, rows):
    @pl.when(pl.program_id(0) == 0)
    def _():
        put_left(left, modulated(middle_ref[...], vec_ref, MLP_GAIN, MLP_SHIFT, MLP_SCALE), 1)

    put_right(right, up_ref[...], 0)
    for block in range(middle_ref.shape[0] // rows):
        at = pl.ds(block * rows, rows)
        pre = dot_nn(left[at, :], right[...]) + bias_ref[...]
        act_ref[at, :], slope_ref[at, :] = gelu_and_slope(pre)


def down_kernel(
    len_ref, act_ref, down_ref, middle_ref, cot_ref, vec_ref, out_ref, sums_ref, left, right, acc
):
    step = pl.program_id(0)

    @pl.when(step == 0)
    def _():
        acc[...] = jnp.zeros_like(acc)

    put_left(left, act_ref[...], 1)
    put_right(right, down_ref[...], 0)
    acc[...] += dot_nn(left[...], right[...])

    @pl.when(step == pl.num_programs(0) - 1)
    def _():
        down_out = acc[...] + row(vec_ref, DOWN_BIAS)
        branch = row(vec_ref, MLP_GATE) * down_out
        out_ref[...] = middle_ref[...] + branch
        valid = lax.broadcasted_iota(jnp.int32, branch.shape, 0) < len_ref[0]
        sums_ref[...] = jnp.zeros_like(sums_ref)
        sums_ref[0:1, :] = column_sum(jnp.where(valid, branch * branch, 0.0))
        sums_ref[1:2, :] = column_sum(cot_ref[...] * down_out)


def down_grad_kernel(cot_ref, vec_ref, act_ref, grad_ref, sums_ref, left, right):
    @pl.when(pl.program_id(0) == 0)
    def _():
        grad = cot_ref[...] * row(vec_ref, MLP_GATE)
        put_left(left, grad.T, 1)
        sums_ref[...] = jnp.zeros_like(sums_ref)
        sums_ref[0:1, :] = column_sum(grad)

    put_right(right, act_ref[...], 0)
    chunk = COLUMNS
    count = left.shape[0] // chunk
    following = dot_nn(left[:chunk, :], right[...])
    for part in range(count):
        turned = following
        if part + 1 < count:
            following = dot_nn(left[(part + 1) * chunk : (part + 2) * chunk, :], right[...])
        grad_ref[:, part * chunk : (part + 1) * chunk] = turned.T


def mlp_backward_kernel(
    cot_ref,
    middle_ref,
    proj_ref,
    vec_ref,
    down_ref,
    up_ref,
    slope_ref,
    up_grad_ref,
    bias_grad_ref,
    middle_grad_ref,
    sums_ref,
    left,
    turned,
    down_cat,
    up_cat,
    pre_cat,
    pre_stack,
    acc,
    *,
    rows,
):
    step = pl.program_id(0)
    full_len = middle_ref.shape[0]

    @pl.when(step == 0)
    def _():
        put_left(left, cot_ref[...] * row(vec_ref, MLP_GATE), 1)
        normed = modulated(middle_ref[...], vec_ref, MLP_GAIN, MLP_SHIFT, MLP_SCALE)
        put_left(turned, normed.T, 1)
        acc[...] = jnp.zeros_like(acc)

    put_right(down_cat, down_ref[...], 1)
    put_right(up_cat, up_ref[...], 1)
    bias_grad = jnp.zeros_like(bias_grad_ref)
    blocks = [pl.ds(block * rows, rows) for block in range(full_len // rows)]

    def add_to_acc(at):
        acc[at, :] += dot_nt(pre_cat[at, :], up_cat[...])

    following = dot_nt(left[blocks[0], :], down_cat[...])
    for block, at in enumerate(blocks):
        act_grad = following
        if block + 1 < len(blocks):
            following = dot_nt(left[blocks[block + 1], :], down_cat[...])
        if block > 0:
            add_to_acc(blocks[block - 1])
        pre_grad = act_grad * slope_ref[at, :]
        bias_grad += column_sum(pre_grad)
        hi, lo = split_bf16(pre_grad)
        columns = hi.shape[1]
        for place, part in enumerate((hi, lo, hi)):
            pre_cat[at, place * columns : (place + 1) * columns] = part
        for place, part in enumerate((hi, hi, lo)):
            pre_stack[pl.ds(place * full_len + block * rows, rows), :] = part
    add_to_acc(blocks[-1])
    bias_grad_ref[...] = bias_grad
    up_grad_ref[...] = dot_nn(turned[...], pre_stack[...])

    @pl.when(step == pl.num_programs(0) - 1)
    def _():
        norm_backward(
            acc, middle_ref, cot_ref, vec_ref, MLP_GAIN, MLP_SCALE, middle_grad_ref, sums_ref, proj_ref
        )


def proj_backward_kernel(
    grad_ref, grad_block_ref, att_ref, vec_ref, vec_block_ref, w_ref, out_ref, w_grad_ref,
    left, turned, w_cat, stack,
):
    @pl.when(pl.program_id(0) == 0)
    def _():
        put_left(left, grad_ref[...] * row(vec_ref, ATTN_GATE), 1)
        put_left(turned, att_ref[...].T, 1)

    put_right(w_cat, w_ref[...], 1)
    out_ref[...] = dot_nt(left[...], w_cat[...])
    put_right(stack, grad_block_ref[...] * row(vec_block_ref, ATTN_GATE), 0)
    w_grad_ref[...] = dot_nn(turned[...], stack[...])


def tokens_grad_kernel(
    grad_ref, w_ref, x_ref, extra_ref, vec_ref, out_ref, sums_ref, left, w_cat, acc
):
    step = pl.program_id(0)

    @pl.when(step == 0)
    def _():
        acc[...] = jnp.zeros_like(acc)

    put_left(left, grad_ref[...], 1)
    put_right(w_cat, w_ref[...], 1)
    acc[...] += dot_nt(left[...], w_cat[...])

    @pl.when(step == pl.num_programs(0) - 1)
    def _():
        norm_backward(acc, x_ref, extra_ref, vec_ref, ATTN_GAIN, ATTN_SCALE, out_ref, sums_ref, None)


def qkv_grad_kernel(x_ref, vec_ref, grad_ref, joined_ref, out_ref, turned, stack):
    del joined_ref

    @pl.when(pl.program_id(0) == 0)
    def _():
        normed = modulated(x_ref[...], vec_ref, ATTN_GAIN, ATTN_SHIFT, ATTN_SCALE)
        put_left(turned, normed.T, 1)

    put_right(stack, grad_ref[...], 0)
    out_ref[...] = dot_nn(turned[...], stack[...])


def whole(shape):
    return pl.BlockSpec(shape, lambda *ids: (0,) * len(shape), pipeline_mode=pl.Buffered(1))


def by_columns(rows, columns, first=0):
    return pl.BlockSpec((rows, columns), lambda j, *refs: (0, first + j))


def by_rows(rows, columns, column=0):
    return pl.BlockSpec((rows, columns), lambda j, *refs: (j, column))


def dense(body, grid, in_specs, out_specs, out_shapes, scratch, products, args, scalars=0, aliases=None):
    moved = sum(a.size for a in args) + sum(o.size for o in out_shapes)
    return pl.pallas_call(
        body,
        out_shape=tuple(out_shapes),
        grid_spec=pltpu.PrefetchScalarGridSpec(
            num_scalar_prefetch=scalars,
            grid=(grid,),
            in_specs=in_specs,
            out_specs=tuple(out_specs),
            scratch_shapes=[pltpu.VMEM(shape, kind) for shape, kind in scratch],
        ),
        input_output_aliases=aliases or {},
        compiler_params=pltpu.CompilerParams(vmem_limit_bytes=60 << 20),
        cost_estimate=pl.CostEstimate(flops=6 * products, bytes_accessed=4 * moved, transcendentals=0),
    )(*args)


def array(*shape):
    return jax.ShapeDtypeStruct(shape, f32)


def mm_qkv(x, vectors, weight):
    t, d = x.shape
    n = 3 * d
    c = COLUMNS
    return dense(
        qkv_kernel,
        n // c,
        [whole((t, d)), whole((VECTORS, d)), by_columns(d, c)],
        [by_columns(t, c)],
        [array(t, n)],
        [((t, 3 * d), bf16), ((3 * d, c), bf16)],
        t * d * n,
        (x, vectors, weight),
    )[0]


def mm_proj(length, attended, x, vectors, weight):
    t, d = x.shape
    c = COLUMNS
    return dense(
        proj_kernel,
        d // c,
        [whole((t, d)), by_columns(t, c), by_columns(VECTORS, c), by_columns(d, c, 3 * d // c)],
        [by_columns(t, c), by_columns(t, c), by_columns(8, c)],
        [array(t, d), array(t, d), array(8, d)],
        [((t, 3 * d), bf16), ((3 * d, c), bf16)],
        t * d * d,
        (length, attended, x, vectors, weight),
        scalars=1,
    )


def mm_up(middle, vectors, up, up_bias):
    t, d = middle.shape
    n = up.shape[1]
    c = COLUMNS
    return dense(
        partial(up_kernel, rows=min(256, t)),
        n // c,
        [whole((t, d)), whole((VECTORS, d)), by_columns(d, c), by_columns(1, c)],
        [by_columns(t, c), by_columns(t, c)],
        [array(t, n), array(t, n)],
        [((t, 3 * d), bf16), ((3 * d, c), bf16)],
        t * d * n,
        (middle, vectors, up, up_bias),
    )


def mm_down(length, act, down, middle, cot, vectors):
    t, n = act.shape
    d = down.shape[1]
    c = 2 * COLUMNS
    return dense(
        down_kernel,
        n // c,
        [by_columns(t, c), by_rows(c, d), whole((t, d)), whole((t, d)), whole((VECTORS, d))],
        [whole((t, d)), whole((8, d))],
        [array(t, d), array(8, d)],
        [((t, 3 * c), bf16), ((3 * c, d), bf16), ((t, d), f32)],
        t * d * n,
        (length, act, down, middle, cot, vectors),
        scalars=1,
    )


def dw_down(cot, vectors, act):
    t, d = cot.shape
    n = act.shape[1]
    c = 2 * COLUMNS
    return dense(
        down_grad_kernel,
        n // c,
        [whole((t, d)), whole((VECTORS, d)), by_columns(t, c)],
        [by_rows(c, d), whole((8, d))],
        [array(n, d), array(8, d)],
        [((d, 3 * t), bf16), ((3 * t, c), bf16)],
        t * d * n,
        (cot, vectors, act),
    )


def mlp_backward(cot, middle, proj_out, vectors, down, up, slope):
    t, d = cot.shape
    n = up.shape[1]
    c = COLUMNS
    return dense(
        partial(mlp_backward_kernel, rows=min(256, t)),
        n // c,
        [
            whole((t, d)),
            whole((t, d)),
            whole((t, d)),
            whole((VECTORS, d)),
            by_rows(c, d),
            by_columns(d, c),
            by_columns(t, c),
        ],
        [by_columns(d, c), by_columns(1, c), whole((t, d)), whole((8, d))],
        [array(d, n), array(1, n), array(t, d), array(8, d)],
        [
            ((t, 3 * d), bf16),
            ((d, 3 * t), bf16),
            ((c, 3 * d), bf16),
            ((d, 3 * c), bf16),
            ((t, 3 * c), bf16),
            ((3 * t, c), bf16),
            ((t, d), f32),
        ],
        3 * t * d * n,
        (cot, middle, proj_out, vectors, down, up, slope),
    )


def proj_backward(middle_grad, attended, vectors, weight):
    t, d = middle_grad.shape
    c = COLUMNS
    return dense(
        proj_backward_kernel,
        d // c,
        [
            whole((t, d)),
            by_columns(t, c),
            whole((t, d)),
            whole((VECTORS, d)),
            by_columns(VECTORS, c),
            by_rows(c, d, 3),
        ],
        [by_columns(t, c), by_columns(d, c, 3 * d // c)],
        [array(t, d), array(d, 4 * d)],
        [((t, 3 * d), bf16), ((d, 3 * t), bf16), ((c, 3 * d), bf16), ((3 * t, c), bf16)],
        2 * t * d * d,
        (middle_grad, middle_grad, attended, vectors, vectors, weight),
    )


def mm_tokens_grad(qkv_grad, weight, x, middle_grad, vectors):
    t, d = x.shape
    n = 3 * d
    c = COLUMNS
    return dense(
        tokens_grad_kernel,
        n // c,
        [by_columns(t, c), by_columns(d, c), whole((t, d)), whole((t, d)), whole((VECTORS, d))],
        [whole((t, d)), whole((8, d))],
        [array(t, d), array(8, d)],
        [((t, 3 * c), bf16), ((d, 3 * c), bf16), ((t, d), f32)],
        t * d * n,
        (qkv_grad, weight, x, middle_grad, vectors),
    )


def dw_qkv(x, vectors, qkv_grad, joined):
    t, d = x.shape
    n = qkv_grad.shape[1]
    c = COLUMNS
    return dense(
        qkv_grad_kernel,
        n // c,
        [
            whole((t, d)),
            whole((VECTORS, d)),
            by_columns(t, c),
            pl.BlockSpec(memory_space=pl.ANY),
        ],
        [by_columns(d, c)],
        [array(*joined.shape)],
        [((d, 3 * t), bf16), ((3 * t, c), bf16)],
        t * d * n,
        (x, vectors, qkv_grad, joined),
        aliases={3: 0},
    )[0]


def padded_row(pieces):
    row = jnp.concatenate([piece.reshape(-1) for piece in pieces])
    return jnp.pad(row, (0, -row.shape[0] % 128))[None, :]


def cut(row, sizes):
    out, start = [], 0
    for size in sizes:
        out.append(row[:, start : start + size])
        start += size
    return out


def shards(
    tokens,
    time_embed,
    lengths,
    positions,
    ada_weight,
    ada_bias,
    attn_gain,
    qkv_weight,
    proj_weight,
    mlp_gain,
    up_weight,
    up_bias,
    down_weight,
    down_bias,
    cotangent,
):
    groups = lax.axis_size("seq")
    owners = lax.axis_size("fsdp")
    mine_seq = lax.axis_index("seq")
    mine_fsdp = lax.axis_index("fsdp")
    seqs_here, local_len, width = tokens.shape
    cond = time_embed.shape[1]
    full_len = local_len * groups
    assert seqs_here == groups

    def to_sequence(field):
        return lax.all_to_all(field, "seq", split_axis=0, concat_axis=1, tiled=True)[0]

    def to_tokens(field):
        pieces = field.reshape(groups, local_len, width)
        return lax.all_to_all(pieces, "seq", split_axis=0, concat_axis=0, tiled=True)

    def gather(shard):
        return lax.all_gather(shard, "fsdp", axis=0, tiled=True)

    def exchanged(rows, axis, count, mine):
        if count > 8:
            all_rows = lax.all_gather(rows, axis, axis=0)
            return lax.dynamic_slice(all_rows, (0, mine, 0), (count, 1, rows.shape[1]))[:, 0]
        out = jnp.zeros_like(rows)
        for shift in range(count):
            target = (mine + shift) % count
            sent = lax.dynamic_slice(rows, (target, 0), (1, rows.shape[1]))
            if shift > 0:
                sent = lax.ppermute(sent, axis, [(i, (i + shift) % count) for i in range(count)])
            out = lax.dynamic_update_slice(out, sent, ((mine - shift) % count, 0))
        return out

    def seq_shift(piece, shift):
        return lax.ppermute(piece, "seq", [(i, (i + shift) % groups) for i in range(groups)])

    def seq_gather(piece):
        pieces = jnp.stack([piece] + [seq_shift(piece, shift) for shift in range(1, groups)])
        order = [(mine_seq - place) % groups for place in range(groups)]
        return jnp.concatenate([lax.dynamic_slice_in_dim(pieces, at, 1, 0) for at in order], axis=0)

    def seq_partial(shard):
        pieces = shard.reshape((groups, -1) + shard.shape[1:])
        total = lax.dynamic_slice_in_dim(pieces, mine_seq, 1, 0)[0]
        for shift in range(1, groups):
            sent = lax.dynamic_slice_in_dim(pieces, (mine_seq + shift) % groups, 1, 0)[0]
            total = total + seq_shift(sent, shift)
        return total

    x = to_sequence(tokens)
    places = exchanged(positions, "seq", groups, mine_seq).reshape(full_len)
    length = lax.dynamic_slice(lengths, (mine_seq,), (1,))
    small = [time_embed, ada_bias, attn_gain, mlp_gain, up_bias, down_bias]
    small_sizes = [piece.size for piece in small]
    packed = gather(padded_row(small))
    time_all, ada_bias_full, attn_gain_full, mlp_gain_full, up_bias_full, down_bias_full = cut(
        packed, small_sizes
    )
    time_all = time_all.reshape(owners * seqs_here, cond)
    ada_bias_full, attn_gain_full, mlp_gain_full, up_bias_full, down_bias_full = (
        piece.reshape(1, -1)
        for piece in (ada_bias_full, attn_gain_full, mlp_gain_full, up_bias_full, down_bias_full)
    )
    silu_all = jax.nn.silu(time_all)
    ada_rows = ada_weight.shape[0]
    silu_cols = lax.dynamic_slice(silu_all, (0, mine_fsdp * ada_rows), (owners * seqs_here, ada_rows))
    silu_group = lax.dynamic_slice(
        silu_cols.reshape(owners, seqs_here, ada_rows), (0, mine_seq, 0), (owners, 1, ada_rows)
    )[:, 0]
    partial_rows = jnp.dot(silu_group, ada_weight, precision=highest)
    partial_rows = exchanged(partial_rows, "fsdp", owners, mine_fsdp)
    modulation = jnp.sum(partial_rows, axis=0, keepdims=True) + ada_bias_full
    shift_attn, scale_attn, gate_attn, shift_mlp, scale_mlp, gate_mlp = jnp.split(modulation, 6, axis=1)
    vectors = [
        attn_gain_full,
        shift_attn,
        scale_attn,
        gate_attn,
        mlp_gain_full,
        shift_mlp,
        scale_mlp,
        gate_mlp,
        down_bias_full,
    ]
    vectors = jnp.concatenate(vectors + [jnp.zeros((VECTORS - len(vectors), width), f32)], axis=0)
    attn_weight = jnp.concatenate([qkv_weight, proj_weight], axis=1)
    attn_full = gather(attn_weight)
    up_full = gather(up_weight)
    down_full = gather(down_weight)
    cosine, sine = rotary_tables(places)

    qkv = mm_qkv(x, vectors, attn_full)
    cot_in, _ = lax.optimization_barrier((cotangent, x))
    cot = to_sequence(cot_in)
    attended, lse = attention_forward(length, qkv, cosine, sine)
    proj_out, middle, attn_sums = mm_proj(length, attended, x, vectors, attn_full)
    hidden_act, gelu_slope = mm_up(middle, vectors, up_full, up_bias_full)
    down_weight_grad, down_sums = dw_down(cot, vectors, hidden_act)
    block_out, mlp_sums = mm_down(length, hidden_act, down_full, middle, cot, vectors)
    block_out = to_tokens(block_out)

    def scatter(grad):
        return lax.psum_scatter(grad, "fsdp", scatter_dimension=0, tiled=True)

    down_shard = scatter(down_weight_grad)
    up_weight_grad, up_bias_grad, middle_grad, mlp_norm_sums = mlp_backward(
        cot, middle, proj_out, vectors, down_full, up_full, gelu_slope
    )
    up_shard = scatter(up_weight_grad)
    attended_grad, joined_grad = proj_backward(middle_grad, attended, vectors, attn_full)
    down_part = seq_partial(down_shard)
    down_total = seq_gather(down_part).reshape(down_shard.shape)
    up_part = seq_partial(up_shard)
    up_total = seq_gather(up_part).reshape(up_shard.shape)
    gate_mlp_grad, down_bias_grad = mlp_sums[1], down_sums[0]
    shift_mlp_grad, scale_mlp_grad, mlp_gain_grad, gate_attn_grad = (mlp_norm_sums[i] for i in range(4))
    sums = jnp.stack(
        [
            jnp.sum(attn_sums[0]),
            jnp.sum(attn_sums[1]),
            jnp.sum(mlp_sums[0]),
            length[0].astype(f32),
        ]
    )
    pairs = width // PAIR
    back_args = (length, qkv, cosine, sine, attended, lse, attended_grad)
    qkv_grad = None
    for part in range(3):
        first, last = pairs * part // 3, pairs * (part + 1) // 3
        qkv_grad = attention_backward(*back_args, first, last, qkv_grad)
    tokens_grad, attn_norm_sums = mm_tokens_grad(qkv_grad, attn_full, x, middle_grad, vectors)
    shift_attn_grad, scale_attn_grad, attn_gain_grad = (attn_norm_sums[i] for i in range(3))
    tokens_grad = to_tokens(tokens_grad)
    attn_shard = scatter(dw_qkv(x, vectors, qkv_grad, joined_grad))
    modulation_rows = [
        shift_attn_grad,
        scale_attn_grad,
        gate_attn_grad,
        shift_mlp_grad,
        scale_mlp_grad,
        gate_mlp_grad,
    ]
    vector_grads = [attn_gain_grad, mlp_gain_grad, up_bias_grad, down_bias_grad]
    late_all = gather(padded_row(modulation_rows + vector_grads + [sums]))
    modulation_grad = late_all[:, : 6 * width]
    group_sum = jnp.sum(late_all, axis=0, keepdims=True)
    ada_bias_sum, *vector_sums, sums_sum = cut(
        group_sum, [6 * width] + [piece.size for piece in vector_grads] + [sums.size]
    )

    def owned(total):
        size = total.shape[1] // owners
        return lax.dynamic_slice(total, (0, mine_fsdp * size), (1, size))

    time_cols = lax.dot_general(modulation_grad, ada_weight, (((1,), (1,)), ((), ())), precision=highest)
    time_cols = lax.all_gather(time_cols, "fsdp", axis=0)
    time_part = lax.dynamic_slice(time_cols, (0, mine_fsdp, 0), (owners, 1, ada_rows)).reshape(1, cond)
    time_part = jnp.where(jnp.arange(seqs_here)[:, None] == mine_seq, time_part, 0.0)
    ada_part = lax.dot_general(silu_group, modulation_grad, (((0,), (0,)), ((), ())), precision=highest)
    owned_sums = [owned(piece) for piece in [ada_bias_sum] + vector_sums]
    vector_part = padded_row(owned_sums + [sums_sum, time_part])
    attn_total, ada_weight_grad, vector_total = lax.psum((attn_shard, ada_part, vector_part), "seq")
    qkv_total, proj_total = attn_total[:, : 3 * width], attn_total[:, 3 * width :]
    ada_bias_total, attn_gain_total, mlp_gain_total, up_bias_total, down_bias_total, sums_total, time_total = (
        piece[0]
        for piece in cut(vector_total, [piece.size for piece in owned_sums] + [sums.size, time_part.size])
    )
    _, silu_back = jax.vjp(jax.nn.silu, time_embed)
    (time_grad,) = silu_back(time_total.reshape(seqs_here, cond))
    rms = jnp.sqrt(sums_total[:3] / (sums_total[3] * width))
    return (
        block_out,
        tokens_grad,
        time_grad,
        ada_weight_grad,
        ada_bias_total,
        attn_gain_total,
        qkv_total,
        proj_total,
        mlp_gain_total,
        up_total,
        up_bias_total,
        down_total,
        down_bias_total,
        rms[0],
        rms[1],
        rms[2],
    )


def solution(mesh):
    field = P("fsdp", "seq", None)
    matrix = P("fsdp", None)
    vector = P("fsdp")

    return jax.shard_map(
        shards,
        mesh=mesh,
        in_specs=(
            field,
            matrix,
            vector,
            P("fsdp", "seq"),
            matrix,
            vector,
            vector,
            matrix,
            matrix,
            vector,
            matrix,
            vector,
            matrix,
            vector,
            field,
        ),
        out_specs=(
            field,
            field,
            matrix,
            matrix,
            vector,
            vector,
            matrix,
            matrix,
            vector,
            matrix,
            vector,
            matrix,
            vector,
            P(),
            P(),
            P(),
        ),
        check_vma=False,
    )
```
